256 devices in a mesh: expert: 64 (over z, x, core), mp: 4 (over y).
Axes of the slice: x: 4, y: 4, z: 8, core: 2. Of those that a mesh axis runs over, the one named last changes fastest.
Arguments:
- tokens: bfloat16 [16384, 1024], P('expert'), may hold values from -6 to 6
- cotangent: bfloat16 [16384, 1024], P('expert'), may hold values from -16 to 16
- routes: int32 [16384, 2], P('expert'), may hold values from 0 to 63, all different within a row; in each aligned block of 256 rows (0 to 255, 256 to 511, ...) at most 12 rows name the same one
- router_weight: bfloat16 [1024, 64], replicated, may hold values from -0.1875 to 0.1875
- gate_weight: bfloat16 [64, 1024, 3584], P('expert', None, 'mp'), may hold values from -0.1875 to 0.1875
- up_weight: bfloat16 [64, 1024, 3584], P('expert', None, 'mp'), may hold values from -0.6875 to 0.6875
- down_weight: bfloat16 [64, 3584, 1024], P('expert', 'mp'), may hold values from -0.3674842 to 0.3674842
- mlp_in: float32 [3, 16], replicated, may hold values from -3.5 to 3.5
- mlp_bias: float32 [16], replicated, may hold values from -2 to 2
- mlp_out: float32 [16], replicated, may hold values from -1.5 to 1.5
Outputs:
- mixed: bfloat16 [16384, 1024], P('expert', 'mp')
- gate_update: bfloat16 [64, 1024, 3584], P('expert', None, 'mp')
- up_update: bfloat16 [64, 1024, 3584], P('expert', None, 'mp')
- down_update: bfloat16 [64, 3584, 1024], P('expert', 'mp')
- router_update: bfloat16 [1024, 64], replicated
The draws below stay inside these ranges and needn't reach their ends.
Inputs may be any that keep to these rules, and one draw needn't show every extreme that they name: `routes`: in the rows of one index of the expert axis each expert is named at most 12 times; the two experts of a row differ.
All inputs are finite; a program needn't handle non-finite values.
Results may differ from the reference program's by a relative error of at most 0.0057.
Values may be sent and summed in bfloat16 or wider, within the bound.
No kernel may reach another device: no remote copies, remote signals or barrier semaphores. Data moves between devices by JAX's collectives and lax.ppermute only.
A program may use at most 128 MiB of HBM per device.

```python
import math
import jax
import jax.numpy as jnp
import numpy as np
from jax import lax

D = 1024
FF = 3584
TOK_DEV = 256
LOPT_UNITS = 16
FEATURES = 3
EXPERTS = 64
CAP = 12
TOKENS = 16384
N_EXPERT = 64


def draw_up_weight(key, part):
    base = jax.random.fold_in(key, 101)
    column_scale = jnp.exp(jax.random.uniform(jax.random.fold_in(base, 1), (FF,), jnp.float32, -1.15, 1.15))
    ramp = jnp.arange(EXPERTS, dtype=jnp.float32) / max(EXPERTS - 1, 1)
    entries = jnp.clip(jax.random.normal(jax.random.fold_in(base, 2), (EXPERTS, D, FF), jnp.float32), -4.0, 4.0)
    expert_scale = 3.0 ** ramp / 1.732
    values = entries * expert_scale[:, None, None] * column_scale[None, None, :] / D ** 0.5
    return values.astype(jnp.bfloat16)


def draw_down_weight(key, part):
    base = jax.random.fold_in(key, 202)
    column_scale = jnp.exp(jax.random.uniform(jax.random.fold_in(base, 1), (D,), jnp.float32, -1.15, 1.15))
    ramp = jnp.arange(EXPERTS, dtype=jnp.float32) / max(EXPERTS - 1, 1)
    entries = jnp.clip(jax.random.normal(jax.random.fold_in(base, 2), (EXPERTS, FF, D), jnp.float32), -4.0, 4.0)
    expert_scale = 3.0 ** ramp / 1.732
    values = entries * expert_scale[:, None, None] * column_scale[None, None, :] / FF ** 0.5
    return values.astype(jnp.bfloat16)


def raised(drawn, key, source, target, shards_of, factor):
    owner, partner = [(jnp.arange(drawn.shape[axis_at]) // (drawn.shape[axis_at] // shards_of)).reshape([-1 if axis == axis_at else 1 for axis in range(drawn.ndim)]) for axis_at in (source, target)]
    chosen = jax.random.permutation(key, shards_of)[partner]
    strong = (owner == chosen) | (owner == (partner + shards_of // 2) % shards_of)
    return jnp.where(strong, factor * drawn, drawn)


def levels(key, extent, pieces, least, largest):
    def one(axis_at, parts):
        heights = jax.random.uniform(jax.random.fold_in(jax.random.fold_in(key, 6), axis_at), (parts,), jnp.float32, least / len(pieces), largest / len(pieces))
        return jnp.repeat(jnp.exp(heights), extent[axis_at] // parts).reshape((-1,) + (1,) * (len(extent) - axis_at - 1))

    level = one(*pieces[0])
    for cut in pieces[1:]:
        level = level * one(*cut)
    return level


def routed_block(rng, own, number, rows, count, top, bound, lean):
    order = jax.random.permutation(rng, count)
    packed, common = shares(count, rows * top, bound, lean, True), shares(count, rows * top, bound, lean, False)
    places = jnp.arange(count)

    def named(tallies, turn):
        used = int((tallies > 0).sum())
        fixed = max(1, used // 4)
        shifted = fixed + (places - fixed + turn * (used - fixed)) % max(1, count - fixed)
        return jnp.zeros((count,), jnp.int32).at[order[jnp.where(places < fixed, places, shifted)]].set(jnp.asarray(tallies, jnp.int32))

    tallies = jnp.where(number % 4 == 0, named(packed, number // 4), named(common, number - number // 4 - 1))
    mixed = jax.random.permutation(jax.random.fold_in(own, 3), count)
    giver, sink = mixed[0:count // 2 * 2:2], mixed[1:count // 2 * 2:2]
    slack = jnp.minimum(tallies[giver] - 1, bound - tallies[sink]) // 2
    slack = jnp.where((giver == order[0]) | (sink == order[0]) | (tallies[sink] == 0), 0, jnp.maximum(slack, 0))
    shifted = jax.random.randint(jax.random.fold_in(own, 4), (count // 2,), 0, 1 << 20) % (slack + 1)
    tallies = tallies.at[giver].add(-shifted).at[sink].add(shifted)
    labels = jnp.searchsorted(jnp.cumsum(tallies), jnp.arange(rows * top), side="right").astype(jnp.int32)
    grid = labels.reshape(top, rows).T
    grid = grid[jax.random.permutation(jax.random.fold_in(own, 1), rows)]
    turn = jax.random.randint(jax.random.fold_in(own, 2), (rows, 1), 0, top)
    return jnp.take_along_axis(grid, (jnp.arange(top)[None, :] + turn) % top, axis=1)


def shares(count, total, most, slope, full):
    weights = [(1 << 20) // math.isqrt(grade ** slope) + 1 for grade in range(1, count + 1)]
    largest = most if full else min(most, max(-(-total // count), total * weights[0] // sum(weights)))
    least = 1 if total - largest >= count - 1 else 0
    given, rest = [largest] + [least] * (count - 1), total - largest - least * (count - 1)
    while rest > 0:
        movable = [i for i in range(1, count) if given[i] < largest] or [i for i in range(1, count) if given[i] < most]
        whole, budget = sum([weights[i] for i in movable]), rest
        for i in movable:
            more = min(most - given[i], max(1, budget * weights[i] // whole), rest)
            given[i] = given[i] + more
            rest = rest - more
    return np.array(given)


def centred(own_key, shape, deviation, most, cuts=(), kind=jnp.bfloat16):
    gain = levels(own_key, shape, cuts, -0.22, 0.18) if cuts else 1.0
    values = jax.random.normal(own_key, shape, jnp.float32) * deviation * gain
    return jnp.minimum(jnp.maximum(values, -most), most).astype(kind)


def heavy_noise(key, extent, spread, reach, cuts, heavy, kind=jnp.bfloat16):
    result = spread * jax.random.normal(key, extent, jnp.float32)
    if cuts:
        result = result * levels(key, extent, cuts, -0.22, 0.18)
    return jnp.clip(raised(result, jax.random.fold_in(key, 3), *heavy), -reach, reach).astype(kind)


def setup_inputs(seed: int = 0) -> dict:
    splits = jax.random.split(jax.random.key(seed), 11)
    tokens = centred(splits[0], (TOKENS, D), 1.0, 6.0, ((0, 64),))
    cotangent = heavy_noise(splits[1], (TOKENS, D), 1.0, 16.0, ((0, 64),), (0, 1, 64, 4.0))
    routes_keys = jax.random.split(jax.random.fold_in(splits[2], 1), TOKENS // TOK_DEV)
    routes_turns = jax.random.permutation(jax.random.fold_in(splits[2], 3), TOKENS // TOK_DEV)
    routes = jax.vmap(lambda own, number: routed_block(jax.random.fold_in(splits[2], 2), own, number, TOK_DEV, EXPERTS, 2, CAP, 2))(routes_keys, routes_turns).reshape((TOKENS, 2))
    router_weight = centred(splits[3], (D, EXPERTS), D ** -0.5, 0.1875)
    gate_weight = centred(splits[4], (EXPERTS, D, FF), D ** -0.5, 0.1875, ((0, 64), (2, 4)))
    up_weight = draw_up_weight(jax.random.fold_in(splits[10], 71), 0)
    down_weight = draw_down_weight(jax.random.fold_in(splits[10], 71), 0)
    mlp_in = centred(splits[7], (FEATURES, LOPT_UNITS), FEATURES ** -0.5, 3.5, (), jnp.float32)
    mlp_bias = centred(splits[8], (LOPT_UNITS,), 0.5, 2.0, (), jnp.float32)
    mlp_out = centred(splits[9], (LOPT_UNITS,), LOPT_UNITS ** -0.5, 1.5, (), jnp.float32)
    return {"tokens": tokens, "cotangent": cotangent, "routes": routes, "router_weight": router_weight, "gate_weight": gate_weight, "up_weight": up_weight, "down_weight": down_weight, "mlp_in": mlp_in, "mlp_bias": mlp_bias, "mlp_out": mlp_out}


EPSILON = 1e-06

def learned_step(gradient, weight, weight_scale, grad_rms, mlp_in, mlp_bias, mlp_out):
    feat_grad = gradient / grad_rms
    feat_weight = weight.astype(jnp.float32) * weight_scale
    feat_tanh = jnp.tanh(feat_grad)
    summed = jnp.zeros_like(feat_grad)
    for neuron in range(mlp_bias.shape[0]):
        hidden = jnp.maximum(mlp_in[0, neuron] * feat_grad + mlp_in[1, neuron] * feat_weight + mlp_in[2, neuron] * feat_tanh + mlp_bias[neuron], 0.0)
        summed = summed + mlp_out[neuron] * hidden
    return summed.astype(jnp.bfloat16)

def expert_pass(operands):
    rows_x, rows_dy, w_gate, w_up, w_down = operands
    act_gate = jnp.dot(rows_x, w_gate, preferred_element_type=jnp.float32)
    act_up = jnp.dot(rows_x, w_up, preferred_element_type=jnp.float32)
    sigmoid_gate = jax.nn.sigmoid(act_gate)
    silu_gate = act_gate * sigmoid_gate
    hidden = (silu_gate * act_up).astype(jnp.bfloat16)
    expert_out = jnp.dot(hidden, w_down, preferred_element_type=jnp.float32).astype(jnp.bfloat16)
    grad_down = jnp.dot(hidden.T, rows_dy, preferred_element_type=jnp.float32)
    grad_hidden = jnp.dot(rows_dy, w_down.T, preferred_element_type=jnp.float32)
    d_gate = (grad_hidden * act_up * sigmoid_gate * (1.0 + act_gate * (1.0 - sigmoid_gate))).astype(jnp.bfloat16)
    d_up = (grad_hidden * silu_gate).astype(jnp.bfloat16)
    grad_gate = jnp.dot(rows_x.T, d_gate, preferred_element_type=jnp.float32)
    grad_up = jnp.dot(rows_x.T, d_up, preferred_element_type=jnp.float32)
    return (expert_out, grad_gate, grad_up, grad_down)

def reference(tokens, cotangent, routes, router_weight, gate_weight, up_weight, down_weight, mlp_in, mlp_bias, mlp_out):
    expert_ids = jnp.arange(EXPERTS, dtype=jnp.int32)
    picks = (routes[:, :, None] == expert_ids[None, None, :]).astype(jnp.int32)
    blocks = picks.reshape(N_EXPERT, TOK_DEV * 2, EXPERTS)
    before = jnp.cumsum(blocks, axis=1) - blocks
    places = lax.optimization_barrier(jnp.sum(before * blocks, axis=2)).reshape(TOKENS, 2).astype(jnp.int32)
    sources = (jnp.arange(TOKENS, dtype=jnp.int32) // TOK_DEV)[:, None]
    slot_rows = (sources * CAP + places).astype(jnp.int32)
    chosen = picks.astype(jnp.float32)
    logits = jnp.dot(tokens, router_weight, preferred_element_type=jnp.float32)
    picked = lax.optimization_barrier(jnp.sum(logits[:, None, :] * chosen, axis=2))
    sigmas = jax.nn.sigmoid(picked)
    denominator = lax.optimization_barrier(jnp.sum(sigmas, axis=1, keepdims=True))
    gates = sigmas / denominator
    scaled_cot = (gates[:, :, None] * cotangent.astype(jnp.float32)[:, None, :]).astype(jnp.bfloat16)
    flat_experts = routes.reshape(-1).astype(jnp.int32)
    flat_rows = slot_rows.reshape(-1)
    x_in = jnp.zeros((EXPERTS, EXPERTS * CAP, D), jnp.bfloat16).at[flat_experts, flat_rows].set(jnp.repeat(tokens, 2, axis=0))
    dy_in = jnp.zeros((EXPERTS, EXPERTS * CAP, D), jnp.bfloat16).at[flat_experts, flat_rows].set(scaled_cot.reshape(TOKENS * 2, D))
    expert_out, grad_gate, grad_up, grad_down = lax.map(expert_pass, (x_in, dy_in, gate_weight, up_weight, down_weight))
    routed = expert_out[flat_experts, flat_rows].astype(jnp.float32).reshape(TOKENS, 2, D)
    mixed = (tokens.astype(jnp.float32) + gates[:, 0:1] * routed[:, 0] + gates[:, 1:2] * routed[:, 1]).astype(jnp.bfloat16)
    gate_grads = lax.optimization_barrier(jnp.sum(cotangent.astype(jnp.float32)[:, None, :] * routed, axis=2))
    mean_part = lax.optimization_barrier(jnp.sum(gates * gate_grads, axis=1, keepdims=True))
    sigma_grads = (gate_grads - mean_part) / denominator
    logit_grads = sigma_grads * sigmas * (1.0 - sigmas)
    dense_grads = lax.optimization_barrier(jnp.sum(logit_grads[:, :, None] * chosen, axis=1)).astype(jnp.bfloat16)
    router_grad = jnp.dot(tokens.T, dense_grads, preferred_element_type=jnp.float32)
    total_count = EXPERTS * D * FF
    gate_rms = jnp.sqrt(jnp.sum(grad_gate * grad_gate) / total_count + EPSILON)
    up_rms = jnp.sqrt(jnp.sum(grad_up * grad_up) / total_count + EPSILON)
    down_rms = jnp.sqrt(jnp.sum(grad_down * grad_down) / total_count + EPSILON)
    router_rms = jnp.sqrt(jnp.sum(router_grad * router_grad) / (D * EXPERTS) + EPSILON)

    def expert_updates(operands):
        g_gate, g_up, g_down, w_gate, w_up, w_down = operands
        return (learned_step(g_gate, w_gate, D ** 0.5, gate_rms, mlp_in, mlp_bias, mlp_out), learned_step(g_up, w_up, D ** 0.5, up_rms, mlp_in, mlp_bias, mlp_out), learned_step(g_down, w_down, FF ** 0.5, down_rms, mlp_in, mlp_bias, mlp_out))
    gate_update, up_update, down_update = lax.map(expert_updates, (grad_gate, grad_up, grad_down, gate_weight, up_weight, down_weight))
    router_update = learned_step(router_grad, router_weight, D ** 0.5, router_rms, mlp_in, mlp_bias, mlp_out)
    return (mixed, gate_update, up_update, down_update, router_update)
```

```python
import functools

import jax
import jax.numpy as jnp
from jax import lax
from jax.experimental import pallas as pl
from jax.experimental.pallas import tpu as pltpu
from jax.sharding import Mesh
from jax.sharding import PartitionSpec as P

D = 1024
FF = 3584
UNITS = 16
EXPERT = ("expert_0", "expert_1", "expert_2")
EXPERT_MP = ("expert_0", "expert_1", "expert_2", "mp")
MP_EXPERT = ("mp", "expert_0", "expert_1", "expert_2")
EPSILON = 1e-06

CAP = 12
GROUP = 16
BLOCK = GROUP * CAP
LANES = 128
BF = jnp.bfloat16
F32 = jnp.float32
HIGHEST = lax.Precision.HIGHEST


def params(**kw):
    return pltpu.CompilerParams(vmem_limit_bytes=48 << 20, **kw)


def iota(shape, dim):
    return lax.broadcasted_iota(jnp.int32, shape, dim)


def dot(a, b, dims=((1,), (0,)), **kw):
    return lax.dot_general(a, b, (dims, ((), ())), preferred_element_type=F32, **kw)


def row_sum(x):
    return jnp.sum(x, axis=1, keepdims=True)


def send_kernel(mp, tok, tok_cols, cot_cols, routes, router, x_out, dy_out, aux_out):
    del mp
    n = tok.shape[0]
    experts = router.shape[1]
    rows = experts * 2 * CAP
    lane_e = iota((n, experts), 1)
    ids = [routes[:, k : k + 1] for k in range(2)]
    hits = [(ids[k] == lane_e).astype(F32) for k in range(2)]
    earlier = (iota((n, n), 0) > iota((n, n), 1)).astype(F32).astype(BF)
    before = dot(earlier, (hits[0] + hits[1]).astype(BF))
    places = [row_sum(before * hits[k]) for k in range(2)]
    base = [ids[k] * (2 * CAP) + places[k].astype(jnp.int32) for k in range(2)]
    lane_r = iota((n, rows), 1)
    picks = [
        [(base[k] + h * CAP == lane_r).astype(F32).astype(BF) for h in range(2)] for k in range(2)
    ]
    total = jnp.zeros((rows, LANES), F32)
    for h in range(2):
        total = total + dot(
            picks[0][h] + picks[1][h], tok_cols[:, h * LANES : (h + 1) * LANES], ((0,), (0,))
        )
    x_out[...] = total.astype(BF)
    logits = dot(tok[...], router[...])
    sig = [1.0 / (1.0 + jnp.exp(-row_sum(logits * hits[k]))) for k in range(2)]
    denominator = sig[0] + sig[1]
    gates = [s / denominator for s in sig]
    cot = cot_cols[...].astype(F32)
    total = jnp.zeros((rows, LANES), F32)
    for k in range(2):
        scaled = (gates[k] * cot).astype(BF)
        for h in range(2):
            total = total + dot(picks[k][h], scaled[:, h * LANES : (h + 1) * LANES], ((0,), (0,)))
    dy_out[...] = total.astype(BF)
    lane = iota((n, LANES), 1)
    aux = jnp.zeros((n, LANES), F32)
    columns = gates + sig + [i.astype(F32) for i in ids] + places
    for i, column in enumerate(columns):
        aux = jnp.where(lane == i, column, aux)
    aux_out[...] = aux


def send_rows(tokens, cotangent, routes, router_weight, mp_index):
    n, width = tokens.shape
    experts = router_weight.shape[1]
    cols = 2 * LANES
    rows = experts * 2 * CAP
    whole = lambda *shape: pl.BlockSpec(shape, lambda i, mp: (0,) * len(shape))
    mine = pl.BlockSpec((n, cols), lambda i, mp: (0, mp[0]))
    return pl.pallas_call(
        send_kernel,
        grid_spec=pltpu.PrefetchScalarGridSpec(
            num_scalar_prefetch=1,
            grid=(1,),
            in_specs=[whole(n, width), mine, mine, whole(n, 2), whole(width, experts)],
            out_specs=[whole(rows, LANES), whole(rows, LANES), whole(n, LANES)],
        ),
        out_shape=[
            jax.ShapeDtypeStruct((rows, LANES), BF),
            jax.ShapeDtypeStruct((rows, LANES), BF),
            jax.ShapeDtypeStruct((n, LANES), F32),
        ],
        compiler_params=params(),
        name="send_rows",
    )(mp_index, tokens, tokens, cotangent, routes, router_weight)


def unpack_rows(perm, messages, at, to, blocks):
    groups = messages.shape[0]
    for b in range(blocks):
        piece = jnp.concatenate(
            [messages[m, (at + b) * 2 * BLOCK : (at + b + 1) * 2 * BLOCK, :] for m in range(groups)],
            axis=1,
        )
        both = dot(perm, piece).astype(BF)
        for h in range(2):
            for m in range(groups):
                c = (2 * m + h) * LANES
                to[b * BLOCK : (b + 1) * BLOCK, c : c + LANES] = both[
                    h * BLOCK : (h + 1) * BLOCK, m * LANES : (m + 1) * LANES
                ]


def forward_kernel(perm, perm_t, msg, gate, up, down, rows_x, hidden, by_gate, by_up, parts):
    step = pl.program_id(0)

    @pl.when(step == 0)
    def _():
        unpack_rows(perm[...], msg, 0, rows_x, rows_x.shape[0] // BLOCK)

    acts = dot(rows_x[...], jnp.concatenate([gate[...], up[...]], axis=1))
    act_gate = acts[:, :LANES]
    act_up = acts[:, LANES:]
    s = 1.0 / (1.0 + jnp.exp(-act_gate))
    silu = act_gate * s
    hidden[:, pl.ds(pl.multiple_of(step * LANES, LANES), LANES)] = (silu * act_up).astype(BF)
    by_gate[...] = act_up * s * (1.0 + act_gate * (1.0 - s))
    by_up[...] = silu

    @pl.when(step == pl.num_programs(0) - 1)
    def _():
        groups = parts.shape[0]
        for b in range(rows_x.shape[0] // BLOCK):
            out = dot(hidden[b * BLOCK : (b + 1) * BLOCK, :], down[...]).astype(BF)
            halves = jnp.concatenate(
                [
                    jnp.concatenate(
                        [
                            out[:, (2 * m + h) * LANES : (2 * m + h + 1) * LANES]
                            for m in range(groups)
                        ],
                        axis=1,
                    )
                    for h in range(2)
                ],
                axis=0,
            )
            packed = dot(perm_t[...], halves).astype(BF)
            for m in range(groups):
                parts[m, b * 2 * BLOCK : (b + 1) * 2 * BLOCK, :] = packed[
                    :, m * LANES : (m + 1) * LANES
                ]


def expert_forward(perm, perm_t, messages, w_gate, w_up, w_down):
    groups, sent, _ = messages.shape
    rows = sent // 2
    width, ff = w_gate.shape
    whole = lambda *shape: pl.BlockSpec(shape, lambda i: (0,) * len(shape))
    column = lambda n: pl.BlockSpec((n, LANES), lambda i: (0, i))
    return pl.pallas_call(
        forward_kernel,
        grid=(ff // LANES,),
        in_specs=[
            whole(*perm.shape),
            whole(*perm.shape),
            whole(*messages.shape),
            column(width),
            column(width),
            whole(ff, width),
        ],
        out_specs=[
            whole(rows, width),
            whole(rows, ff),
            column(rows),
            column(rows),
            whole(groups, sent, LANES),
        ],
        out_shape=[
            jax.ShapeDtypeStruct((rows, width), BF),
            jax.ShapeDtypeStruct((rows, ff), BF),
            jax.ShapeDtypeStruct((rows, ff), F32),
            jax.ShapeDtypeStruct((rows, ff), F32),
            jax.ShapeDtypeStruct((groups, sent, LANES), BF),
        ],
        compiler_params=params(),
        name="expert_forward",
    )(perm, perm_t, messages, w_gate, w_up, w_down)


def slot_masks(rows):
    source = iota((rows // CAP, rows), 1) // CAP == iota((rows // CAP, rows), 0)
    slot = iota((rows, LANES), 0) % CAP == iota((rows, LANES), 1)
    return source.astype(F32), slot.astype(F32)


def backward_kernel(
    perm, source, slot, msg, down, hidden, by_gate, by_up, rows_dy, d_gate, d_up, q_out
):
    unpack_rows(perm[...], msg, 0, rows_dy, rows_dy.shape[0] // BLOCK)
    grad_hidden = dot(rows_dy[...], down[...], ((1,), (1,)))
    d_gate[...] = (grad_hidden * by_gate[...]).astype(BF)
    d_up[...] = (grad_hidden * by_up[...]).astype(BF)
    q = row_sum(hidden[...].astype(F32) * grad_hidden)
    q_out[...] = dot(source[...], q * slot[...], precision=HIGHEST)


def expert_backward(perm, messages, w_down, hidden, by_gate, by_up):
    groups, sent, _ = messages.shape
    steps = 2
    rows = sent // 2
    part = rows // steps
    ff, width = w_down.shape
    source, slot = slot_masks(part)
    whole = lambda *shape: pl.BlockSpec(shape, lambda i: (0,) * len(shape))
    row = lambda n, m: pl.BlockSpec((n, m), lambda i: (i, 0))
    return pl.pallas_call(
        backward_kernel,
        grid=(steps,),
        in_specs=[
            whole(*perm.shape),
            whole(*source.shape),
            whole(*slot.shape),
            pl.BlockSpec((groups, sent // steps, LANES), lambda i: (0, i, 0)),
            whole(ff, width),
            row(part, ff),
            row(part, ff),
            row(part, ff),
        ],
        out_specs=[row(part, width), row(part, ff), row(part, ff), row(part // CAP, LANES)],
        out_shape=[
            jax.ShapeDtypeStruct((rows, width), BF),
            jax.ShapeDtypeStruct((rows, ff), BF),
            jax.ShapeDtypeStruct((rows, ff), BF),
            jax.ShapeDtypeStruct((rows // CAP, LANES), F32),
        ],
        compiler_params=params(),
        name="expert_backward",
    )(perm, source, slot, messages, w_down, hidden, by_gate, by_up)


def add_squares(total, grad, to):
    step = pl.program_id(0)
    squares = jnp.sum(grad * grad, axis=0, keepdims=True)

    @pl.when(step == 0)
    def _():
        total[...] = squares

    @pl.when(step > 0)
    def _():
        total[...] += squares

    @pl.when(step == pl.num_programs(0) - 1)
    def _():
        to[...] = jnp.broadcast_to(row_sum(total[...]), to.shape)


def grad_in_kernel(rows_x, d_gate, d_up, g_gate, g_up, s_gate, s_up, t_gate, t_up):
    across = rows_x[...].T
    for d, g, s, t in ((d_gate, g_gate, s_gate, t_gate), (d_up, g_up, s_up, t_up)):
        grad = dot(across, d[...])
        g[...] = grad
        add_squares(t, grad, s)


def grad_in(rows_x, d_gate, d_up):
    rows, width = rows_x.shape
    ff = d_gate.shape[1]
    chunk = 256
    whole = lambda *shape: pl.BlockSpec(shape, lambda i: (0,) * len(shape))
    return pl.pallas_call(
        grad_in_kernel,
        grid=(width // chunk,),
        in_specs=[pl.BlockSpec((rows, chunk), lambda i: (0, i)), whole(rows, ff), whole(rows, ff)],
        out_specs=[pl.BlockSpec((chunk, ff), lambda i: (i, 0))] * 2 + [whole(1, LANES)] * 2,
        out_shape=[jax.ShapeDtypeStruct((width, ff), F32)] * 2
        + [jax.ShapeDtypeStruct((1, LANES), F32)] * 2,
        scratch_shapes=[pltpu.VMEM((1, ff), F32)] * 2,
        compiler_params=params(),
        name="grad_in",
    )(rows_x, d_gate, d_up)


def grad_down_kernel(hidden, rows_dy, g_down, s_down, across, total):
    @pl.when(pl.program_id(0) == 0)
    def _():
        across[...] = hidden[...].T

    grad = dot(across[...], rows_dy[...])
    g_down[...] = grad
    add_squares(total, grad, s_down)


def grad_down(hidden, rows_dy):
    rows, ff = hidden.shape
    width = rows_dy.shape[1]
    chunk = 256
    whole = lambda *shape: pl.BlockSpec(shape, lambda i: (0,) * len(shape))
    return pl.pallas_call(
        grad_down_kernel,
        grid=(width // chunk,),
        in_specs=[whole(rows, ff), pl.BlockSpec((rows, chunk), lambda i: (0, i))],
        out_specs=[pl.BlockSpec((ff, chunk), lambda i: (0, i)), whole(1, LANES)],
        out_shape=[
            jax.ShapeDtypeStruct((ff, width), F32),
            jax.ShapeDtypeStruct((1, LANES), F32),
        ],
        scratch_shapes=[pltpu.VMEM((ff, rows), BF), pltpu.VMEM((1, chunk), F32)],
        compiler_params=params(),
        name="grad_down",
    )(hidden, rows_dy)


NET_ROWS = 32


def two_parts(x):
    high = x.astype(BF)
    return high, (x - high.astype(F32)).astype(BF)


def spread_kernel(coef, to):
    k = UNITS * NET_ROWS
    c = 8 * NET_ROWS
    same = iota((k, c), 0) % NET_ROWS == iota((k, c), 1) % NET_ROWS
    feature = iota((k, c), 1) // NET_ROWS
    value = jnp.zeros((k, c), F32)
    for part in range(3):
        a = coef[:, part : part + 1]
        high = a.astype(BF).astype(F32)
        low = a - high
        if part < 2:
            values = (high, low, high)
        else:
            values = (high, low)
        for i, v in enumerate(values):
            value = jnp.where(feature == part * 3 + i, v, value)
    to[...] = jnp.where(same, value, 0.0).astype(BF)


def spread_weights(mlp_in, weight_scale):
    coef = jnp.stack([mlp_in[0], mlp_in[2], mlp_in[1] * weight_scale], axis=1)
    coef = jnp.repeat(coef, NET_ROWS, axis=0)
    return pl.pallas_call(
        spread_kernel,
        out_shape=jax.ShapeDtypeStruct((UNITS * NET_ROWS, 8 * NET_ROWS), BF),
        compiler_params=params(),
        name="spread_weights",
    )(coef)


def step_kernel(scalars, rms, spread, grad, weight, out, *, rows):
    n = NET_ROWS
    height, width = grad.shape
    inverse = rms[0]
    constant = scalars[2, 0]

    def features(r, c, lanes):
        w = weight[pl.ds(r, n), c : c + lanes]
        f0 = grad[pl.ds(r, n), c : c + lanes] * inverse
        h0, l0 = two_parts(f0)
        h2, l2 = two_parts(jnp.tanh(f0))
        return jnp.concatenate([h0, h0, l0, h2, h2, l2, w, w], axis=0)

    def network(feats):
        y = dot(spread[...], feats)
        total = jnp.full((n, feats.shape[1]), constant, F32)
        for j in range(UNITS):
            total = total + scalars[1, j] * jnp.maximum(y[j * n : (j + 1) * n], scalars[0, j])
        return total.astype(BF)

    def body(i, carry):
        r = pl.multiple_of(i * rows, rows)
        for pair in range(0, rows, 2 * n):
            at = [r + pair, r + pair + n]
            whole = width // 256 * 256
            for c in range(0, whole, 256):
                for a in at:
                    out[pl.ds(a, n), c : c + 256] = network(features(a, c, 256))
            if whole < width:
                u = network(jnp.concatenate([features(a, whole, 128) for a in at], axis=1))
                for i, a in enumerate(at):
                    out[pl.ds(a, n), whole:width] = u[:, i * 128 : (i + 1) * 128]
        return carry

    lax.fori_loop(0, height // rows, body, 0)


def learned_step(grad, weight, rms, spread, scalars):
    height, width = grad.shape
    block = 128
    tile = pl.BlockSpec((block, width), lambda i: (i, 0))
    return pl.pallas_call(
        functools.partial(step_kernel, rows=128),
        grid=(height // block,),
        in_specs=[
            pl.BlockSpec(memory_space=pltpu.SMEM),
            pl.BlockSpec(memory_space=pltpu.SMEM),
            pl.BlockSpec(spread.shape, lambda i: (0, 0)),
            tile,
            tile,
        ],
        out_specs=tile,
        out_shape=jax.ShapeDtypeStruct((height, width), BF),
        compiler_params=params(),
        name="learned_step",
    )(scalars, rms, spread, grad, weight)


def mix_kernel(mp, aux, tok_cols, back, out):
    del mp
    n = aux.shape[0]
    rows = back.shape[0]
    lane = iota((n, rows), 1)
    for h in range(2):
        total = tok_cols[:, h * LANES : (h + 1) * LANES].astype(F32)
        for k in range(2):
            base = (aux[:, 4 + k : 5 + k] * (2 * CAP) + aux[:, 6 + k : 7 + k]).astype(jnp.int32)
            pick = (base + h * CAP == lane).astype(F32).astype(BF)
            total = total + aux[:, k : k + 1] * dot(pick, back[...])
        out[:, h * LANES : (h + 1) * LANES] = total.astype(BF)


def mix(mp_index, aux, tokens, back):
    n = tokens.shape[0]
    cols = 2 * LANES
    whole = lambda *shape: pl.BlockSpec(shape, lambda i, mp: (0,) * len(shape))
    return pl.pallas_call(
        mix_kernel,
        grid_spec=pltpu.PrefetchScalarGridSpec(
            num_scalar_prefetch=1,
            grid=(1,),
            in_specs=[
                whole(n, LANES),
                pl.BlockSpec((n, cols), lambda i, mp: (0, mp[0])),
                whole(*back.shape),
            ],
            out_specs=whole(n, cols),
        ),
        out_shape=jax.ShapeDtypeStruct((n, cols), BF),
        compiler_params=params(),
        name="mix",
    )(mp_index, aux, tokens, back)


def logit_kernel(aux, q, out):
    n = aux.shape[0]
    experts = q.shape[0]
    hits = []
    slots = []
    got = []
    for k in range(2):
        expert = aux[:, 4 + k : 5 + k].astype(jnp.int32)
        place = aux[:, 6 + k : 7 + k].astype(jnp.int32)
        hits.append((expert == iota((n, experts), 1)).astype(F32))
        slots.append((place == iota((n, LANES), 1)).astype(F32))
        got.append(row_sum(dot(hits[k], q[...], precision=HIGHEST) * slots[k]))
    both = got[0] + got[1]
    total = jnp.zeros((experts, LANES), F32)
    for k in range(2):
        grad = (got[k] - aux[:, k : k + 1] * both) * (1.0 - aux[:, 2 + k : 3 + k])
        total = total + dot(hits[k], slots[k] * grad, ((0,), (0,)), precision=HIGHEST)
    out[...] = total


def logit_grads(aux, q):
    return pl.pallas_call(
        logit_kernel,
        out_shape=jax.ShapeDtypeStruct(q.shape, F32),
        compiler_params=params(),
        name="logit_grads",
    )(aux, q)


def router_kernel(source, slot, grads, rows_x, out):
    column = row_sum(dot(source[...], grads[...], ((0,), (0,)), precision=HIGHEST) * slot[...])
    total = jnp.zeros((1, rows_x.shape[1]), F32)
    part = rows_x.shape[0] // 4
    for b in range(4):
        at = slice(b * part, (b + 1) * part)
        total = total + jnp.sum(rows_x[at, :].astype(F32) * column[at, :], axis=0, keepdims=True)
    out[...] = total


def router_column(grads, rows_x):
    source, slot = slot_masks(rows_x.shape[0])
    return pl.pallas_call(
        router_kernel,
        out_shape=jax.ShapeDtypeStruct((1, rows_x.shape[1]), F32),
        compiler_params=params(),
        name="router_column",
    )(source, slot, grads, rows_x)


def router_step_kernel(net, parts, weight, out):
    experts = weight.shape[0]
    grad = parts[0:experts, :]
    for m in range(1, parts.shape[0] // experts):
        grad = grad + parts[m * experts : (m + 1) * experts, :]
    mean = jnp.sum(row_sum(grad * grad), axis=0, keepdims=True) * (1.0 / grad.size)
    f0 = grad / jnp.sqrt(mean + EPSILON)
    f1 = weight[...].astype(F32) * D**0.5
    f2 = jnp.tanh(f0)
    total = jnp.zeros_like(f0)
    for j in range(UNITS):
        total = total + net[4, j] * jnp.maximum(
            net[0, j] * f0 + net[1, j] * f1 + net[2, j] * f2 + net[3, j], 0.0
        )
    out[...] = total.T.astype(BF)


def router_step(net, parts, weight):
    return pl.pallas_call(
        router_step_kernel,
        in_specs=[
            pl.BlockSpec(memory_space=pltpu.SMEM),
            pl.BlockSpec(memory_space=pltpu.VMEM),
            pl.BlockSpec(memory_space=pltpu.VMEM),
        ],
        out_shape=jax.ShapeDtypeStruct(weight.shape[::-1], BF),
        compiler_params=params(),
        name="router_step",
    )(net, parts, weight)


def to_experts(x, peers):
    sent = x.reshape(peers, x.shape[0] // peers, x.shape[1])
    return lax.all_to_all(sent, EXPERT, 0, 0, tiled=True).reshape(x.shape)


def on_device(
    tokens,
    cotangent,
    routes,
    router_weight,
    gate_weight,
    up_weight,
    down_weight,
    mlp_in,
    mlp_bias,
    mlp_out,
):
    experts = lax.axis_size(EXPERT)
    groups = lax.axis_size("mp")
    width = tokens.shape[1]
    mp_index = lax.axis_index("mp").astype(jnp.int32).reshape(1)
    w_gate = gate_weight[0]
    w_up = up_weight[0]
    w_down = down_weight[0]

    pos = jnp.arange(2 * BLOCK, dtype=jnp.int32)
    inner = pos % BLOCK
    source_row = inner + inner // CAP * CAP + pos // BLOCK * CAP
    perm = (source_row[:, None] == pos[None, :]).astype(BF)
    perm_t = (source_row[None, :] == pos[:, None]).astype(BF)
    spread_in = spread_weights(mlp_in, D**0.5)
    spread_down = spread_weights(mlp_in, FF**0.5)
    scalars = jnp.stack(
        [-mlp_bias, mlp_out, jnp.broadcast_to(jnp.sum(mlp_bias * mlp_out), mlp_out.shape)]
    )
    net = jnp.concatenate([mlp_in, mlp_bias[None], mlp_out[None]], axis=0)
    router_across = router_weight.T

    send_x, send_dy, aux = send_rows(tokens, cotangent, routes, router_weight, mp_index)
    msg_x = lax.all_gather(to_experts(send_x, experts), "mp")
    msg_dy = lax.all_gather(to_experts(send_dy, experts), "mp")

    rows_x, hidden, by_gate, by_up, parts = expert_forward(
        perm, perm_t, msg_x, w_gate, w_up, w_down
    )
    swapped = lax.all_to_all(parts, "mp", 0, 0, tiled=True)
    expert_out = jnp.sum(swapped.astype(F32), axis=0).astype(BF)
    back = to_experts(expert_out, experts)

    rows_dy, d_gate, d_up, q = expert_backward(perm, msg_dy, w_down, hidden, by_gate, by_up)
    q_back = lax.all_to_all(q, EXPERT, 0, 0, tiled=True)
    g_gate, g_up, s_gate, s_up = grad_in(rows_x, d_gate, d_up)
    g_down, s_down = grad_down(hidden, rows_dy)
    squares = lax.psum(jnp.stack([s_gate[0, 0], s_up[0, 0], s_down[0, 0]]), EXPERT_MP)
    total_count = experts * width * w_gate.shape[1] * groups
    inverse = 1.0 / jnp.sqrt(squares / total_count + EPSILON)

    lg = lax.all_to_all(logit_grads(aux, q_back), EXPERT, 0, 0, tiled=True)
    column = router_column(lg, rows_x)
    router_parts = lax.all_gather(column, MP_EXPERT, tiled=True)

    gate_update = learned_step(g_gate, w_gate, inverse[0:1], spread_in, scalars)
    up_update = learned_step(g_up, w_up, inverse[1:2], spread_in, scalars)
    down_update = learned_step(g_down, w_down, inverse[2:3], spread_down, scalars)
    mixed = mix(mp_index, aux, tokens, back)
    router_update = router_step(net, router_parts, router_across)
    return (mixed, gate_update[None], up_update[None], down_update[None], router_update)


def solution(mesh):
    torus = Mesh(
        mesh.devices.reshape(8, 4, 2, mesh.shape["mp"]), ("expert_0", "expert_1", "expert_2", "mp")
    )
    placed = (
        P(EXPERT, None),
        P(EXPERT, None),
        P(EXPERT, None),
        P(),
        P(EXPERT, None, "mp"),
        P(EXPERT, None, "mp"),
        P(EXPERT, "mp", None),
        P(),
        P(),
        P(),
    )
    return jax.shard_map(
        on_device,
        mesh=torus,
        in_specs=placed,
        out_specs=(
            P(EXPERT, "mp"),
            P(EXPERT, None, "mp"),
            P(EXPERT, None, "mp"),
            P(EXPERT, "mp", None),
            P(),
        ),
        check_vma=False,
    )
```

```python
import functools

import jax
import jax.numpy as jnp
from jax import lax
from jax.experimental import pallas as pl
from jax.experimental.pallas import tpu as pltpu
from jax.sharding import Mesh
from jax.sharding import PartitionSpec as P

D = 1024
FF = 3584
UNITS = 16
EXPERT = ("expert_0", "expert_1", "expert_2")
EPSILON = 1e-06

CAP = 12
GROUP = 16
GROUPS = 4
BLOCK = GROUP * CAP
LANES = 128
BF = jnp.bfloat16
F32 = jnp.float32
HIGHEST = lax.Precision.HIGHEST


def params(**kw):
    return pltpu.CompilerParams(vmem_limit_bytes=48 << 20, **kw)


def iota(shape, dim):
    return lax.broadcasted_iota(jnp.int32, shape, dim)


def dot(a, b, dims=((1,), (0,)), **kw):
    return lax.dot_general(a, b, (dims, ((), ())), preferred_element_type=F32, **kw)


def row_sum(x):
    return jnp.sum(x, axis=1, keepdims=True)


def send_kernel(mp, tok, tok_cols, cot_cols, routes, router, x_out, dy_out, aux_out):
    del mp
    n = tok.shape[0]
    experts = router.shape[1]
    rows = experts * 2 * CAP
    lane_e = iota((n, experts), 1)
    ids = [routes[:, k : k + 1] for k in range(2)]
    hits = [(ids[k] == lane_e).astype(F32) for k in range(2)]
    earlier = (iota((n, n), 0) > iota((n, n), 1)).astype(F32).astype(BF)
    before = dot(earlier, (hits[0] + hits[1]).astype(BF))
    places = [row_sum(before * hits[k]) for k in range(2)]
    base = [ids[k] * (2 * CAP) + places[k].astype(jnp.int32) for k in range(2)]
    lane_r = iota((n, rows), 1)
    picks = [
        [(base[k] + h * CAP == lane_r).astype(F32).astype(BF) for h in range(2)] for k in range(2)
    ]
    total = jnp.zeros((rows, LANES), F32)
    for h in range(2):
        total = total + dot(
            picks[0][h] + picks[1][h], tok_cols[:, h * LANES : (h + 1) * LANES], ((0,), (0,))
        )
    x_out[...] = total.astype(BF)
    logits = dot(tok[...], router[...])
    sig = [1.0 / (1.0 + jnp.exp(-row_sum(logits * hits[k]))) for k in range(2)]
    denominator = sig[0] + sig[1]
    gates = [s / denominator for s in sig]
    cot = cot_cols[...].astype(F32)
    total = jnp.zeros((rows, LANES), F32)
    for k in range(2):
        scaled = (gates[k] * cot).astype(BF)
        for h in range(2):
            total = total + dot(picks[k][h], scaled[:, h * LANES : (h + 1) * LANES], ((0,), (0,)))
    dy_out[...] = total.astype(BF)
    lane = iota((n, LANES), 1)
    aux = jnp.zeros((n, LANES), F32)
    columns = gates + sig + [i.astype(F32) for i in ids] + places
    for i, column in enumerate(columns):
        aux = jnp.where(lane == i, column, aux)
    aux_out[...] = aux


def send_rows(tokens, cotangent, routes, router_weight, mp_index):
    n, width = tokens.shape
    experts = router_weight.shape[1]
    cols = 2 * LANES
    rows = experts * 2 * CAP
    whole = lambda *shape: pl.BlockSpec(shape, lambda i, mp: (0,) * len(shape))
    mine = pl.BlockSpec((n, cols), lambda i, mp: (0, mp[0]))
    return pl.pallas_call(
        send_kernel,
        grid_spec=pltpu.PrefetchScalarGridSpec(
            num_scalar_prefetch=1,
            grid=(1,),
            in_specs=[whole(n, width), mine, mine, whole(n, 2), whole(width, experts)],
            out_specs=[whole(rows, LANES), whole(rows, LANES), whole(n, LANES)],
        ),
        out_shape=[
            jax.ShapeDtypeStruct((rows, LANES), BF),
            jax.ShapeDtypeStruct((rows, LANES), BF),
            jax.ShapeDtypeStruct((n, LANES), F32),
        ],
        compiler_params=params(),
        name="send_rows",
    )(mp_index, tokens, tokens, cotangent, routes, router_weight)


def column_of(mp, k, h):
    member = lax.rem(mp + k + GROUPS, GROUPS)
    return pl.multiple_of((2 * member + h) * LANES, LANES)


def unpack_rows(perm, mp, messages, to, blocks):
    for b in range(blocks):
        at = slice(b * 2 * BLOCK, (b + 1) * 2 * BLOCK)
        both = dot(perm, jnp.concatenate([m[at, :] for m in messages], axis=1)).astype(BF)
        for h in range(2):
            for k in range(GROUPS):
                to[b * BLOCK : (b + 1) * BLOCK, pl.ds(column_of(mp, -k, h), LANES)] = both[
                    h * BLOCK : (h + 1) * BLOCK, k * LANES : (k + 1) * LANES
                ]


def forward_kernel(mp, perm, perm_t, m0, m1, m2, m3, gate, up, down, *refs):
    rows_x, hidden, by_gate, by_up = refs[:4]
    parts = refs[4 : 4 + GROUPS]
    outs = refs[4 + GROUPS]
    step = pl.program_id(0)
    blocks = rows_x.shape[0] // BLOCK

    @pl.when(step == 0)
    def _():
        unpack_rows(perm[...], mp[0], (m0, m1, m2, m3), rows_x, blocks)

    acts = dot(rows_x[...], jnp.concatenate([gate[...], up[...]], axis=1))
    act_gate = acts[:, :LANES]
    act_up = acts[:, LANES:]
    s = 1.0 / (1.0 + jnp.exp(-act_gate))
    silu = act_gate * s
    hidden[:, pl.ds(pl.multiple_of(step * LANES, LANES), LANES)] = (silu * act_up).astype(BF)
    by_gate[...] = act_up * s * (1.0 + act_gate * (1.0 - s))
    by_up[...] = silu

    @pl.when(step == pl.num_programs(0) - 1)
    def _():
        outs[...] = dot(hidden[...], down[...]).astype(BF)
        for b in range(blocks):
            halves = [
                jnp.concatenate(
                    [
                        outs[b * BLOCK : (b + 1) * BLOCK, pl.ds(column_of(mp[0], k, h), LANES)]
                        for k in range(GROUPS)
                    ],
                    axis=1,
                )
                for h in range(2)
            ]
            packed = dot(perm_t[...], jnp.concatenate(halves, axis=0)).astype(BF)
            for k in range(GROUPS):
                parts[k][b * 2 * BLOCK : (b + 1) * 2 * BLOCK, :] = packed[
                    :, k * LANES : (k + 1) * LANES
                ]


def expert_forward(mp_index, perm, perm_t, messages, w_gate, w_up, w_down):
    sent, _ = messages[0].shape
    rows = sent // 2
    width, ff = w_gate.shape
    whole = lambda *shape: pl.BlockSpec(shape, lambda i, mp: (0,) * len(shape))
    column = lambda n: pl.BlockSpec((n, LANES), lambda i, mp: (0, i))
    return pl.pallas_call(
        forward_kernel,
        grid_spec=pltpu.PrefetchScalarGridSpec(
            num_scalar_prefetch=1,
            grid=(ff // LANES,),
            in_specs=[whole(*perm.shape), whole(*perm.shape)]
            + [whole(sent, LANES)] * GROUPS
            + [column(width), column(width), whole(ff, width)],
            out_specs=[whole(rows, width), whole(rows, ff), column(rows), column(rows)]
            + [whole(sent, LANES)] * GROUPS,
            scratch_shapes=[pltpu.VMEM((rows, width), BF)],
        ),
        out_shape=[
            jax.ShapeDtypeStruct((rows, width), BF),
            jax.ShapeDtypeStruct((rows, ff), BF),
            jax.ShapeDtypeStruct((rows, ff), F32),
            jax.ShapeDtypeStruct((rows, ff), F32),
        ]
        + [jax.ShapeDtypeStruct((sent, LANES), BF)] * GROUPS,
        compiler_params=params(),
        name="expert_forward",
    )(mp_index, perm, perm_t, *messages, w_gate, w_up, w_down)


def slot_masks(rows):
    source = iota((rows // CAP, rows), 1) // CAP == iota((rows // CAP, rows), 0)
    slot = iota((rows, LANES), 0) % CAP == iota((rows, LANES), 1)
    return source.astype(F32), slot.astype(F32)


def backward_kernel(mp, perm, m0, m1, m2, m3, down, by_gate, by_up, rows_dy, d_gate, d_up):
    unpack_rows(perm[...], mp[0], (m0, m1, m2, m3), rows_dy, rows_dy.shape[0] // BLOCK)
    grad_hidden = dot(rows_dy[...], down[...], ((1,), (1,)))
    d_gate[...] = (grad_hidden * by_gate[...]).astype(BF)
    d_up[...] = (grad_hidden * by_up[...]).astype(BF)


def expert_backward(mp_index, perm, messages, w_down, by_gate, by_up):
    sent, _ = messages[0].shape
    steps = 2
    rows = sent // 2
    part = rows // steps
    ff, width = w_down.shape
    whole = lambda *shape: pl.BlockSpec(shape, lambda i, mp: (0,) * len(shape))
    row = lambda n, m: pl.BlockSpec((n, m), lambda i, mp: (i, 0))
    return pl.pallas_call(
        backward_kernel,
        grid_spec=pltpu.PrefetchScalarGridSpec(
            num_scalar_prefetch=1,
            grid=(steps,),
            in_specs=[whole(*perm.shape)]
            + [row(sent // steps, LANES)] * GROUPS
            + [whole(ff, width), row(part, ff), row(part, ff)],
            out_specs=[row(part, width), row(part, ff), row(part, ff)],
        ),
        out_shape=[
            jax.ShapeDtypeStruct((rows, width), BF),
            jax.ShapeDtypeStruct((rows, ff), BF),
            jax.ShapeDtypeStruct((rows, ff), BF),
        ],
        compiler_params=params(),
        name="expert_backward",
    )(mp_index, perm, *messages, w_down, by_gate, by_up)


def add_squares(total, grad, to):
    step = pl.program_id(0)
    squares = jnp.sum(grad * grad, axis=0, keepdims=True)

    @pl.when(step == 0)
    def _():
        total[...] = squares

    @pl.when(step > 0)
    def _():
        total[...] += squares

    @pl.when(step == pl.num_programs(0) - 1)
    def _():
        to[...] = jnp.broadcast_to(row_sum(total[...]), to.shape)


def grad_in_kernel(rows_x, d_gate, d_up, g_gate, g_up, s_gate, s_up, t_gate, t_up):
    across = rows_x[...].T
    for d, g, s, t in ((d_gate, g_gate, s_gate, t_gate), (d_up, g_up, s_up, t_up)):
        grad = dot(across, d[...])
        g[...] = grad
        add_squares(t, grad, s)


def grad_in(rows_x, d_gate, d_up):
    rows, width = rows_x.shape
    ff = d_gate.shape[1]
    chunk = 256
    whole = lambda *shape: pl.BlockSpec(shape, lambda i: (0,) * len(shape))
    return pl.pallas_call(
        grad_in_kernel,
        grid=(width // chunk,),
        in_specs=[pl.BlockSpec((rows, chunk), lambda i: (0, i)), whole(rows, ff), whole(rows, ff)],
        out_specs=[pl.BlockSpec((chunk, ff), lambda i: (i, 0))] * 2 + [whole(1, LANES)] * 2,
        out_shape=[jax.ShapeDtypeStruct((width, ff), F32)] * 2
        + [jax.ShapeDtypeStruct((1, LANES), F32)] * 2,
        scratch_shapes=[pltpu.VMEM((1, ff), F32)] * 2,
        compiler_params=params(),
        name="grad_in",
    )(rows_x, d_gate, d_up)


def grad_down_kernel(hidden, rows_dy, g_down, s_down, across, total):
    @pl.when(pl.program_id(0) == 0)
    def _():
        across[...] = hidden[...].T

    grad = dot(across[...], rows_dy[...])
    g_down[...] = grad
    add_squares(total, grad, s_down)


def grad_down(hidden, rows_dy):
    rows, ff = hidden.shape
    width = rows_dy.shape[1]
    chunk = 256
    whole = lambda *shape: pl.BlockSpec(shape, lambda i: (0,) * len(shape))
    return pl.pallas_call(
        grad_down_kernel,
        grid=(width // chunk,),
        in_specs=[whole(rows, ff), pl.BlockSpec((rows, chunk), lambda i: (0, i))],
        out_specs=[pl.BlockSpec((ff, chunk), lambda i: (0, i)), whole(1, LANES)],
        out_shape=[
            jax.ShapeDtypeStruct((ff, width), F32),
            jax.ShapeDtypeStruct((1, LANES), F32),
        ],
        scratch_shapes=[pltpu.VMEM((ff, rows), BF), pltpu.VMEM((1, chunk), F32)],
        compiler_params=params(),
        name="grad_down",
    )(hidden, rows_dy)


NET_ROWS = 32


def two_parts(x):
    high = x.astype(BF)
    return high, (x - high.astype(F32)).astype(BF)


def spread_kernel(coef, to):
    k = UNITS * NET_ROWS
    c = 8 * NET_ROWS
    same = iota((k, c), 0) % NET_ROWS == iota((k, c), 1) % NET_ROWS
    feature = iota((k, c), 1) // NET_ROWS
    value = jnp.zeros((k, c), F32)
    for part in range(3):
        a = coef[:, part : part + 1]
        high = a.astype(BF).astype(F32)
        low = a - high
        if part < 2:
            values = (high, low, high)
        else:
            values = (high, low)
        for i, v in enumerate(values):
            value = jnp.where(feature == part * 3 + i, v, value)
    to[...] = jnp.where(same, value, 0.0).astype(BF)


def spread_weights(mlp_in, weight_scale):
    coef = jnp.stack([mlp_in[0], mlp_in[2], mlp_in[1] * weight_scale], axis=1)
    coef = jnp.repeat(coef, NET_ROWS, axis=0)
    return pl.pallas_call(
        spread_kernel,
        out_shape=jax.ShapeDtypeStruct((UNITS * NET_ROWS, 8 * NET_ROWS), BF),
        compiler_params=params(),
        name="spread_weights",
    )(coef)


def step_kernel(scalars, rms, spread, grad, weight, *refs, rows):
    out = refs[-1]
    n = NET_ROWS
    height, width = grad.shape
    inverse = rms[0]
    constant = scalars[2, 0]

    def features(r, c, lanes):
        w = weight[pl.ds(r, n), c : c + lanes]
        f0 = grad[pl.ds(r, n), c : c + lanes] * inverse
        h0, l0 = two_parts(f0)
        h2, l2 = two_parts(jnp.tanh(f0))
        return jnp.concatenate([h0, h0, l0, h2, h2, l2, w, w], axis=0)

    def network(feats):
        y = dot(spread[...], feats)
        total = jnp.full((n, feats.shape[1]), constant, F32)
        for j in range(UNITS):
            total = total + scalars[1, j] * jnp.maximum(y[j * n : (j + 1) * n], scalars[0, j])
        return total.astype(BF)

    def body(i, carry):
        r = pl.multiple_of(i * rows, rows)
        for pair in range(0, rows, 2 * n):
            at = [r + pair, r + pair + n]
            whole = width // 256 * 256
            for c in range(0, whole, 256):
                for a in at:
                    out[pl.ds(a, n), c : c + 256] = network(features(a, c, 256))
            if whole < width:
                u = network(jnp.concatenate([features(a, whole, 128) for a in at], axis=1))
                for i, a in enumerate(at):
                    out[pl.ds(a, n), whole:width] = u[:, i * 128 : (i + 1) * 128]
        return carry

    lax.fori_loop(0, height // rows, body, 0)


def learned_step(grad, weight, rms, spread, scalars, half=None, into=None):
    height, width = grad.shape
    block = 128
    steps = height // block
    first = 0
    if half is not None:
        steps = steps // 2
        first = half * steps
    tile = pl.BlockSpec((block, width), lambda i: (first + i, 0))
    operands = [scalars, rms, spread, grad, weight]
    in_specs = [
        pl.BlockSpec(memory_space=pltpu.SMEM),
        pl.BlockSpec(memory_space=pltpu.SMEM),
        pl.BlockSpec(spread.shape, lambda i: (0, 0)),
        tile,
        tile,
    ]
    aliases = {}
    if into is not None:
        operands.append(into)
        in_specs.append(pl.BlockSpec(memory_space=pl.ANY))
        aliases = {5: 0}
    return pl.pallas_call(
        functools.partial(step_kernel, rows=128),
        grid=(steps,),
        in_specs=in_specs,
        out_specs=tile,
        out_shape=jax.ShapeDtypeStruct((height, width), BF),
        input_output_aliases=aliases,
        compiler_params=params(),
        name="learned_step",
    )(*operands)


def mix_kernel(mp, aux, tok_cols, cot_cols, back, out, lg_out):
    del mp
    n = aux.shape[0]
    rows = back.shape[0]
    experts = lg_out.shape[0]
    lane = iota((n, rows), 1)
    gates = [aux[:, k : k + 1] for k in range(2)]
    ids = [aux[:, 4 + k : 5 + k].astype(jnp.int32) for k in range(2)]
    places = [aux[:, 6 + k : 7 + k].astype(jnp.int32) for k in range(2)]
    products = [jnp.zeros((n, 1), F32) for _ in range(2)]
    for h in range(2):
        cols = slice(h * LANES, (h + 1) * LANES)
        total = tok_cols[:, cols].astype(F32)
        cot = cot_cols[:, cols].astype(F32)
        for k in range(2):
            pick = ids[k] * (2 * CAP) + places[k] + h * CAP == lane
            routed = dot(pick.astype(F32).astype(BF), back[...])
            total = total + gates[k] * routed
            products[k] = products[k] + row_sum(cot * routed)
        out[:, cols] = total.astype(BF)
    weighted = [gates[k] * products[k] for k in range(2)]
    both = weighted[0] + weighted[1]
    total = jnp.zeros((experts, LANES), F32)
    for k in range(2):
        grad = (weighted[k] - gates[k] * both) * (1.0 - aux[:, 2 + k : 3 + k])
        hit = (ids[k] == iota((n, experts), 1)).astype(F32)
        slot = (places[k] == iota((n, LANES), 1)).astype(F32)
        total = total + dot(hit, slot * grad, ((0,), (0,)), precision=HIGHEST)
    lg_out[...] = total


def mix(mp_index, aux, tokens, cotangent, back):
    n = tokens.shape[0]
    cols = 2 * LANES
    experts = back.shape[0] // (2 * CAP)
    whole = lambda *shape: pl.BlockSpec(shape, lambda i, mp: (0,) * len(shape))
    mine = pl.BlockSpec((n, cols), lambda i, mp: (0, mp[0]))
    return pl.pallas_call(
        mix_kernel,
        grid_spec=pltpu.PrefetchScalarGridSpec(
            num_scalar_prefetch=1,
            grid=(1,),
            in_specs=[whole(n, LANES), mine, mine, whole(*back.shape)],
            out_specs=[whole(n, cols), whole(experts, LANES)],
        ),
        out_shape=[
            jax.ShapeDtypeStruct((n, cols), BF),
            jax.ShapeDtypeStruct((experts, LANES), F32),
        ],
        compiler_params=params(),
        name="mix",
    )(mp_index, aux, tokens, cotangent, back)


def router_kernel(source, slot, grads, rows_x, out):
    column = row_sum(dot(source[...], grads[...], ((0,), (0,)), precision=HIGHEST) * slot[...])
    total = jnp.zeros((1, rows_x.shape[1]), F32)
    part = rows_x.shape[0] // 4
    for b in range(4):
        at = slice(b * part, (b + 1) * part)
        total = total + jnp.sum(rows_x[at, :].astype(F32) * column[at, :], axis=0, keepdims=True)
    for j in range(out.shape[0]):
        out[j : j + 1, :] = total[:, j * LANES : (j + 1) * LANES]


def router_column(grads, rows_x):
    source, slot = slot_masks(rows_x.shape[0])
    return pl.pallas_call(
        router_kernel,
        out_shape=jax.ShapeDtypeStruct((rows_x.shape[1] // LANES, LANES), F32),
        compiler_params=params(),
        name="router_column",
    )(source, slot, grads, rows_x)


def router_step_kernel(net, columns, weight, out):
    experts, width = weight.shape
    grad = jnp.concatenate([columns[:, j, :] for j in range(width // LANES)], axis=1)
    mean = jnp.sum(row_sum(grad * grad), axis=0, keepdims=True) * (1.0 / grad.size)
    f0 = grad / jnp.sqrt(mean + EPSILON)
    f1 = weight[...].astype(F32) * D**0.5
    f2 = jnp.tanh(f0)
    total = jnp.zeros_like(f0)
    for j in range(UNITS):
        total = total + net[4, j] * jnp.maximum(
            net[0, j] * f0 + net[1, j] * f1 + net[2, j] * f2 + net[3, j], 0.0
        )
    out[...] = total.T.astype(BF)


def router_step(net, parts, weight):
    return pl.pallas_call(
        router_step_kernel,
        in_specs=[
            pl.BlockSpec(memory_space=pltpu.SMEM),
            pl.BlockSpec(memory_space=pltpu.VMEM),
            pl.BlockSpec(memory_space=pltpu.VMEM),
        ],
        out_shape=jax.ShapeDtypeStruct(weight.shape[::-1], BF),
        compiler_params=params(),
        name="router_step",
    )(net, parts, weight)


def to_experts(x, peers):
    sent = x.reshape(peers, x.shape[0] // peers, x.shape[1])
    return lax.all_to_all(sent, EXPERT, 0, 0, tiled=True).reshape(x.shape)


def from_members(pieces):
    return [pieces[0]] + [
        lax.ppermute(pieces[k], "mp", [(i, (i + k) % GROUPS) for i in range(GROUPS)])
        for k in range(1, GROUPS)
    ]


def together(values):
    return lax.optimization_barrier(values)


def to_all_experts(x, peers):
    return lax.all_to_all(jnp.broadcast_to(x[None], (peers, *x.shape)), EXPERT, 0, 0, tiled=True)


def on_device(
    tokens,
    cotangent,
    routes,
    router_weight,
    gate_weight,
    up_weight,
    down_weight,
    mlp_in,
    mlp_bias,
    mlp_out,
):
    experts = lax.axis_size(EXPERT)
    groups = lax.axis_size("mp")
    width = tokens.shape[1]
    mp_index = lax.axis_index("mp").astype(jnp.int32).reshape(1)
    w_gate = gate_weight[0]
    w_up = up_weight[0]
    w_down = down_weight[0]

    pos = jnp.arange(2 * BLOCK, dtype=jnp.int32)
    inner = pos % BLOCK
    source_row = inner + inner // CAP * CAP + pos // BLOCK * CAP
    perm = (source_row[:, None] == pos[None, :]).astype(BF)
    perm_t = (source_row[None, :] == pos[:, None]).astype(BF)
    spread_in = spread_weights(mlp_in, D**0.5)
    spread_down = spread_weights(mlp_in, FF**0.5)
    scalars = jnp.stack(
        [-mlp_bias, mlp_out, jnp.broadcast_to(jnp.sum(mlp_bias * mlp_out), mlp_out.shape)]
    )
    net = jnp.concatenate([mlp_in, mlp_bias[None], mlp_out[None]], axis=0)
    router_across = router_weight.T

    send_x, send_dy, aux = send_rows(tokens, cotangent, routes, router_weight, mp_index)
    msg_x = from_members([to_experts(send_x, experts)] * GROUPS)
    own_dy = to_experts(send_dy, experts)
    msg_x, own_dy = together((msg_x, own_dy))
    msg_dy = from_members([own_dy] * GROUPS)

    rows_x, hidden, by_gate, by_up, *parts = expert_forward(
        mp_index, perm, perm_t, msg_x, w_gate, w_up, w_down
    )
    swapped = from_members(parts)

    rows_dy, d_gate, d_up = expert_backward(mp_index, perm, msg_dy, w_down, by_gate, by_up)
    g_down, s_down = grad_down(hidden, rows_dy)
    g_gate, g_up, s_gate, s_up = grad_in(rows_x, d_gate, d_up)
    lane = iota((1, LANES), 1)
    squares = jnp.where(lane == 0, s_gate, jnp.where(lane == 1, s_up, s_down))
    swapped, squares = together((swapped, squares))
    squares = sum(from_members([squares] * GROUPS))
    squares = jnp.sum(to_all_experts(squares, experts), axis=(0, 1))
    total_count = experts * width * w_gate.shape[1] * groups
    inverse = 1.0 / jnp.sqrt(squares / total_count + EPSILON)

    expert_out = sum(p.astype(F32) for p in swapped).astype(BF)
    expert_out, inverse = together((expert_out, inverse))
    back = to_experts(expert_out, experts)
    down_update = learned_step(g_down, w_down, inverse[2:3], spread_down, scalars)
    back, down_update = together((back, down_update))
    mixed, lg = mix(mp_index, aux, tokens, cotangent, back)
    lg, g_gate = together((lg, g_gate))
    lg = lax.all_to_all(lg[:, None], EXPERT, 0, 0, tiled=True)[:, 0]
    gate_update = learned_step(g_gate, w_gate, inverse[0:1], spread_in, scalars)
    lg, gate_update = together((lg, gate_update))
    column = router_column(lg, rows_x)
    column, g_up = together((column, g_up))
    columns = from_members([column] * GROUPS)
    up_update = learned_step(g_up, w_up, inverse[1:2], spread_in, scalars, 0)
    columns, up_update = together((columns, up_update))
    columns = to_all_experts(sum(columns), experts)
    up_update = learned_step(g_up, w_up, inverse[1:2], spread_in, scalars, 1, up_update)
    router_update = router_step(net, columns, router_across)
    return (mixed, gate_update[None], up_update[None], down_update[None], router_update)


def solution(mesh):
    torus = Mesh(
        mesh.devices.reshape(8, 4, 2, mesh.shape["mp"]), ("expert_0", "expert_1", "expert_2", "mp")
    )
    placed = (
        P(EXPERT, None),
        P(EXPERT, None),
        P(EXPERT, None),
        P(),
        P(EXPERT, None, "mp"),
        P(EXPERT, None, "mp"),
        P(EXPERT, "mp", None),
        P(),
        P(),
        P(),
    )
    return jax.shard_map(
        on_device,
        mesh=torus,
        in_specs=placed,
        out_specs=(
            P(EXPERT, "mp"),
            P(EXPERT, None, "mp"),
            P(EXPERT, None, "mp"),
            P(EXPERT, "mp", None),
            P(),
        ),
        check_vma=False,
    )
```

```python
import functools

import jax
import jax.numpy as jnp
from jax import lax
from jax.experimental import pallas as pl
from jax.experimental.pallas import tpu as pltpu
from jax.sharding import Mesh
from jax.sharding import PartitionSpec as P

D = 1024
FF = 3584
UNITS = 16
EXPERT = ("expert_0", "expert_1", "expert_2")
EPSILON = 1e-06

CAP = 12
GROUP = 16
GROUPS = 4
BLOCK = GROUP * CAP
LANES = 128
BF = jnp.bfloat16
F32 = jnp.float32
HIGHEST = lax.Precision.HIGHEST


def params(**kw):
    return pltpu.CompilerParams(vmem_limit_bytes=48 << 20, **kw)


def in_hbm(x):
    return pltpu.with_memory_space_constraint(x, pltpu.HBM)


def iota(shape, dim):
    return lax.broadcasted_iota(jnp.int32, shape, dim)


def dot(a, b, dims=((1,), (0,)), **kw):
    return lax.dot_general(a, b, (dims, ((), ())), preferred_element_type=F32, **kw)


def row_sum(x):
    return jnp.sum(x, axis=1, keepdims=True)


DATA = 2 * CAP
SIDE = 8


def routing(routes, experts):
    across = routes[...].astype(F32).T
    n = across.shape[0]
    ids = [across[:, k : k + 1].astype(jnp.int32) for k in range(2)]
    hits = [(ids[k] == iota((n, experts), 1)).astype(F32) for k in range(2)]
    earlier = (iota((n, n), 0) > iota((n, n), 1)).astype(F32).astype(BF)
    before = dot(earlier, (hits[0] + hits[1]).astype(BF))
    places = [row_sum(before * hits[k]).astype(jnp.int32) for k in range(2)]
    return ids, places, hits


def one_hot(index, size):
    return (index == iota((index.shape[0], size), 1)).astype(F32).astype(BF)


def send_x_kernel(mp, tok_cols, routes, x_out, *, experts):
    del mp
    ids, places, _ = routing(routes, experts)
    rows = x_out.shape[0]
    total = jnp.zeros((rows, LANES), F32)
    for h in range(2):
        picks = [one_hot(ids[k] * DATA + places[k] + h * CAP, rows) for k in range(2)]
        total = total + dot(
            picks[0] + picks[1], tok_cols[:, h * LANES : (h + 1) * LANES], ((0,), (0,))
        )
    x_out[...] = total.astype(BF)


def send_dy_kernel(mp, tok, cot_cols, routes, router, dy_out, aux_out):
    del mp
    n = tok.shape[0]
    experts = router.shape[0]
    rows = dy_out.shape[0]
    size = DATA + SIDE
    ids, places, hits = routing(routes, experts)
    logits = dot(tok[...], router[...], ((1,), (1,)))
    sig = [1.0 / (1.0 + jnp.exp(-row_sum(logits * hits[k]))) for k in range(2)]
    denominator = sig[0] + sig[1]
    gates = [s / denominator for s in sig]
    cot = cot_cols[...].astype(F32)
    total = jnp.zeros((rows, LANES), F32)
    sides = [jnp.zeros((experts, LANES), F32) for _ in range(5)]
    for k in range(2):
        scaled = (gates[k] * cot).astype(BF)
        for h in range(2):
            pick = one_hot(ids[k] * size + places[k] + h * CAP, rows)
            total = total + dot(pick, scaled[:, h * LANES : (h + 1) * LANES], ((0,), (0,)))
        own = gates[1 - k] * (1.0 - sig[k])
        other = -gates[1 - k] * (1.0 - sig[1 - k])
        values = two_parts(own) + two_parts(other) + (ids[1 - k],)
        slot = one_hot(places[k], LANES).astype(F32)
        for i, value in enumerate(values):
            placed = (slot * value.astype(F32)).astype(BF)
            sides[i] = sides[i] + dot(hits[k].astype(BF), placed, ((0,), (0,)))
    expert = iota((experts, rows), 0) * size + DATA
    for i in range(5):
        row = (expert + i == iota((experts, rows), 1)).astype(F32).astype(BF)
        total = total + dot(row, sides[i].astype(BF), ((0,), (0,)))
    dy_out[...] = total.astype(BF)
    lane = iota((n, LANES), 1)
    aux = jnp.zeros((n, LANES), F32)
    for i, column in enumerate(gates + [i.astype(F32) for i in ids + places]):
        aux = jnp.where(lane == i, column, aux)
    aux_out[...] = aux


def send_x(tokens, routes, experts, index):
    n, _ = tokens.shape
    rows = experts * DATA
    return pl.pallas_call(
        functools.partial(send_x_kernel, experts=experts),
        grid_spec=pltpu.PrefetchScalarGridSpec(
            num_scalar_prefetch=1,
            grid=(1,),
            in_specs=[
                pl.BlockSpec((n, 2 * LANES), lambda i, at: (0, at[0])),
                pl.BlockSpec((2, n), lambda i, at: (0, 0)),
            ],
            out_specs=pl.BlockSpec((rows, LANES), lambda i, at: (0, 0)),
        ),
        out_shape=jax.ShapeDtypeStruct((rows, LANES), BF),
        compiler_params=params(),
        name="send_x",
    )(index, tokens, routes)


def send_dy(tokens, cotangent, routes, router, index):
    n, width = tokens.shape
    experts = router.shape[0]
    rows = experts * (DATA + SIDE)
    whole = lambda *shape: pl.BlockSpec(shape, lambda i, at: (0,) * len(shape))
    return pl.pallas_call(
        send_dy_kernel,
        grid_spec=pltpu.PrefetchScalarGridSpec(
            num_scalar_prefetch=1,
            grid=(1,),
            in_specs=[
                whole(n, width),
                pl.BlockSpec((n, 2 * LANES), lambda i, at: (0, at[0])),
                whole(2, n),
                whole(experts, width),
            ],
            out_specs=[whole(rows, LANES), whole(n, LANES)],
        ),
        out_shape=[
            jax.ShapeDtypeStruct((rows, LANES), BF),
            jax.ShapeDtypeStruct((n, LANES), F32),
        ],
        compiler_params=params(),
        name="send_dy",
    )(index, tokens, cotangent, routes, router)


def column_of(mp, k, h):
    member = lax.rem(mp + k + GROUPS, GROUPS)
    return pl.multiple_of((2 * member + h) * LANES, LANES)


def unpack_rows(perm, mp, messages, to, blocks):
    for b in range(blocks):
        at = slice(b * 2 * BLOCK, (b + 1) * 2 * BLOCK)
        both = dot(perm, jnp.concatenate([m[at, :] for m in messages], axis=1)).astype(BF)
        for h in range(2):
            for k in range(GROUPS):
                to[b * BLOCK : (b + 1) * BLOCK, pl.ds(column_of(mp, -k, h), LANES)] = both[
                    h * BLOCK : (h + 1) * BLOCK, k * LANES : (k + 1) * LANES
                ]


def forward_kernel(mp, perm, perm_t, m0, m1, m2, m3, gate, up, down, *refs):
    rows_x, hidden, by_gate, by_up = refs[:4]
    parts = refs[4 : 4 + GROUPS]
    outs = refs[4 + GROUPS]
    step = pl.program_id(0)
    blocks = rows_x.shape[0] // BLOCK

    @pl.when(step == 0)
    def _():
        unpack_rows(perm[...], mp[0], (m0, m1, m2, m3), rows_x, blocks)

    acts = dot(rows_x[...], jnp.concatenate([gate[...], up[...]], axis=1))
    act_gate = acts[:, :LANES]
    act_up = acts[:, LANES:]
    s = 1.0 / (1.0 + jnp.exp(-act_gate))
    silu = act_gate * s
    hidden[:, pl.ds(pl.multiple_of(step * LANES, LANES), LANES)] = (silu * act_up).astype(BF)
    by_gate[...] = act_up * s * (1.0 + act_gate * (1.0 - s))
    by_up[...] = silu

    @pl.when(step == pl.num_programs(0) - 1)
    def _():
        outs[...] = dot(hidden[...], down[...]).astype(BF)
        for b in range(blocks):
            halves = [
                jnp.concatenate(
                    [
                        outs[b * BLOCK : (b + 1) * BLOCK, pl.ds(column_of(mp[0], k, h), LANES)]
                        for k in range(GROUPS)
                    ],
                    axis=1,
                )
                for h in range(2)
            ]
            packed = dot(perm_t[...], jnp.concatenate(halves, axis=0)).astype(BF)
            for k in range(GROUPS):
                parts[k][b * 2 * BLOCK : (b + 1) * 2 * BLOCK, :] = packed[
                    :, k * LANES : (k + 1) * LANES
                ]


def expert_forward(mp_index, perm, perm_t, messages, w_gate, w_up, w_down):
    sent, _ = messages[0].shape
    rows = sent // 2
    width, ff = w_gate.shape
    whole = lambda *shape: pl.BlockSpec(shape, lambda i, mp: (0,) * len(shape))
    column = lambda n: pl.BlockSpec((n, LANES), lambda i, mp: (0, i))
    return pl.pallas_call(
        forward_kernel,
        grid_spec=pltpu.PrefetchScalarGridSpec(
            num_scalar_prefetch=1,
            grid=(ff // LANES,),
            in_specs=[whole(*perm.shape), whole(*perm.shape)]
            + [whole(sent, LANES)] * GROUPS
            + [column(width), column(width), whole(ff, width)],
            out_specs=[whole(rows, width), whole(rows, ff), column(rows), column(rows)]
            + [whole(sent, LANES)] * GROUPS,
            scratch_shapes=[pltpu.VMEM((rows, width), BF)],
        ),
        out_shape=[
            jax.ShapeDtypeStruct((rows, width), BF),
            jax.ShapeDtypeStruct((rows, ff), BF),
            jax.ShapeDtypeStruct((rows, ff), F32),
            jax.ShapeDtypeStruct((rows, ff), F32),
        ]
        + [jax.ShapeDtypeStruct((sent, LANES), BF)] * GROUPS,
        compiler_params=params(),
        name="expert_forward",
    )(mp_index, perm, perm_t, *messages, w_gate, w_up, w_down)


def backward_kernel(
    at, perm, m0, m1, m2, m3, side, down, hidden, by_gate, by_up, rows_x,
    rows_dy, d_gate, d_up, router, total,
):
    part = rows_dy.shape[0]
    experts = router.shape[0]
    unpack_rows(perm[...], at[0], (m0, m1, m2, m3), rows_dy, part // BLOCK)
    grad_hidden = dot(rows_dy[...], down[...], ((1,), (1,)))
    d_gate[...] = (grad_hidden * by_gate[...]).astype(BF)
    d_up[...] = (grad_hidden * by_up[...]).astype(BF)
    q = row_sum(hidden[...].astype(F32) * grad_hidden)
    row = iota((part, part // CAP), 0)
    first = iota((part, part // CAP), 1) * CAP
    source = ((row >= first) & (row < first + CAP)).astype(F32)
    place = (iota((part, 1), 0).astype(F32) - row_sum(source * first.astype(F32))).astype(jnp.int32)
    slot = (place == iota((part, LANES), 1)).astype(F32)
    spread = dot(source.astype(BF), jnp.concatenate([side[i] for i in range(5)], axis=1))
    values = [row_sum(spread[:, i * LANES : (i + 1) * LANES] * slot) for i in range(5)]
    own = q * (values[0] + values[1])
    other = q * (values[2] + values[3])
    lane = iota((part, experts), 1)
    grads = jnp.where(lane == at[1], own, 0.0)
    grads = jnp.where(lane == values[4].astype(jnp.int32), other, grads)
    both = dot(jnp.concatenate(two_parts(grads), axis=1), rows_x[...], ((0,), (0,)))
    grad = both[:experts] + both[experts:]

    @pl.when(pl.program_id(0) == 0)
    def _():
        total[...] = grad

    @pl.when(pl.program_id(0) == pl.num_programs(0) - 1)
    def _():
        whole = total[...] + grad
        for j in range(router.shape[1]):
            router[:, j, :] = whole[:, j * LANES : (j + 1) * LANES]


def expert_backward(index, perm, messages, side, w_down, hidden, by_gate, by_up, rows_x):
    sent, _ = messages[0].shape
    steps = 2
    rows = sent // 2
    part = rows // steps
    experts = rows // CAP
    ff, width = w_down.shape
    whole = lambda *shape: pl.BlockSpec(shape, lambda i, at: (0,) * len(shape))
    row = lambda n, m: pl.BlockSpec((n, m), lambda i, at: (i, 0))
    return pl.pallas_call(
        backward_kernel,
        grid_spec=pltpu.PrefetchScalarGridSpec(
            num_scalar_prefetch=1,
            grid=(steps,),
            in_specs=[whole(*perm.shape)]
            + [row(sent // steps, LANES)] * GROUPS
            + [pl.BlockSpec((SIDE, part // CAP, LANES), lambda i, at: (0, i, 0))]
            + [whole(ff, width), row(part, ff), row(part, ff), row(part, ff), row(part, width)],
            out_specs=[
                row(part, width),
                row(part, ff),
                row(part, ff),
                whole(experts, width // LANES, LANES),
            ],
            scratch_shapes=[pltpu.VMEM((experts, width), F32)],
        ),
        out_shape=[
            jax.ShapeDtypeStruct((rows, width), BF),
            jax.ShapeDtypeStruct((rows, ff), BF),
            jax.ShapeDtypeStruct((rows, ff), BF),
            jax.ShapeDtypeStruct((experts, width // LANES, LANES), F32),
        ],
        compiler_params=params(),
        name="expert_backward",
    )(index, perm, *messages, side, w_down, hidden, by_gate, by_up, rows_x)


def add_squares(total, grad, to):
    step = pl.program_id(0)
    squares = jnp.sum(grad * grad, axis=0, keepdims=True)

    @pl.when(step == 0)
    def _():
        total[...] = squares

    @pl.when(step > 0)
    def _():
        total[...] += squares

    @pl.when(step == pl.num_programs(0) - 1)
    def _():
        to[...] = jnp.broadcast_to(row_sum(total[...]), to.shape)


def grad_in_kernel(rows_x, d_gate, d_up, g_gate, g_up, s_gate, s_up, t_gate, t_up):
    across = rows_x[...].T
    for d, g, s, t in ((d_gate, g_gate, s_gate, t_gate), (d_up, g_up, s_up, t_up)):
        grad = dot(across, d[...])
        g[...] = grad
        add_squares(t, grad, s)


def grad_in(rows_x, d_gate, d_up):
    rows, width = rows_x.shape
    ff = d_gate.shape[1]
    chunk = 256
    whole = lambda *shape: pl.BlockSpec(shape, lambda i: (0,) * len(shape))
    return pl.pallas_call(
        grad_in_kernel,
        grid=(width // chunk,),
        in_specs=[pl.BlockSpec((rows, chunk), lambda i: (0, i)), whole(rows, ff), whole(rows, ff)],
        out_specs=[pl.BlockSpec((chunk, ff), lambda i: (i, 0))] * 2 + [whole(1, LANES)] * 2,
        out_shape=[jax.ShapeDtypeStruct((width, ff), F32)] * 2
        + [jax.ShapeDtypeStruct((1, LANES), F32)] * 2,
        scratch_shapes=[pltpu.VMEM((1, ff), F32)] * 2,
        compiler_params=params(),
        name="grad_in",
    )(rows_x, d_gate, d_up)


def grad_down_kernel(hidden, rows_dy, g_down, s_down, across, total):
    @pl.when(pl.program_id(0) == 0)
    def _():
        across[...] = hidden[...].T

    grad = dot(across[...], rows_dy[...])
    g_down[...] = grad
    add_squares(total, grad, s_down)


def grad_down(hidden, rows_dy):
    rows, ff = hidden.shape
    width = rows_dy.shape[1]
    chunk = 256
    whole = lambda *shape: pl.BlockSpec(shape, lambda i: (0,) * len(shape))
    return pl.pallas_call(
        grad_down_kernel,
        grid=(width // chunk,),
        in_specs=[whole(rows, ff), pl.BlockSpec((rows, chunk), lambda i: (0, i))],
        out_specs=[pl.BlockSpec((ff, chunk), lambda i: (0, i)), whole(1, LANES)],
        out_shape=[
            jax.ShapeDtypeStruct((ff, width), F32),
            jax.ShapeDtypeStruct((1, LANES), F32),
        ],
        scratch_shapes=[pltpu.VMEM((ff, rows), BF), pltpu.VMEM((1, chunk), F32)],
        compiler_params=params(),
        name="grad_down",
    )(hidden, rows_dy)


NET_ROWS = 32


def two_parts(x):
    high = x.astype(BF)
    return high, (x - high.astype(F32)).astype(BF)


def spread_kernel(coef, to):
    k = UNITS * NET_ROWS
    c = 8 * NET_ROWS
    same = iota((k, c), 0) % NET_ROWS == iota((k, c), 1) % NET_ROWS
    feature = iota((k, c), 1) // NET_ROWS
    value = jnp.zeros((k, c), F32)
    for part in range(3):
        a = coef[:, part : part + 1]
        high = a.astype(BF).astype(F32)
        low = a - high
        if part < 2:
            values = (high, low, high)
        else:
            values = (high, low)
        for i, v in enumerate(values):
            value = jnp.where(feature == part * 3 + i, v, value)
    to[...] = jnp.where(same, value, 0.0).astype(BF)


def spread_weights(mlp_in, weight_scale):
    coef = jnp.stack([mlp_in[0], mlp_in[2], mlp_in[1] * weight_scale], axis=1)
    coef = jnp.repeat(coef, NET_ROWS, axis=0)
    return pl.pallas_call(
        spread_kernel,
        out_shape=jax.ShapeDtypeStruct((UNITS * NET_ROWS, 8 * NET_ROWS), BF),
        compiler_params=params(),
        name="spread_weights",
    )(coef)


def step_kernel(scalars, rms, spread, grad, weight, out, *, rows):
    n = NET_ROWS
    height, width = grad.shape
    inverse = rms[0]
    constant = scalars[2, 0]

    def features(r, c, lanes):
        w = weight[pl.ds(r, n), c : c + lanes]
        f0 = grad[pl.ds(r, n), c : c + lanes] * inverse
        h0, l0 = two_parts(f0)
        h2, l2 = two_parts(jnp.tanh(f0))
        return jnp.concatenate([h0, h0, l0, h2, h2, l2, w, w], axis=0)

    def network(feats):
        y = dot(spread[...], feats)
        total = jnp.full((n, feats.shape[1]), constant, F32)
        for j in range(UNITS):
            total = total + scalars[1, j] * jnp.maximum(y[j * n : (j + 1) * n], scalars[0, j])
        return total.astype(BF)

    def body(i, carry):
        r = pl.multiple_of(i * rows, rows)
        for pair in range(0, rows, 2 * n):
            at = [r + pair, r + pair + n]
            whole = width // 256 * 256
            for c in range(0, whole, 256):
                for a in at:
                    out[pl.ds(a, n), c : c + 256] = network(features(a, c, 256))
            if whole < width:
                u = network(jnp.concatenate([features(a, whole, 128) for a in at], axis=1))
                for i, a in enumerate(at):
                    out[pl.ds(a, n), whole:width] = u[:, i * 128 : (i + 1) * 128]
        return carry

    lax.fori_loop(0, height // rows, body, 0)


def learned_step(grad, weight, rms, spread, scalars):
    height, width = grad.shape
    block = 128
    tile = pl.BlockSpec((block, width), lambda i: (i, 0))
    return pl.pallas_call(
        functools.partial(step_kernel, rows=128),
        grid=(height // block,),
        in_specs=[
            pl.BlockSpec(memory_space=pltpu.SMEM),
            pl.BlockSpec(memory_space=pltpu.SMEM),
            pl.BlockSpec(spread.shape, lambda i: (0, 0)),
            tile,
            tile,
        ],
        out_specs=tile,
        out_shape=jax.ShapeDtypeStruct((height, width), BF),
        compiler_params=params(),
        name="learned_step",
    )(scalars, rms, spread, in_hbm(grad), in_hbm(weight))


def mix_kernel(at, aux, tok_cols, back, out, *, size):
    del at
    rows = back.shape[0]
    for h in range(2):
        cols = slice(h * LANES, (h + 1) * LANES)
        total = tok_cols[:, cols].astype(F32)
        for k in range(2):
            base = aux[:, 2 + k : 3 + k] * size + aux[:, 4 + k : 5 + k] + h * CAP
            total = total + aux[:, k : k + 1] * dot(
                one_hot(base.astype(jnp.int32), rows), back[...]
            )
        out[:, cols] = total.astype(BF)


def mix(index, aux, tokens, back, experts):
    n = tokens.shape[0]
    cols = 2 * LANES
    whole = lambda *shape: pl.BlockSpec(shape, lambda i, at: (0,) * len(shape))
    mine = pl.BlockSpec((n, cols), lambda i, at: (0, at[0]))
    return pl.pallas_call(
        functools.partial(mix_kernel, size=back.shape[0] // experts),
        grid_spec=pltpu.PrefetchScalarGridSpec(
            num_scalar_prefetch=1,
            grid=(1,),
            in_specs=[whole(n, LANES), mine, whole(*back.shape)],
            out_specs=whole(n, cols),
        ),
        out_shape=jax.ShapeDtypeStruct((n, cols), BF),
        compiler_params=params(),
        name="mix",
    )(index, aux, tokens, back)


def router_step_kernel(net, columns, weight, out):
    experts, width = weight.shape
    grad = jnp.concatenate([columns[:, j, :] for j in range(width // LANES)], axis=1)
    mean = jnp.sum(row_sum(grad * grad), axis=0, keepdims=True) * (1.0 / grad.size)
    f0 = grad / jnp.sqrt(mean + EPSILON)
    f1 = weight[...].astype(F32) * D**0.5
    f2 = jnp.tanh(f0)
    total = jnp.zeros_like(f0)
    for j in range(UNITS):
        total = total + net[4, j] * jnp.maximum(
            net[0, j] * f0 + net[1, j] * f1 + net[2, j] * f2 + net[3, j], 0.0
        )
    out[...] = total.astype(BF)


def router_step(net, parts, weight):
    return pl.pallas_call(
        router_step_kernel,
        in_specs=[
            pl.BlockSpec(memory_space=pltpu.SMEM),
            pl.BlockSpec(memory_space=pltpu.VMEM),
            pl.BlockSpec(memory_space=pltpu.VMEM),
        ],
        out_shape=jax.ShapeDtypeStruct(weight.shape, BF),
        compiler_params=params(),
        name="router_step",
    )(net, parts, weight)


def to_experts(x, peers):
    sent = x.reshape(peers, -1, x.shape[-1])
    return lax.all_to_all(sent, EXPERT, 0, 0, tiled=True)


def from_members(pieces):
    return [pieces[0]] + [
        lax.ppermute(pieces[k], "mp", [(i, (i + k) % GROUPS) for i in range(GROUPS)])
        for k in range(1, GROUPS)
    ]


def together(values):
    return lax.optimization_barrier(values)


def to_all_experts(x, peers):
    return lax.all_to_all(jnp.broadcast_to(x[None], (peers, *x.shape)), EXPERT, 0, 0, tiled=True)


def on_device(
    tokens,
    cotangent,
    routes,
    router_weight,
    gate_weight,
    up_weight,
    down_weight,
    mlp_in,
    mlp_bias,
    mlp_out,
):
    experts = lax.axis_size(EXPERT)
    groups = lax.axis_size("mp")
    width = tokens.shape[1]
    index = jnp.stack([lax.axis_index("mp"), lax.axis_index(EXPERT)]).astype(jnp.int32)
    w_gate = gate_weight[0]
    w_up = up_weight[0]
    w_down = down_weight[0]

    pos = jnp.arange(2 * BLOCK, dtype=jnp.int32)
    inner = pos % BLOCK
    source_row = inner + inner // CAP * CAP + pos // BLOCK * CAP
    perm = (source_row[:, None] == pos[None, :]).astype(BF)
    perm_t = (source_row[None, :] == pos[:, None]).astype(BF)
    spread_in = spread_weights(mlp_in, D**0.5)
    spread_down = spread_weights(mlp_in, FF**0.5)
    scalars = jnp.stack(
        [-mlp_bias, mlp_out, jnp.broadcast_to(jnp.sum(mlp_bias * mlp_out), mlp_out.shape)]
    )
    net = jnp.concatenate([mlp_in, mlp_bias[None], mlp_out[None]], axis=0)
    router_across = router_weight.T

    routes_across = routes.T
    sent_x = send_x(tokens, routes_across, experts, index)
    own_x = to_experts(sent_x, experts).reshape(-1, LANES)
    sent_dy, aux = send_dy(tokens, cotangent, routes_across, router_across, index)
    msg_x = from_members([own_x] * GROUPS)
    own_dy = to_experts(sent_dy, experts)
    side = own_dy[:, DATA:].transpose(1, 0, 2)
    own_dy = own_dy[:, :DATA].reshape(-1, LANES)
    msg_x, own_dy = together((msg_x, own_dy))
    msg_dy = from_members([own_dy] * GROUPS)

    rows_x, hidden, by_gate, by_up, *parts = expert_forward(
        index, perm, perm_t, msg_x, w_gate, w_up, w_down
    )
    swapped = from_members(parts)

    rows_dy, d_gate, d_up, router_part = expert_backward(
        index, perm, msg_dy, side, w_down, hidden, by_gate, by_up, rows_x
    )
    g_down, s_down = grad_down(hidden, rows_dy)
    g_gate, g_up, s_gate, s_up = grad_in(rows_x, d_gate, d_up)
    lane = iota((SIDE, LANES), 1)
    squares = jnp.where(lane == 0, s_gate, jnp.where(lane == 1, s_up, s_down))
    high = lax.reduce_precision(squares, 8, 7)
    squares = jnp.where(iota((SIDE, LANES), 0) == 0, high, squares - high)
    swapped, squares = together((swapped, squares))
    expert_out = sum(p.astype(F32) for p in swapped).astype(BF).reshape(experts, DATA, LANES)
    squares = jnp.broadcast_to(squares.astype(BF)[None], (experts, SIDE, LANES))
    back = to_experts(
        jnp.concatenate([expert_out, router_part.astype(BF), squares], axis=1), experts
    )
    sums = jnp.sum(back[:, DATA:].astype(F32), axis=0)
    mixed = mix(index, aux, tokens, back.reshape(-1, LANES), experts)
    sums = sum(from_members([sums] * GROUPS))
    total_count = experts * width * w_gate.shape[1] * groups
    inverse = 1.0 / jnp.sqrt((sums[SIDE] + sums[SIDE + 1]) / total_count + EPSILON)
    columns = to_all_experts(sums[:SIDE], experts)

    down_update = learned_step(g_down, w_down, inverse[2:3], spread_down, scalars)
    gate_update = learned_step(g_gate, w_gate, inverse[0:1], spread_in, scalars)
    up_update = learned_step(g_up, w_up, inverse[1:2], spread_in, scalars)
    columns, up_update = together((columns, up_update))
    router_update = router_step(net, columns, router_across).T
    return (mixed, gate_update[None], up_update[None], down_update[None], router_update)


def solution(mesh):
    torus = Mesh(
        mesh.devices.reshape(8, 4, 2, mesh.shape["mp"]), ("expert_0", "expert_1", "expert_2", "mp")
    )
    placed = (
        P(EXPERT, None),
        P(EXPERT, None),
        P(EXPERT, None),
        P(),
        P(EXPERT, None, "mp"),
        P(EXPERT, None, "mp"),
        P(EXPERT, "mp", None),
        P(),
        P(),
        P(),
    )
    return jax.shard_map(
        on_device,
        mesh=torus,
        in_specs=placed,
        out_specs=(
            P(EXPERT, "mp"),
            P(EXPERT, None, "mp"),
            P(EXPERT, None, "mp"),
            P(EXPERT, "mp", None),
            P(),
        ),
        check_vma=False,
    )
```

```python
import functools

import jax
import jax.numpy as jnp
from jax import lax
from jax.experimental import pallas as pl
from jax.experimental.pallas import tpu as pltpu
from jax.sharding import Mesh
from jax.sharding import PartitionSpec as P

D = 1024
FF = 3584
UNITS = 16
EXPERT = ("expert_0", "expert_1", "expert_2")
EPSILON = 1e-06

CAP = 12
GROUP = 16
GROUPS = 4
BLOCK = GROUP * CAP
LANES = 128
BF = jnp.bfloat16
F32 = jnp.float32
HIGHEST = lax.Precision.HIGHEST


def params(**kw):
    return pltpu.CompilerParams(vmem_limit_bytes=48 << 20, **kw)


def in_hbm(x):
    return pltpu.with_memory_space_constraint(x, pltpu.HBM)


def iota(shape, dim):
    return lax.broadcasted_iota(jnp.int32, shape, dim)


def dot(a, b, dims=((1,), (0,)), **kw):
    return lax.dot_general(a, b, (dims, ((), ())), preferred_element_type=F32, **kw)


def row_sum(x):
    return jnp.sum(x, axis=1, keepdims=True)


DATA = 2 * CAP
SIDE = 8


def routing(routes, experts):
    across = routes[...].astype(F32).T
    n = across.shape[0]
    ids = [across[:, k : k + 1].astype(jnp.int32) for k in range(2)]
    hits = [(ids[k] == iota((n, experts), 1)).astype(F32) for k in range(2)]
    earlier = (iota((n, n), 0) > iota((n, n), 1)).astype(F32).astype(BF)
    before = dot(earlier, (hits[0] + hits[1]).astype(BF))
    places = [row_sum(before * hits[k]).astype(jnp.int32) for k in range(2)]
    return ids, places, hits


def one_hot(index, size):
    return (index == iota((index.shape[0], size), 1)).astype(F32).astype(BF)


def send_x_kernel(mp, tok_cols, routes, x_out, *, experts):
    del mp
    ids, places, _ = routing(routes, experts)
    rows = x_out.shape[0]
    total = jnp.zeros((rows, LANES), F32)
    for h in range(2):
        picks = [one_hot(ids[k] * DATA + places[k] + h * CAP, rows) for k in range(2)]
        total = total + dot(
            picks[0] + picks[1], tok_cols[:, h * LANES : (h + 1) * LANES], ((0,), (0,))
        )
    x_out[...] = total.astype(BF)


def send_dy_kernel(mp, tok, cot_cols, routes, router, dy_out, aux_out):
    del mp
    n = tok.shape[0]
    experts = router.shape[0]
    rows = dy_out.shape[0]
    size = DATA + SIDE
    ids, places, hits = routing(routes, experts)
    logits = dot(tok[...], router[...], ((1,), (1,)))
    sig = [1.0 / (1.0 + jnp.exp(-row_sum(logits * hits[k]))) for k in range(2)]
    denominator = sig[0] + sig[1]
    gates = [s / denominator for s in sig]
    cot = cot_cols[...].astype(F32)
    total = jnp.zeros((rows, LANES), F32)
    sides = [jnp.zeros((experts, LANES), F32) for _ in range(5)]
    for k in range(2):
        scaled = (gates[k] * cot).astype(BF)
        for h in range(2):
            pick = one_hot(ids[k] * size + places[k] + h * CAP, rows)
            total = total + dot(pick, scaled[:, h * LANES : (h + 1) * LANES], ((0,), (0,)))
        own = gates[1 - k] * (1.0 - sig[k])
        other = -gates[1 - k] * (1.0 - sig[1 - k])
        values = two_parts(own) + two_parts(other) + (ids[1 - k],)
        slot = one_hot(places[k], LANES).astype(F32)
        for i, value in enumerate(values):
            placed = (slot * value.astype(F32)).astype(BF)
            sides[i] = sides[i] + dot(hits[k].astype(BF), placed, ((0,), (0,)))
    expert = iota((experts, rows), 0) * size + DATA
    for i in range(5):
        row = (expert + i == iota((experts, rows), 1)).astype(F32).astype(BF)
        total = total + dot(row, sides[i].astype(BF), ((0,), (0,)))
    dy_out[...] = total.astype(BF)
    lane = iota((n, LANES), 1)
    aux = jnp.zeros((n, LANES), F32)
    for i, column in enumerate(gates + [i.astype(F32) for i in ids + places]):
        aux = jnp.where(lane == i, column, aux)
    aux_out[...] = aux


def send_x(tokens, routes, experts, index):
    n, _ = tokens.shape
    rows = experts * DATA
    return pl.pallas_call(
        functools.partial(send_x_kernel, experts=experts),
        grid_spec=pltpu.PrefetchScalarGridSpec(
            num_scalar_prefetch=1,
            grid=(1,),
            in_specs=[
                pl.BlockSpec((n, 2 * LANES), lambda i, at: (0, at[0])),
                pl.BlockSpec((2, n), lambda i, at: (0, 0)),
            ],
            out_specs=pl.BlockSpec((rows, LANES), lambda i, at: (0, 0)),
        ),
        out_shape=jax.ShapeDtypeStruct((rows, LANES), BF),
        compiler_params=params(),
        name="send_x",
    )(index, tokens, routes)


def send_dy(tokens, cotangent, routes, router, index):
    n, width = tokens.shape
    experts = router.shape[0]
    rows = experts * (DATA + SIDE)
    whole = lambda *shape: pl.BlockSpec(shape, lambda i, at: (0,) * len(shape))
    return pl.pallas_call(
        send_dy_kernel,
        grid_spec=pltpu.PrefetchScalarGridSpec(
            num_scalar_prefetch=1,
            grid=(1,),
            in_specs=[
                whole(n, width),
                pl.BlockSpec((n, 2 * LANES), lambda i, at: (0, at[0])),
                whole(2, n),
                whole(experts, width),
            ],
            out_specs=[whole(rows, LANES), whole(n, LANES)],
        ),
        out_shape=[
            jax.ShapeDtypeStruct((rows, LANES), BF),
            jax.ShapeDtypeStruct((n, LANES), F32),
        ],
        compiler_params=params(),
        name="send_dy",
    )(index, tokens, cotangent, routes, router)


def column_of(mp, k, h):
    member = lax.rem(mp + k + GROUPS, GROUPS)
    return pl.multiple_of((2 * member + h) * LANES, LANES)


def unpack_rows(perm, mp, messages, to, blocks):
    def body(b, carry):
        at = pl.ds(pl.multiple_of(b * 2 * BLOCK, 2 * BLOCK), 2 * BLOCK)
        rows = pl.ds(pl.multiple_of(b * BLOCK, BLOCK), BLOCK)
        both = dot(perm[...], jnp.concatenate([m[at, :] for m in messages], axis=1)).astype(BF)
        for h in range(2):
            for k in range(GROUPS):
                to[rows, pl.ds(column_of(mp, -k, h), LANES)] = both[
                    h * BLOCK : (h + 1) * BLOCK, k * LANES : (k + 1) * LANES
                ]
        return carry

    lax.fori_loop(0, blocks, body, 0)


def forward_kernel(mp, perm, perm_t, m0, m1, m2, m3, gate, up, down, *refs):
    rows_x, hidden, by_gate, by_up = refs[:4]
    parts = refs[4 : 4 + GROUPS]
    outs = refs[4 + GROUPS]
    step = pl.program_id(0)
    blocks = rows_x.shape[0] // BLOCK

    @pl.when(step == 0)
    def _():
        unpack_rows(perm, mp[0], (m0, m1, m2, m3), rows_x, blocks)

    acts = dot(rows_x[...], jnp.concatenate([gate[...], up[...]], axis=1))
    act_gate = acts[:, :LANES]
    act_up = acts[:, LANES:]
    s = 1.0 / (1.0 + jnp.exp(-act_gate))
    silu = act_gate * s
    hidden[:, pl.ds(pl.multiple_of(step * LANES, LANES), LANES)] = (silu * act_up).astype(BF)
    by_gate[...] = act_up * s * (1.0 + act_gate * (1.0 - s))
    by_up[...] = silu

    @pl.when(step == pl.num_programs(0) - 1)
    def _():
        outs[...] = dot(hidden[...], down[...]).astype(BF)

        def body(b, carry):
            at = pl.ds(pl.multiple_of(b * 2 * BLOCK, 2 * BLOCK), 2 * BLOCK)
            rows = pl.ds(pl.multiple_of(b * BLOCK, BLOCK), BLOCK)
            halves = [
                jnp.concatenate(
                    [outs[rows, pl.ds(column_of(mp[0], k, h), LANES)] for k in range(GROUPS)],
                    axis=1,
                )
                for h in range(2)
            ]
            packed = dot(perm_t[...], jnp.concatenate(halves, axis=0)).astype(BF)
            for k in range(GROUPS):
                parts[k][at, :] = packed[:, k * LANES : (k + 1) * LANES]
            return carry

        lax.fori_loop(0, blocks, body, 0)


def expert_forward(mp_index, perm, perm_t, messages, w_gate, w_up, w_down):
    sent, _ = messages[0].shape
    rows = sent // 2
    width, ff = w_gate.shape
    whole = lambda *shape: pl.BlockSpec(shape, lambda i, mp: (0,) * len(shape))
    column = lambda n: pl.BlockSpec((n, LANES), lambda i, mp: (0, i))
    return pl.pallas_call(
        forward_kernel,
        grid_spec=pltpu.PrefetchScalarGridSpec(
            num_scalar_prefetch=1,
            grid=(ff // LANES,),
            in_specs=[whole(*perm.shape), whole(*perm.shape)]
            + [whole(sent, LANES)] * GROUPS
            + [column(width), column(width), whole(ff, width)],
            out_specs=[whole(rows, width), whole(rows, ff), column(rows), column(rows)]
            + [whole(sent, LANES)] * GROUPS,
            scratch_shapes=[pltpu.VMEM((rows, width), BF)],
        ),
        out_shape=[
            jax.ShapeDtypeStruct((rows, width), BF),
            jax.ShapeDtypeStruct((rows, ff), BF),
            jax.ShapeDtypeStruct((rows, ff), F32),
            jax.ShapeDtypeStruct((rows, ff), F32),
        ]
        + [jax.ShapeDtypeStruct((sent, LANES), BF)] * GROUPS,
        compiler_params=params(),
        name="expert_forward",
    )(mp_index, perm, perm_t, *messages, w_gate, w_up, w_down)


HALVES = 2
CHUNKS = 4


def logit_terms(q, side, expert, experts):
    part = q.shape[0]
    row = iota((part, part // CAP), 0)
    first = iota((part, part // CAP), 1) * CAP
    source = ((row >= first) & (row < first + CAP)).astype(F32)
    place = (iota((part, 1), 0).astype(F32) - row_sum(source * first.astype(F32))).astype(jnp.int32)
    slot = (place == iota((part, LANES), 1)).astype(F32)
    spread = dot(source.astype(BF), jnp.concatenate([side[i] for i in range(5)], axis=1))
    values = [row_sum(spread[:, i * LANES : (i + 1) * LANES] * slot) for i in range(5)]
    own = q * (values[0] + values[1])
    other = q * (values[2] + values[3])
    lane = iota((part, experts), 1)
    grads = jnp.where(lane == expert, own, 0.0)
    return jnp.where(lane == values[4].astype(jnp.int32), other, grads)


def backward_kernel(
    at, perm, m0, m1, m2, m3, side, down, hidden, by_gate, by_up, rows_x,
    g_gate, g_up, g_down, squares, router,
    rows_dy, d_gate, d_up, x_across, hidden_across, router_total, sums,
):
    step = pl.program_id(0)
    part = rows_x.shape[0]
    experts = router.shape[0]

    @pl.when(step < HALVES)
    def _():
        at_rows = pl.ds(pl.multiple_of(step * part, part), part)
        dy = rows_dy.at[at_rows]
        unpack_rows(perm, at[0], (m0, m1, m2, m3), dy, part // BLOCK)
        grad_hidden = dot(dy[...], down[...], ((1,), (1,)))
        d_gate[at_rows, :] = (grad_hidden * by_gate[...]).astype(BF)
        d_up[at_rows, :] = (grad_hidden * by_up[...]).astype(BF)
        x_across[:, at_rows] = rows_x[...].T
        hidden_across[:, at_rows] = hidden[...].T
        q = row_sum(hidden[...].astype(F32) * grad_hidden)
        grads = logit_terms(q, side, at[1], experts)
        both = dot(jnp.concatenate(two_parts(grads), axis=1), rows_x[...], ((0,), (0,)))
        grad = both[:experts] + both[experts:]

        @pl.when(step == 0)
        def _():
            router_total[...] = grad
            sums[...] = jnp.zeros_like(sums)

        @pl.when(step == HALVES - 1)
        def _():
            whole = router_total[...] + grad
            for j in range(router.shape[1]):
                router[:, j, :] = whole[:, j * LANES : (j + 1) * LANES]

    @pl.when(step >= HALVES)
    def _():
        chunk = step - HALVES
        outs = (
            (g_gate, x_across, d_gate),
            (g_up, x_across, d_up),
            (g_down, hidden_across, rows_dy),
        )
        for i, (out, left, right) in enumerate(outs):
            n = out.shape[0]
            grad = dot(left[pl.ds(pl.multiple_of(chunk * n, n), n), :], right[...])
            out[...] = grad
            total = jnp.sum(grad * grad, axis=0, keepdims=True)
            sums[i : i + 1, : grad.shape[1]] += total

    @pl.when(step == pl.num_programs(0) - 1)
    def _():
        lane = iota(squares.shape, 1)
        values = jnp.zeros(squares.shape, F32)
        for i in range(3):
            values = jnp.where(lane == i, row_sum(sums[i : i + 1, :]), values)
        squares[...] = values


def expert_backward(index, perm, messages, side, w_down, hidden, by_gate, by_up, rows_x):
    sent, _ = messages[0].shape
    rows = sent // 2
    part = rows // HALVES
    experts = rows // CAP
    ff, width = w_down.shape
    first = lambda i: jnp.minimum(i, HALVES - 1)
    then = lambda i: jnp.maximum(i - HALVES, 0)
    whole = lambda *shape: pl.BlockSpec(shape, lambda i, at: (0,) * len(shape))
    row = lambda n, m: pl.BlockSpec((n, m), lambda i, at: (first(i), 0))
    out = lambda n, m: pl.BlockSpec((n // CHUNKS, m), lambda i, at: (then(i), 0))
    return pl.pallas_call(
        backward_kernel,
        grid_spec=pltpu.PrefetchScalarGridSpec(
            num_scalar_prefetch=1,
            grid=(HALVES + CHUNKS,),
            in_specs=[whole(*perm.shape)]
            + [row(sent // HALVES, LANES)] * GROUPS
            + [pl.BlockSpec((SIDE, part // CAP, LANES), lambda i, at: (0, first(i), 0))]
            + [whole(ff, width), row(part, ff), row(part, ff), row(part, ff), row(part, width)],
            out_specs=[
                out(width, ff),
                out(width, ff),
                out(ff, width),
                whole(1, LANES),
                whole(experts, width // LANES, LANES),
            ],
            scratch_shapes=[
                pltpu.VMEM((rows, width), BF),
                pltpu.VMEM((rows, ff), BF),
                pltpu.VMEM((rows, ff), BF),
                pltpu.VMEM((width, rows), BF),
                pltpu.VMEM((ff, rows), BF),
                pltpu.VMEM((experts, width), F32),
                pltpu.VMEM((SIDE, width), F32),
            ],
        ),
        out_shape=[
            jax.ShapeDtypeStruct((width, ff), F32),
            jax.ShapeDtypeStruct((width, ff), F32),
            jax.ShapeDtypeStruct((ff, width), F32),
            jax.ShapeDtypeStruct((1, LANES), F32),
            jax.ShapeDtypeStruct((experts, width // LANES, LANES), F32),
        ],
        compiler_params=params(),
        name="expert_backward",
    )(index, perm, *messages, side, w_down, hidden, by_gate, by_up, rows_x)


NET_ROWS = 32


def two_parts(x):
    high = x.astype(BF)
    return high, (x - high.astype(F32)).astype(BF)


def spread_kernel(coef, to):
    k = UNITS * NET_ROWS
    c = 8 * NET_ROWS
    same = iota((k, c), 0) % NET_ROWS == iota((k, c), 1) % NET_ROWS
    feature = iota((k, c), 1) // NET_ROWS
    value = jnp.zeros((k, c), F32)
    for part in range(3):
        a = coef[:, part : part + 1]
        high = a.astype(BF).astype(F32)
        low = a - high
        if part < 2:
            values = (high, low, high)
        else:
            values = (high, low)
        for i, v in enumerate(values):
            value = jnp.where(feature == part * 3 + i, v, value)
    to[...] = jnp.where(same, value, 0.0).astype(BF)


def spread_weights(mlp_in, weight_scale):
    coef = jnp.stack([mlp_in[0], mlp_in[2], mlp_in[1] * weight_scale], axis=1)
    coef = jnp.repeat(coef, NET_ROWS, axis=0)
    return pl.pallas_call(
        spread_kernel,
        out_shape=jax.ShapeDtypeStruct((UNITS * NET_ROWS, 8 * NET_ROWS), BF),
        compiler_params=params(),
        name="spread_weights",
    )(coef)


def step_kernel(scalars, rms, spread, grad, weight, out, *, rows):
    n = NET_ROWS
    height, width = grad.shape
    inverse = rms[0]
    constant = scalars[2, 0]

    def features(r, c, lanes):
        w = weight[pl.ds(r, n), c : c + lanes]
        f0 = grad[pl.ds(r, n), c : c + lanes] * inverse
        h0, l0 = two_parts(f0)
        h2, l2 = two_parts(jnp.tanh(f0))
        return jnp.concatenate([h0, h0, l0, h2, h2, l2, w, w], axis=0)

    def network(feats):
        y = dot(spread[...], feats)
        total = jnp.full((n, feats.shape[1]), constant, F32)
        for j in range(UNITS):
            total = total + scalars[1, j] * jnp.maximum(y[j * n : (j + 1) * n], scalars[0, j])
        return total.astype(BF)

    def body(i, carry):
        r = pl.multiple_of(i * rows, rows)
        for pair in range(0, rows, 2 * n):
            at = [r + pair, r + pair + n]
            whole = width // 256 * 256
            for c in range(0, whole, 256):
                for a in at:
                    out[pl.ds(a, n), c : c + 256] = network(features(a, c, 256))
            if whole < width:
                u = network(jnp.concatenate([features(a, whole, 128) for a in at], axis=1))
                for i, a in enumerate(at):
                    out[pl.ds(a, n), whole:width] = u[:, i * 128 : (i + 1) * 128]
        return carry

    lax.fori_loop(0, height // rows, body, 0)


def learned_step(grad, weight, rms, spread, scalars):
    height, width = grad.shape
    block = 128
    tile = pl.BlockSpec((block, width), lambda i: (i, 0))
    return pl.pallas_call(
        functools.partial(step_kernel, rows=128 if width % 256 == 0 else 64),
        grid=(height // block,),
        in_specs=[
            pl.BlockSpec(memory_space=pltpu.SMEM),
            pl.BlockSpec(memory_space=pltpu.SMEM),
            pl.BlockSpec(spread.shape, lambda i: (0, 0)),
            tile,
            tile,
        ],
        out_specs=tile,
        out_shape=jax.ShapeDtypeStruct((height, width), BF),
        compiler_params=params(),
        name="learned_step",
    )(scalars, rms, spread, in_hbm(grad), in_hbm(weight))


def mix_kernel(at, aux, tok_cols, back, out, *, size):
    del at
    rows = back.shape[0]
    for h in range(2):
        cols = slice(h * LANES, (h + 1) * LANES)
        total = tok_cols[:, cols].astype(F32)
        for k in range(2):
            base = aux[:, 2 + k : 3 + k] * size + aux[:, 4 + k : 5 + k] + h * CAP
            total = total + aux[:, k : k + 1] * dot(
                one_hot(base.astype(jnp.int32), rows), back[...]
            )
        out[:, cols] = total.astype(BF)


def mix(index, aux, tokens, back, experts):
    n = tokens.shape[0]
    cols = 2 * LANES
    whole = lambda *shape: pl.BlockSpec(shape, lambda i, at: (0,) * len(shape))
    mine = pl.BlockSpec((n, cols), lambda i, at: (0, at[0]))
    return pl.pallas_call(
        functools.partial(mix_kernel, size=back.shape[0] // experts),
        grid_spec=pltpu.PrefetchScalarGridSpec(
            num_scalar_prefetch=1,
            grid=(1,),
            in_specs=[whole(n, LANES), mine, whole(*back.shape)],
            out_specs=whole(n, cols),
        ),
        out_shape=jax.ShapeDtypeStruct((n, cols), BF),
        compiler_params=params(),
        name="mix",
    )(index, aux, tokens, back)


def router_step_kernel(net, columns, weight, out):
    experts, width = weight.shape
    grad = jnp.concatenate([columns[:, j, :] for j in range(width // LANES)], axis=1)
    mean = jnp.sum(row_sum(grad * grad), axis=0, keepdims=True) * (1.0 / grad.size)
    f0 = grad / jnp.sqrt(mean + EPSILON)
    f1 = weight[...].astype(F32) * D**0.5
    f2 = jnp.tanh(f0)
    total = jnp.zeros_like(f0)
    for j in range(UNITS):
        total = total + net[4, j] * jnp.maximum(
            net[0, j] * f0 + net[1, j] * f1 + net[2, j] * f2 + net[3, j], 0.0
        )
    out[...] = total.astype(BF)


def router_step(net, parts, weight):
    return pl.pallas_call(
        router_step_kernel,
        in_specs=[
            pl.BlockSpec(memory_space=pltpu.SMEM),
            pl.BlockSpec(memory_space=pltpu.VMEM),
            pl.BlockSpec(memory_space=pltpu.VMEM),
        ],
        out_shape=jax.ShapeDtypeStruct(weight.shape, BF),
        compiler_params=params(),
        name="router_step",
    )(net, parts, weight)


def to_experts(x, peers):
    sent = x.reshape(peers, -1, x.shape[-1])
    return lax.all_to_all(sent, EXPERT, 0, 0, tiled=True)


def from_members(pieces):
    return [pieces[0]] + [
        lax.ppermute(pieces[k], "mp", [(i, (i + k) % GROUPS) for i in range(GROUPS)])
        for k in range(1, GROUPS)
    ]


def together(values):
    return lax.optimization_barrier(values)


def to_all_experts(x, peers):
    return lax.all_to_all(jnp.broadcast_to(x[None], (peers, *x.shape)), EXPERT, 0, 0, tiled=True)


def on_device(
    tokens,
    cotangent,
    routes,
    router_weight,
    gate_weight,
    up_weight,
    down_weight,
    mlp_in,
    mlp_bias,
    mlp_out,
):
    experts = lax.axis_size(EXPERT)
    groups = lax.axis_size("mp")
    width = tokens.shape[1]
    index = jnp.stack([lax.axis_index("mp"), lax.axis_index(EXPERT)]).astype(jnp.int32)
    w_gate = gate_weight[0]
    w_up = up_weight[0]
    w_down = down_weight[0]

    pos = jnp.arange(2 * BLOCK, dtype=jnp.int32)
    inner = pos % BLOCK
    source_row = inner + inner // CAP * CAP + pos // BLOCK * CAP
    perm = (source_row[:, None] == pos[None, :]).astype(BF)
    perm_t = (source_row[None, :] == pos[:, None]).astype(BF)
    spread_in = spread_weights(mlp_in, D**0.5)
    spread_down = spread_weights(mlp_in, FF**0.5)
    scalars = jnp.stack(
        [-mlp_bias, mlp_out, jnp.broadcast_to(jnp.sum(mlp_bias * mlp_out), mlp_out.shape)]
    )
    net = jnp.concatenate([mlp_in, mlp_bias[None], mlp_out[None]], axis=0)
    router_across = router_weight.T

    routes_across = routes.T
    sent_x = send_x(in_hbm(tokens), routes_across, experts, index)
    own_x = to_experts(sent_x, experts).reshape(-1, LANES)
    sent_dy, aux = send_dy(in_hbm(tokens), in_hbm(cotangent), routes_across, router_across, index)
    sent_dy, perm, perm_t, spread_in, spread_down, scalars, net = together(
        (sent_dy, perm, perm_t, spread_in, spread_down, scalars, net)
    )
    msg_x = from_members([own_x] * GROUPS)
    own_dy = to_experts(sent_dy, experts)
    side = own_dy[:, DATA:].transpose(1, 0, 2)
    own_dy = own_dy[:, :DATA].reshape(-1, LANES)
    perm, own_dy = together((perm, own_dy))
    msg_dy = from_members([own_dy] * GROUPS)

    rows_x, hidden, by_gate, by_up, *parts = expert_forward(
        index, perm, perm_t, msg_x, w_gate, w_up, w_down
    )
    swapped = from_members(parts)

    g_gate, g_up, g_down, squares, router_part = expert_backward(
        index, perm, msg_dy, side, w_down, hidden, by_gate, by_up, rows_x
    )
    swapped, squares = together((swapped, squares))
    squares = sum(from_members([squares] * GROUPS))
    expert_out = sum(p.astype(F32) for p in swapped).astype(BF).reshape(experts, DATA, LANES)
    message = jnp.concatenate([expert_out, router_part.astype(BF)], axis=1)
    message, squares = together((message, squares))
    squares = jnp.sum(to_all_experts(squares, experts), axis=0)
    total_count = experts * width * w_gate.shape[1] * groups
    inverse = 1.0 / jnp.sqrt(squares[0] / total_count + EPSILON)

    message, inverse = together((message, inverse))
    back = to_experts(message, experts)
    down_update = learned_step(g_down, w_down, inverse[2:3], spread_down, scalars)
    gate_update = learned_step(g_gate, w_gate, inverse[0:1], spread_in, scalars)
    back, gate_update, down_update = together((back, gate_update, down_update))
    sums = jnp.sum(back[:, DATA:].astype(F32), axis=0)
    sums = from_members([sums] * GROUPS)
    mixed = mix(index, aux, tokens, back.reshape(-1, LANES), experts)
    mixed, sums = together((mixed, sums))
    sums = sum(sums)
    sums, g_up = together((sums, g_up))
    columns = to_all_experts(sums, experts)
    up_update = learned_step(g_up, w_up, inverse[1:2], spread_in, scalars)
    columns, up_update = together((columns, up_update))
    router_update = router_step(net, columns, router_across).T
    return (mixed, gate_update[None], up_update[None], down_update[None], router_update)


def solution(mesh):
    torus = Mesh(
        mesh.devices.reshape(8, 4, 2, mesh.shape["mp"]), ("expert_0", "expert_1", "expert_2", "mp")
    )
    placed = (
        P(EXPERT, None),
        P(EXPERT, None),
        P(EXPERT, None),
        P(),
        P(EXPERT, None, "mp"),
        P(EXPERT, None, "mp"),
        P(EXPERT, "mp", None),
        P(),
        P(),
        P(),
    )
    return jax.shard_map(
        on_device,
        mesh=torus,
        in_specs=placed,
        out_specs=(
            P(EXPERT, "mp"),
            P(EXPERT, None, "mp"),
            P(EXPERT, None, "mp"),
            P(EXPERT, "mp", None),
            P(),
        ),
        check_vma=False,
    )
```

```python
import functools

import jax
import jax.numpy as jnp
from jax import lax
from jax.experimental import pallas as pl
from jax.experimental.pallas import tpu as pltpu
from jax.sharding import Mesh
from jax.sharding import PartitionSpec as P

D = 1024
FF = 3584
UNITS = 16
EXPERT = ("expert_0", "expert_1", "expert_2")
EPSILON = 1e-06

CAP = 12
GROUP = 16
GROUPS = 4
BLOCK = GROUP * CAP
LANES = 128
BF = jnp.bfloat16
F32 = jnp.float32
HIGHEST = lax.Precision.HIGHEST


def params(**kw):
    return pltpu.CompilerParams(vmem_limit_bytes=48 << 20, **kw)


def in_hbm(x):
    return pltpu.with_memory_space_constraint(x, pltpu.HBM)


def iota(shape, dim):
    return lax.broadcasted_iota(jnp.int32, shape, dim)


def dot(a, b, dims=((1,), (0,)), **kw):
    return lax.dot_general(a, b, (dims, ((), ())), preferred_element_type=F32, **kw)


def row_sum(x):
    return jnp.sum(x, axis=1, keepdims=True)


DATA = 2 * CAP
SIDE = 8


def routing(routes, experts):
    across = routes[...].astype(F32).T
    n = across.shape[0]
    ids = [across[:, k : k + 1].astype(jnp.int32) for k in range(2)]
    hits = [(ids[k] == iota((n, experts), 1)).astype(F32) for k in range(2)]
    earlier = (iota((n, n), 0) > iota((n, n), 1)).astype(F32).astype(BF)
    before = dot(earlier, (hits[0] + hits[1]).astype(BF))
    places = [row_sum(before * hits[k]).astype(jnp.int32) for k in range(2)]
    return ids, places, hits


def one_hot(index, size):
    return (index == iota((index.shape[0], size), 1)).astype(F32).astype(BF)


def send_x_kernel(at, tok_cols, routes, x_out, *, experts):
    del at
    n = tok_cols.shape[0]
    rows = x_out.shape[0]
    ids = [routes[k : k + 1, :] for k in range(2)]
    hits = [(ids[k] == iota((experts, n), 0)).astype(F32) for k in range(2)]
    earlier = (iota((n, n), 0) < iota((n, n), 1)).astype(F32).astype(BF)
    before = dot((hits[0] + hits[1]).astype(BF), earlier)
    base = [
        ids[k] * DATA + jnp.sum(before * hits[k], axis=0, keepdims=True).astype(jnp.int32)
        for k in range(2)
    ]
    row = iota((rows, n), 0)
    total = jnp.zeros((rows, LANES), F32)
    for h in range(2):
        picked = (base[0] + h * CAP == row) | (base[1] + h * CAP == row)
        total = total + dot(
            picked.astype(F32).astype(BF), tok_cols[:, h * LANES : (h + 1) * LANES]
        )
    x_out[...] = total.astype(BF)


def send_dy_kernel(mp, tok, cot_cols, routes, router, dy_out, aux_out):
    del mp
    n = tok.shape[0]
    experts = router.shape[0]
    rows = dy_out.shape[0]
    size = DATA + SIDE
    ids, places, hits = routing(routes, experts)
    logits = dot(tok[...], router[...], ((1,), (1,)))
    sig = [1.0 / (1.0 + jnp.exp(-row_sum(logits * hits[k]))) for k in range(2)]
    denominator = sig[0] + sig[1]
    gates = [s / denominator for s in sig]
    cot = cot_cols[...].astype(F32)
    total = jnp.zeros((rows, LANES), F32)
    sides = [jnp.zeros((experts, LANES), F32) for _ in range(5)]
    for k in range(2):
        scaled = (gates[k] * cot).astype(BF)
        for h in range(2):
            pick = one_hot(ids[k] * size + places[k] + h * CAP, rows)
            total = total + dot(pick, scaled[:, h * LANES : (h + 1) * LANES], ((0,), (0,)))
        own = gates[1 - k] * (1.0 - sig[k])
        other = -gates[1 - k] * (1.0 - sig[1 - k])
        values = two_parts(own) + two_parts(other) + (ids[1 - k],)
        slot = one_hot(places[k], LANES).astype(F32)
        for i, value in enumerate(values):
            placed = (slot * value.astype(F32)).astype(BF)
            sides[i] = sides[i] + dot(hits[k].astype(BF), placed, ((0,), (0,)))
    expert = iota((experts, rows), 0) * size + DATA
    for i in range(5):
        row = (expert + i == iota((experts, rows), 1)).astype(F32).astype(BF)
        total = total + dot(row, sides[i].astype(BF), ((0,), (0,)))
    dy_out[...] = total.astype(BF)
    lane = iota((n, LANES), 1)
    aux = jnp.zeros((n, LANES), F32)
    for i, column in enumerate(gates + [i.astype(F32) for i in ids + places]):
        aux = jnp.where(lane == i, column, aux)
    aux_out[...] = aux


def send_x(tokens, routes, experts, index):
    n, _ = tokens.shape
    rows = experts * DATA
    return pl.pallas_call(
        functools.partial(send_x_kernel, experts=experts),
        grid_spec=pltpu.PrefetchScalarGridSpec(
            num_scalar_prefetch=1,
            grid=(1,),
            in_specs=[
                pl.BlockSpec((n, 2 * LANES), lambda i, at: (0, at[0])),
                pl.BlockSpec((2, n), lambda i, at: (0, 0)),
            ],
            out_specs=pl.BlockSpec((rows, LANES), lambda i, at: (0, 0)),
        ),
        out_shape=jax.ShapeDtypeStruct((rows, LANES), BF),
        compiler_params=params(),
        name="send_x",
    )(index, tokens, routes)


def send_dy(tokens, cotangent, routes, router, index):
    n, width = tokens.shape
    experts = router.shape[0]
    rows = experts * (DATA + SIDE)
    whole = lambda *shape: pl.BlockSpec(shape, lambda i, at: (0,) * len(shape))
    return pl.pallas_call(
        send_dy_kernel,
        grid_spec=pltpu.PrefetchScalarGridSpec(
            num_scalar_prefetch=1,
            grid=(1,),
            in_specs=[
                whole(n, width),
                pl.BlockSpec((n, 2 * LANES), lambda i, at: (0, at[0])),
                whole(2, n),
                whole(experts, width),
            ],
            out_specs=[whole(rows, LANES), whole(n, LANES)],
        ),
        out_shape=[
            jax.ShapeDtypeStruct((rows, LANES), BF),
            jax.ShapeDtypeStruct((n, LANES), F32),
        ],
        compiler_params=params(),
        name="send_dy",
    )(index, tokens, cotangent, routes, router)


def column_of(mp, k, h):
    member = lax.rem(mp + k + GROUPS, GROUPS)
    return pl.multiple_of((2 * member + h) * LANES, LANES)


def unpack_rows(perm, mp, messages, to, blocks):
    def body(b, carry):
        at = pl.ds(pl.multiple_of(b * 2 * BLOCK, 2 * BLOCK), 2 * BLOCK)
        rows = pl.ds(pl.multiple_of(b * BLOCK, BLOCK), BLOCK)
        both = dot(perm[...], jnp.concatenate([m[at, :] for m in messages], axis=1)).astype(BF)
        for h in range(2):
            for k in range(GROUPS):
                to[rows, pl.ds(column_of(mp, -k, h), LANES)] = both[
                    h * BLOCK : (h + 1) * BLOCK, k * LANES : (k + 1) * LANES
                ]
        return carry

    lax.fori_loop(0, blocks, body, 0)


def forward_kernel(mp, perm, m0, m1, m2, m3, gate, up, down, *refs):
    rows_x, hidden, by_gate, by_up = refs[:4]
    parts = refs[4 : 4 + GROUPS]
    outs = refs[4 + GROUPS]
    step = pl.program_id(0)
    blocks = rows_x.shape[0] // BLOCK

    @pl.when(step == 0)
    def _():
        unpack_rows(perm, mp[0], (m0, m1, m2, m3), rows_x, blocks)

    acts = dot(rows_x[...], jnp.concatenate([gate[...], up[...]], axis=1))
    act_gate = acts[:, :LANES]
    act_up = acts[:, LANES:]
    s = 1.0 / (1.0 + jnp.exp(-act_gate))
    silu = act_gate * s
    hidden[:, pl.ds(pl.multiple_of(step * LANES, LANES), LANES)] = (silu * act_up).astype(BF)
    by_gate[...] = act_up * s * (1.0 + act_gate * (1.0 - s))
    by_up[...] = silu

    @pl.when(step == pl.num_programs(0) - 1)
    def _():
        outs[...] = dot(hidden[...], down[...]).astype(BF)
        for k in range(GROUPS):
            parts[k][...] = outs[:, pl.ds(column_of(mp[0], k, 0), 2 * LANES)]


def expert_forward(mp_index, perm, messages, w_gate, w_up, w_down):
    sent, _ = messages[0].shape
    rows = sent // 2
    width, ff = w_gate.shape
    whole = lambda *shape: pl.BlockSpec(shape, lambda i, mp: (0,) * len(shape))
    column = lambda n: pl.BlockSpec((n, LANES), lambda i, mp: (0, i))
    return pl.pallas_call(
        forward_kernel,
        grid_spec=pltpu.PrefetchScalarGridSpec(
            num_scalar_prefetch=1,
            grid=(ff // LANES,),
            in_specs=[whole(*perm.shape)]
            + [whole(sent, LANES)] * GROUPS
            + [column(width), column(width), whole(ff, width)],
            out_specs=[whole(rows, width), whole(rows, ff), column(rows), column(rows)]
            + [whole(rows, 2 * LANES)] * GROUPS,
            scratch_shapes=[pltpu.VMEM((rows, width), BF)],
        ),
        out_shape=[
            jax.ShapeDtypeStruct((rows, width), BF),
            jax.ShapeDtypeStruct((rows, ff), BF),
            jax.ShapeDtypeStruct((rows, ff), F32),
            jax.ShapeDtypeStruct((rows, ff), F32),
        ]
        + [jax.ShapeDtypeStruct((rows, 2 * LANES), BF)] * GROUPS,
        compiler_params=params(),
        name="expert_forward",
    )(mp_index, perm, *messages, w_gate, w_up, w_down)


def pack_kernel(perm_t, p0, p1, p2, p3, out):
    for b in range(p0.shape[0] // BLOCK):
        rows = slice(b * BLOCK, (b + 1) * BLOCK)
        total = p0[rows, :].astype(F32)
        for p in (p1, p2, p3):
            total = total + p[rows, :].astype(F32)
        total = total.astype(BF)
        halves = jnp.concatenate([total[:, :LANES], total[:, LANES:]], axis=0)
        out[b * 2 * BLOCK : (b + 1) * 2 * BLOCK, :] = dot(perm_t[...], halves).astype(BF)


def pack_rows(perm_t, pieces):
    return pl.pallas_call(
        pack_kernel,
        out_shape=jax.ShapeDtypeStruct((2 * pieces[0].shape[0], LANES), BF),
        compiler_params=params(),
        name="pack_rows",
    )(perm_t, *pieces)


HALVES = 2
CHUNKS = 4


def logit_terms(q, side, expert, experts):
    part = q.shape[0]
    row = iota((part, part // CAP), 0)
    first = iota((part, part // CAP), 1) * CAP
    source = ((row >= first) & (row < first + CAP)).astype(F32)
    place = (iota((part, 1), 0).astype(F32) - row_sum(source * first.astype(F32))).astype(jnp.int32)
    slot = (place == iota((part, LANES), 1)).astype(F32)
    spread = dot(source.astype(BF), jnp.concatenate([side[i] for i in range(5)], axis=1))
    values = [row_sum(spread[:, i * LANES : (i + 1) * LANES] * slot) for i in range(5)]
    own = q * (values[0] + values[1])
    other = q * (values[2] + values[3])
    lane = iota((part, experts), 1)
    grads = jnp.where(lane == expert, own, 0.0)
    return jnp.where(lane == values[4].astype(jnp.int32), other, grads)


def backward_kernel(
    at, perm, m0, m1, m2, m3, side, down, hidden, by_gate, by_up, rows_x,
    g_gate, g_up, g_down, squares, router,
    rows_dy, d_gate, d_up, x_across, hidden_across, router_total, sums,
):
    step = pl.program_id(0)
    part = rows_x.shape[0]
    experts = router.shape[0]

    @pl.when(step < HALVES)
    def _():
        at_rows = pl.ds(pl.multiple_of(step * part, part), part)
        dy = rows_dy.at[at_rows]
        unpack_rows(perm, at[0], (m0, m1, m2, m3), dy, part // BLOCK)
        grad_hidden = dot(dy[...], down[...], ((1,), (1,)))
        d_gate[at_rows, :] = (grad_hidden * by_gate[...]).astype(BF)
        d_up[at_rows, :] = (grad_hidden * by_up[...]).astype(BF)
        x_across[:, at_rows] = rows_x[...].T
        hidden_across[:, at_rows] = hidden[...].T
        q = row_sum(hidden[...].astype(F32) * grad_hidden)
        grads = logit_terms(q, side, at[1], experts)
        both = dot(jnp.concatenate(two_parts(grads), axis=1), rows_x[...], ((0,), (0,)))
        grad = both[:experts] + both[experts:]

        @pl.when(step == 0)
        def _():
            router_total[...] = grad
            sums[...] = jnp.zeros_like(sums)

        @pl.when(step == HALVES - 1)
        def _():
            whole = router_total[...] + grad
            for j in range(router.shape[1]):
                router[:, j, :] = whole[:, j * LANES : (j + 1) * LANES]

    @pl.when(step >= HALVES)
    def _():
        chunk = step - HALVES
        outs = (
            (g_gate, x_across, d_gate),
            (g_up, x_across, d_up),
            (g_down, hidden_across, rows_dy),
        )
        for i, (out, left, right) in enumerate(outs):
            n = out.shape[0]
            grad = dot(left[pl.ds(pl.multiple_of(chunk * n, n), n), :], right[...])
            out[...] = grad
            total = jnp.sum(grad * grad, axis=0, keepdims=True)
            sums[i : i + 1, : grad.shape[1]] += total

    @pl.when(step == pl.num_programs(0) - 1)
    def _():
        lane = iota(squares.shape, 1)
        values = jnp.zeros(squares.shape, F32)
        for i in range(3):
            values = jnp.where(lane == i, row_sum(sums[i : i + 1, :]), values)
        squares[...] = values


def expert_backward(index, perm, messages, side, w_down, hidden, by_gate, by_up, rows_x):
    sent, _ = messages[0].shape
    rows = sent // 2
    part = rows // HALVES
    experts = rows // CAP
    ff, width = w_down.shape
    first = lambda i: jnp.minimum(i, HALVES - 1)
    then = lambda i: jnp.maximum(i - HALVES, 0)
    whole = lambda *shape: pl.BlockSpec(shape, lambda i, at: (0,) * len(shape))
    row = lambda n, m: pl.BlockSpec((n, m), lambda i, at: (first(i), 0))
    out = lambda n, m: pl.BlockSpec((n // CHUNKS, m), lambda i, at: (then(i), 0))
    return pl.pallas_call(
        backward_kernel,
        grid_spec=pltpu.PrefetchScalarGridSpec(
            num_scalar_prefetch=1,
            grid=(HALVES + CHUNKS,),
            in_specs=[whole(*perm.shape)]
            + [row(sent // HALVES, LANES)] * GROUPS
            + [pl.BlockSpec((SIDE, part // CAP, LANES), lambda i, at: (0, first(i), 0))]
            + [whole(ff, width), row(part, ff), row(part, ff), row(part, ff), row(part, width)],
            out_specs=[
                out(width, ff),
                out(width, ff),
                out(ff, width),
                whole(1, LANES),
                whole(experts, width // LANES, LANES),
            ],
            scratch_shapes=[
                pltpu.VMEM((rows, width), BF),
                pltpu.VMEM((rows, ff), BF),
                pltpu.VMEM((rows, ff), BF),
                pltpu.VMEM((width, rows), BF),
                pltpu.VMEM((ff, rows), BF),
                pltpu.VMEM((experts, width), F32),
                pltpu.VMEM((SIDE, width), F32),
            ],
        ),
        out_shape=[
            jax.ShapeDtypeStruct((width, ff), F32),
            jax.ShapeDtypeStruct((width, ff), F32),
            jax.ShapeDtypeStruct((ff, width), F32),
            jax.ShapeDtypeStruct((1, LANES), F32),
            jax.ShapeDtypeStruct((experts, width // LANES, LANES), F32),
        ],
        compiler_params=params(),
        name="expert_backward",
    )(index, perm, *messages, side, w_down, hidden, by_gate, by_up, rows_x)


NET_ROWS = 32


def two_parts(x):
    high = x.astype(BF)
    return high, (x - high.astype(F32)).astype(BF)


def spread_kernel(coef, to):
    k = UNITS * NET_ROWS
    c = 8 * NET_ROWS
    same = iota((k, c), 0) % NET_ROWS == iota((k, c), 1) % NET_ROWS
    feature = iota((k, c), 1) // NET_ROWS
    value = jnp.zeros((k, c), F32)
    for part in range(3):
        a = coef[:, part : part + 1]
        high = a.astype(BF).astype(F32)
        low = a - high
        if part < 2:
            values = (high, low, high)
        else:
            values = (high, low)
        for i, v in enumerate(values):
            value = jnp.where(feature == part * 3 + i, v, value)
    to[...] = jnp.where(same, value, 0.0).astype(BF)


def spread_weights(mlp_in, weight_scale):
    coef = jnp.stack([mlp_in[0], mlp_in[2], mlp_in[1] * weight_scale], axis=1)
    coef = jnp.repeat(coef, NET_ROWS, axis=0)
    return pl.pallas_call(
        spread_kernel,
        out_shape=jax.ShapeDtypeStruct((UNITS * NET_ROWS, 8 * NET_ROWS), BF),
        compiler_params=params(),
        name="spread_weights",
    )(coef)


def step_kernel(scalars, rms, spread, grad, weight, out, *, rows):
    n = NET_ROWS
    height, width = grad.shape
    inverse = rms[0]
    constant = scalars[2, 0]

    def features(r, c, lanes):
        w = weight[pl.ds(r, n), c : c + lanes]
        f0 = grad[pl.ds(r, n), c : c + lanes] * inverse
        h0, l0 = two_parts(f0)
        h2, l2 = two_parts(jnp.tanh(f0))
        return jnp.concatenate([h0, h0, l0, h2, h2, l2, w, w], axis=0)

    def network(feats):
        y = dot(spread[...], feats)
        total = jnp.full((n, feats.shape[1]), constant, F32)
        for j in range(UNITS):
            total = total + scalars[1, j] * jnp.maximum(y[j * n : (j + 1) * n], scalars[0, j])
        return total.astype(BF)

    def body(i, carry):
        r = pl.multiple_of(i * rows, rows)
        for pair in range(0, rows, 2 * n):
            at = [r + pair, r + pair + n]
            whole = width // 256 * 256
            for c in range(0, whole, 256):
                for a in at:
                    out[pl.ds(a, n), c : c + 256] = network(features(a, c, 256))
            if whole < width:
                u = network(jnp.concatenate([features(a, whole, 128) for a in at], axis=1))
                for i, a in enumerate(at):
                    out[pl.ds(a, n), whole:width] = u[:, i * 128 : (i + 1) * 128]
        return carry

    lax.fori_loop(0, height // rows, body, 0)


def learned_step(grad, weight, rms, spread, scalars):
    height, width = grad.shape
    block = 128
    tile = pl.BlockSpec((block, width), lambda i: (i, 0))
    return pl.pallas_call(
        functools.partial(step_kernel, rows=128),
        grid=(height // block,),
        in_specs=[
            pl.BlockSpec(memory_space=pltpu.SMEM),
            pl.BlockSpec(memory_space=pltpu.SMEM),
            pl.BlockSpec(spread.shape, lambda i: (0, 0)),
            tile,
            tile,
        ],
        out_specs=tile,
        out_shape=jax.ShapeDtypeStruct((height, width), BF),
        compiler_params=params(),
        name="learned_step",
    )(scalars, rms, spread, in_hbm(grad), in_hbm(weight))


def mix_kernel(at, aux, tok_cols, back, out, *, size):
    del at
    rows = back.shape[0]
    for h in range(2):
        cols = slice(h * LANES, (h + 1) * LANES)
        total = tok_cols[:, cols].astype(F32)
        for k in range(2):
            base = aux[:, 2 + k : 3 + k] * size + aux[:, 4 + k : 5 + k] + h * CAP
            total = total + aux[:, k : k + 1] * dot(
                one_hot(base.astype(jnp.int32), rows), back[...]
            )
        out[:, cols] = total.astype(BF)


def mix(index, aux, tokens, back, experts):
    n = tokens.shape[0]
    cols = 2 * LANES
    whole = lambda *shape: pl.BlockSpec(shape, lambda i, at: (0,) * len(shape))
    mine = pl.BlockSpec((n, cols), lambda i, at: (0, at[0]))
    return pl.pallas_call(
        functools.partial(mix_kernel, size=back.shape[0] // experts),
        grid_spec=pltpu.PrefetchScalarGridSpec(
            num_scalar_prefetch=1,
            grid=(1,),
            in_specs=[whole(n, LANES), mine, whole(*back.shape)],
            out_specs=whole(n, cols),
        ),
        out_shape=jax.ShapeDtypeStruct((n, cols), BF),
        compiler_params=params(),
        name="mix",
    )(index, aux, tokens, back)


def router_step_kernel(net, columns, weight, out):
    experts, width = weight.shape
    grad = jnp.concatenate([columns[:, j, :] for j in range(width // LANES)], axis=1)
    mean = jnp.sum(row_sum(grad * grad), axis=0, keepdims=True) * (1.0 / grad.size)
    f0 = grad / jnp.sqrt(mean + EPSILON)
    f1 = weight[...].astype(F32) * D**0.5
    f2 = jnp.tanh(f0)
    total = jnp.zeros_like(f0)
    for j in range(UNITS):
        total = total + net[4, j] * jnp.maximum(
            net[0, j] * f0 + net[1, j] * f1 + net[2, j] * f2 + net[3, j], 0.0
        )
    out[...] = total.astype(BF)


def router_step(net, parts, weight):
    return pl.pallas_call(
        router_step_kernel,
        in_specs=[
            pl.BlockSpec(memory_space=pltpu.SMEM),
            pl.BlockSpec(memory_space=pltpu.VMEM),
            pl.BlockSpec(memory_space=pltpu.VMEM),
        ],
        out_shape=jax.ShapeDtypeStruct(weight.shape, BF),
        compiler_params=params(),
        name="router_step",
    )(net, parts, weight)


def to_experts(x, peers):
    sent = x.reshape(peers, -1, x.shape[-1])
    return lax.all_to_all(sent, EXPERT, 0, 0, tiled=True)


def from_members(pieces):
    return [pieces[0]] + [
        lax.ppermute(pieces[k], "mp", [(i, (i + k) % GROUPS) for i in range(GROUPS)])
        for k in range(1, GROUPS)
    ]


def together(values):
    return lax.optimization_barrier(values)


def on_device(
    tokens,
    cotangent,
    routes,
    router_weight,
    gate_weight,
    up_weight,
    down_weight,
    mlp_in,
    mlp_bias,
    mlp_out,
):
    experts = lax.axis_size(EXPERT)
    groups = lax.axis_size("mp")
    width = tokens.shape[1]
    index = jnp.stack([lax.axis_index("mp"), lax.axis_index(EXPERT)]).astype(jnp.int32)
    w_gate = gate_weight[0]
    w_up = up_weight[0]
    w_down = down_weight[0]

    pos = jnp.arange(2 * BLOCK, dtype=jnp.int32)
    inner = pos % BLOCK
    source_row = inner + inner // CAP * CAP + pos // BLOCK * CAP
    perm = (source_row[:, None] == pos[None, :]).astype(BF)
    perm_t = (source_row[None, :] == pos[:, None]).astype(BF)
    spread_in = spread_weights(mlp_in, D**0.5)
    spread_down = spread_weights(mlp_in, FF**0.5)
    scalars = jnp.stack(
        [-mlp_bias, mlp_out, jnp.broadcast_to(jnp.sum(mlp_bias * mlp_out), mlp_out.shape)]
    )
    net = jnp.concatenate([mlp_in, mlp_bias[None], mlp_out[None]], axis=0)
    router_across = router_weight.T

    routes_across = routes.T
    sent_x = send_x(in_hbm(tokens), routes_across, experts, index)
    own_x = to_experts(sent_x, experts).reshape(-1, LANES)
    sent_dy, aux = send_dy(in_hbm(tokens), in_hbm(cotangent), routes_across, router_across, index)
    sent_dy, perm, perm_t, spread_in, spread_down, scalars, net = together(
        (sent_dy, perm, perm_t, spread_in, spread_down, scalars, net)
    )
    msg_x = from_members([own_x] * GROUPS)
    own_dy = to_experts(sent_dy, experts)
    side = own_dy[:, DATA:].transpose(1, 0, 2)
    own_dy = own_dy[:, :DATA].reshape(-1, LANES)
    perm, own_dy = together((perm, own_dy))
    msg_dy = from_members([own_dy] * GROUPS)

    rows_x, hidden, by_gate, by_up, *parts = expert_forward(
        index, perm, msg_x, w_gate, w_up, w_down
    )
    swapped = from_members(parts)

    g_gate, g_up, g_down, squares, router_part = expert_backward(
        index, perm, msg_dy, side, w_down, hidden, by_gate, by_up, rows_x
    )
    high = lax.reduce_precision(squares, 8, 7)
    row = iota((SIDE, LANES), 0)
    squares = jnp.where(row == 0, high, jnp.where(row == 1, squares - high, 0.0))
    terms = jnp.concatenate(
        [router_part, jnp.broadcast_to(squares[None], (experts, SIDE, LANES))], axis=1
    ).astype(BF)
    swapped, terms = together((swapped, terms))
    expert_out = pack_rows(perm_t, swapped).reshape(experts, DATA, LANES)
    sums = jnp.sum(to_experts(terms, experts).astype(F32), axis=0)
    sums = sum(from_members([sums] * GROUPS))
    total_count = experts * width * w_gate.shape[1] * groups
    inverse = 1.0 / jnp.sqrt((sums[SIDE] + sums[SIDE + 1]) / total_count + EPSILON)
    column = sums[:SIDE]
    high = lax.reduce_precision(column, 8, 7)
    column = jnp.concatenate([high, column - high], axis=0).astype(BF)
    column = jnp.broadcast_to(column[None], (experts, 2 * SIDE, LANES))
    back = to_experts(jnp.concatenate([expert_out, column], axis=1), experts)

    down_update = learned_step(g_down, w_down, inverse[2:3], spread_down, scalars)
    gate_update = learned_step(g_gate, w_gate, inverse[0:1], spread_in, scalars)
    up_update = learned_step(g_up, w_up, inverse[1:2], spread_in, scalars)
    back, up_update = together((back, up_update))
    mixed = mix(index, aux, tokens, back.reshape(-1, LANES), experts)
    columns = back[:, DATA : DATA + SIDE].astype(F32) + back[:, DATA + SIDE :].astype(F32)
    router_update = router_step(net, columns, router_across).T
    return (mixed, gate_update[None], up_update[None], down_update[None], router_update)


def solution(mesh):
    torus = Mesh(
        mesh.devices.reshape(8, 4, 2, mesh.shape["mp"]), ("expert_0", "expert_1", "expert_2", "mp")
    )
    placed = (
        P(EXPERT, None),
        P(EXPERT, None),
        P(EXPERT, None),
        P(),
        P(EXPERT, None, "mp"),
        P(EXPERT, None, "mp"),
        P(EXPERT, "mp", None),
        P(),
        P(),
        P(),
    )
    return jax.shard_map(
        on_device,
        mesh=torus,
        in_specs=placed,
        out_specs=(
            P(EXPERT, "mp"),
            P(EXPERT, None, "mp"),
            P(EXPERT, None, "mp"),
            P(EXPERT, "mp", None),
            P(),
        ),
        check_vma=False,
    )
```

```python
import functools

import jax
import jax.numpy as jnp
from jax import lax
from jax.experimental import pallas as pl
from jax.experimental.pallas import tpu as pltpu
from jax.sharding import Mesh
from jax.sharding import PartitionSpec as P

D = 1024
FF = 3584
UNITS = 16
EXPERT = ("expert_0", "expert_1", "expert_2")
EPSILON = 1e-06

CAP = 12
GROUP = 16
GROUPS = 4
BLOCK = GROUP * CAP
LANES = 128
BF = jnp.bfloat16
F32 = jnp.float32
HIGHEST = lax.Precision.HIGHEST


def params(**kw):
    return pltpu.CompilerParams(vmem_limit_bytes=48 << 20, **kw)


def in_hbm(x):
    return pltpu.with_memory_space_constraint(x, pltpu.HBM)


def iota(shape, dim):
    return lax.broadcasted_iota(jnp.int32, shape, dim)


def dot(a, b, dims=((1,), (0,)), **kw):
    return lax.dot_general(a, b, (dims, ((), ())), preferred_element_type=F32, **kw)


def row_sum(x):
    return jnp.sum(x, axis=1, keepdims=True)


DATA = 2 * CAP
SIDE = 8


def routing(routes, experts):
    across = routes[...].astype(F32).T
    n = across.shape[0]
    ids = [across[:, k : k + 1].astype(jnp.int32) for k in range(2)]
    hits = [(ids[k] == iota((n, experts), 1)).astype(F32) for k in range(2)]
    earlier = (iota((n, n), 0) > iota((n, n), 1)).astype(F32).astype(BF)
    before = dot(earlier, (hits[0] + hits[1]).astype(BF))
    places = [row_sum(before * hits[k]).astype(jnp.int32) for k in range(2)]
    return ids, places, hits


def one_hot(index, size):
    return (index == iota((index.shape[0], size), 1)).astype(F32).astype(BF)


def send_x_kernel(at, tok_cols, routes, x_out, *, experts):
    del at
    n = tok_cols.shape[0]
    rows = x_out.shape[0]
    ids = [routes[k : k + 1, :] for k in range(2)]
    hits = [(ids[k] == iota((experts, n), 0)).astype(F32) for k in range(2)]
    earlier = (iota((n, n), 0) < iota((n, n), 1)).astype(F32).astype(BF)
    before = dot((hits[0] + hits[1]).astype(BF), earlier)
    base = [
        ids[k] * DATA + jnp.sum(before * hits[k], axis=0, keepdims=True).astype(jnp.int32)
        for k in range(2)
    ]
    row = iota((rows, n), 0)
    total = jnp.zeros((rows, LANES), F32)
    for h in range(2):
        picked = (base[0] + h * CAP == row) | (base[1] + h * CAP == row)
        total = total + dot(
            picked.astype(F32).astype(BF), tok_cols[:, h * LANES : (h + 1) * LANES]
        )
    x_out[...] = total.astype(BF)


def send_dy_kernel(mp, tok, cot_cols, routes, router, dy_out, aux_out):
    del mp
    n = tok.shape[0]
    experts = router.shape[0]
    rows = dy_out.shape[0]
    size = DATA + SIDE
    ids, places, hits = routing(routes, experts)
    logits = dot(tok[...], router[...], ((1,), (1,)))
    sig = [1.0 / (1.0 + jnp.exp(-row_sum(logits * hits[k]))) for k in range(2)]
    denominator = sig[0] + sig[1]
    gates = [s / denominator for s in sig]
    cot = cot_cols[...].astype(F32)
    total = jnp.zeros((rows, LANES), F32)
    sides = [jnp.zeros((experts, LANES), F32) for _ in range(5)]
    for k in range(2):
        scaled = (gates[k] * cot).astype(BF)
        for h in range(2):
            pick = one_hot(ids[k] * size + places[k] + h * CAP, rows)
            total = total + dot(pick, scaled[:, h * LANES : (h + 1) * LANES], ((0,), (0,)))
        own = gates[1 - k] * (1.0 - sig[k])
        other = -gates[1 - k] * (1.0 - sig[1 - k])
        values = two_parts(own) + two_parts(other) + (ids[1 - k],)
        slot = one_hot(places[k], LANES).astype(F32)
        for i, value in enumerate(values):
            placed = (slot * value.astype(F32)).astype(BF)
            sides[i] = sides[i] + dot(hits[k].astype(BF), placed, ((0,), (0,)))
    expert = iota((experts, rows), 0) * size + DATA
    for i in range(5):
        row = (expert + i == iota((experts, rows), 1)).astype(F32).astype(BF)
        total = total + dot(row, sides[i].astype(BF), ((0,), (0,)))
    dy_out[...] = total.astype(BF)
    lane = iota((n, LANES), 1)
    aux = jnp.zeros((n, LANES), F32)
    for i, column in enumerate(gates + [i.astype(F32) for i in ids + places]):
        aux = jnp.where(lane == i, column, aux)
    aux_out[...] = aux


def send_x(tokens, routes, experts, index):
    n, _ = tokens.shape
    rows = experts * DATA
    return pl.pallas_call(
        functools.partial(send_x_kernel, experts=experts),
        grid_spec=pltpu.PrefetchScalarGridSpec(
            num_scalar_prefetch=1,
            grid=(1,),
            in_specs=[
                pl.BlockSpec((n, 2 * LANES), lambda i, at: (0, at[0])),
                pl.BlockSpec((2, n), lambda i, at: (0, 0)),
            ],
            out_specs=pl.BlockSpec((rows, LANES), lambda i, at: (0, 0)),
        ),
        out_shape=jax.ShapeDtypeStruct((rows, LANES), BF),
        compiler_params=params(),
        name="send_x",
    )(index, tokens, routes)


def send_dy(tokens, cotangent, routes, router, index):
    n, width = tokens.shape
    experts = router.shape[0]
    rows = experts * (DATA + SIDE)
    whole = lambda *shape: pl.BlockSpec(shape, lambda i, at: (0,) * len(shape))
    return pl.pallas_call(
        send_dy_kernel,
        grid_spec=pltpu.PrefetchScalarGridSpec(
            num_scalar_prefetch=1,
            grid=(1,),
            in_specs=[
                whole(n, width),
                pl.BlockSpec((n, 2 * LANES), lambda i, at: (0, at[0])),
                whole(2, n),
                whole(experts, width),
            ],
            out_specs=[whole(rows, LANES), whole(n, LANES)],
        ),
        out_shape=[
            jax.ShapeDtypeStruct((rows, LANES), BF),
            jax.ShapeDtypeStruct((n, LANES), F32),
        ],
        compiler_params=params(),
        name="send_dy",
    )(index, tokens, cotangent, routes, router)


def column_of(mp, k, h):
    member = lax.rem(mp + k + GROUPS, GROUPS)
    return pl.multiple_of((2 * member + h) * LANES, LANES)


def unpack_rows(perm, mp, messages, to, blocks):
    def body(b, carry):
        at = pl.ds(pl.multiple_of(b * 2 * BLOCK, 2 * BLOCK), 2 * BLOCK)
        rows = pl.ds(pl.multiple_of(b * BLOCK, BLOCK), BLOCK)
        both = dot(perm[...], jnp.concatenate([m[at, :] for m in messages], axis=1)).astype(BF)
        for h in range(2):
            for k in range(GROUPS):
                to[rows, pl.ds(column_of(mp, -k, h), LANES)] = both[
                    h * BLOCK : (h + 1) * BLOCK, k * LANES : (k + 1) * LANES
                ]
        return carry

    lax.fori_loop(0, blocks, body, 0)


def forward_kernel(mp, perm, m0, m1, m2, m3, gate, up, down, *refs):
    rows_x, hidden, by_gate, by_up = refs[:4]
    parts = refs[4 : 4 + GROUPS]
    outs = refs[4 + GROUPS]
    step = pl.program_id(0)
    blocks = rows_x.shape[0] // BLOCK

    @pl.when(step == 0)
    def _():
        unpack_rows(perm, mp[0], (m0, m1, m2, m3), rows_x, blocks)

    acts = dot(rows_x[...], jnp.concatenate([gate[...], up[...]], axis=1))
    act_gate = acts[:, :LANES]
    act_up = acts[:, LANES:]
    s = 1.0 / (1.0 + jnp.exp(-act_gate))
    silu = act_gate * s
    hidden[:, pl.ds(pl.multiple_of(step * LANES, LANES), LANES)] = (silu * act_up).astype(BF)
    by_gate[...] = act_up * s * (1.0 + act_gate * (1.0 - s))
    by_up[...] = silu

    @pl.when(step == pl.num_programs(0) - 1)
    def _():
        outs[...] = dot(hidden[...], down[...]).astype(BF)
        for k in range(GROUPS):
            parts[k][...] = outs[:, pl.ds(column_of(mp[0], k, 0), 2 * LANES)]


def expert_forward(mp_index, perm, messages, w_gate, w_up, w_down):
    sent, _ = messages[0].shape
    rows = sent // 2
    width, ff = w_gate.shape
    whole = lambda *shape: pl.BlockSpec(shape, lambda i, mp: (0,) * len(shape))
    column = lambda n: pl.BlockSpec((n, LANES), lambda i, mp: (0, i))
    return pl.pallas_call(
        forward_kernel,
        grid_spec=pltpu.PrefetchScalarGridSpec(
            num_scalar_prefetch=1,
            grid=(ff // LANES,),
            in_specs=[whole(*perm.shape)]
            + [whole(sent, LANES)] * GROUPS
            + [column(width), column(width), whole(ff, width)],
            out_specs=[whole(rows, width), whole(rows, ff), column(rows), column(rows)]
            + [whole(rows, 2 * LANES)] * GROUPS,
            scratch_shapes=[pltpu.VMEM((rows, width), BF)],
        ),
        out_shape=[
            pltpu.HBM((rows, width), BF),
            pltpu.HBM((rows, ff), BF),
            pltpu.HBM((rows, ff), F32),
            pltpu.HBM((rows, ff), F32),
        ]
        + [pltpu.HBM((rows, 2 * LANES), BF)] * GROUPS,
        compiler_params=params(),
        name="expert_forward",
    )(mp_index, perm, *messages, w_gate, w_up, w_down)


def pack_kernel(perm_t, p0, p1, p2, p3, out):
    for b in range(p0.shape[0] // BLOCK):
        rows = slice(b * BLOCK, (b + 1) * BLOCK)
        total = p0[rows, :].astype(F32)
        for p in (p1, p2, p3):
            total = total + p[rows, :].astype(F32)
        total = total.astype(BF)
        halves = jnp.concatenate([total[:, :LANES], total[:, LANES:]], axis=0)
        out[b * 2 * BLOCK : (b + 1) * 2 * BLOCK, :] = dot(perm_t[...], halves).astype(BF)


def pack_rows(perm_t, pieces):
    return pl.pallas_call(
        pack_kernel,
        out_shape=jax.ShapeDtypeStruct((2 * pieces[0].shape[0], LANES), BF),
        compiler_params=params(),
        name="pack_rows",
    )(perm_t, *pieces)


HALVES = 2
CHUNKS = 4


def logit_terms(q, side, expert, experts):
    part = q.shape[0]
    row = iota((part, part // CAP), 0)
    first = iota((part, part // CAP), 1) * CAP
    source = ((row >= first) & (row < first + CAP)).astype(F32)
    place = (iota((part, 1), 0).astype(F32) - row_sum(source * first.astype(F32))).astype(jnp.int32)
    slot = (place == iota((part, LANES), 1)).astype(F32)
    both = side[...].astype(F32)
    both = jnp.concatenate([both[:, DATA + i, :] for i in range(5)], axis=1).astype(BF)
    spread = dot(source.astype(BF), both)
    values = [row_sum(spread[:, i * LANES : (i + 1) * LANES] * slot) for i in range(5)]
    own = q * (values[0] + values[1])
    other = q * (values[2] + values[3])
    lane = iota((part, experts), 1)
    grads = jnp.where(lane == expert, own, 0.0)
    return jnp.where(lane == values[4].astype(jnp.int32), other, grads)


def backward_kernel(
    at, perm, m0, m1, m2, m3, side, down, hidden, by_gate, by_up, rows_x,
    g_gate, g_up, g_down, squares, router,
    rows_dy, d_gate, d_up, x_across, hidden_across, router_total, sums,
):
    step = pl.program_id(0)
    part = rows_x.shape[0]
    experts = router.shape[0]

    @pl.when(step < HALVES)
    def _():
        at_rows = pl.ds(pl.multiple_of(step * part, part), part)
        dy = rows_dy.at[at_rows]
        unpack_rows(perm, at[0], (m0, m1, m2, m3), dy, part // BLOCK)
        grad_hidden = dot(dy[...], down[...], ((1,), (1,)))
        d_gate[at_rows, :] = (grad_hidden * by_gate[...]).astype(BF)
        d_up[at_rows, :] = (grad_hidden * by_up[...]).astype(BF)
        x_across[:, at_rows] = rows_x[...].T
        hidden_across[:, at_rows] = hidden[...].T
        q = row_sum(hidden[...].astype(F32) * grad_hidden)
        grads = logit_terms(q, side, at[1], experts)
        both = dot(jnp.concatenate(two_parts(grads), axis=1), rows_x[...], ((0,), (0,)))
        grad = both[:experts] + both[experts:]

        @pl.when(step == 0)
        def _():
            router_total[...] = grad
            sums[...] = jnp.zeros_like(sums)

        @pl.when(step == HALVES - 1)
        def _():
            whole = router_total[...] + grad
            for j in range(router.shape[1]):
                router[:, j, :] = whole[:, j * LANES : (j + 1) * LANES]

    @pl.when(step >= HALVES)
    def _():
        chunk = step - HALVES
        outs = (
            (g_gate, x_across, d_gate),
            (g_up, x_across, d_up),
            (g_down, hidden_across, rows_dy),
        )
        for i, (out, left, right) in enumerate(outs):
            n = out.shape[0]
            grad = dot(left[pl.ds(pl.multiple_of(chunk * n, n), n), :], right[...])
            out[...] = grad
            total = jnp.sum(grad * grad, axis=0, keepdims=True)
            sums[i : i + 1, : grad.shape[1]] += total

    @pl.when(step == pl.num_programs(0) - 1)
    def _():
        lane = iota(squares.shape, 1)
        values = jnp.zeros(squares.shape, F32)
        for i in range(3):
            values = jnp.where(lane == i, row_sum(sums[i : i + 1, :]), values)
        squares[...] = values


def expert_backward(index, perm, messages, side, w_down, hidden, by_gate, by_up, rows_x):
    sent, _ = messages[0].shape
    rows = sent // 2
    part = rows // HALVES
    experts = rows // CAP
    ff, width = w_down.shape
    first = lambda i: jnp.minimum(i, HALVES - 1)
    then = lambda i: jnp.maximum(i - HALVES, 0)
    whole = lambda *shape: pl.BlockSpec(shape, lambda i, at: (0,) * len(shape))
    row = lambda n, m: pl.BlockSpec((n, m), lambda i, at: (first(i), 0))
    out = lambda n, m: pl.BlockSpec((n // CHUNKS, m), lambda i, at: (then(i), 0))
    return pl.pallas_call(
        backward_kernel,
        grid_spec=pltpu.PrefetchScalarGridSpec(
            num_scalar_prefetch=1,
            grid=(HALVES + CHUNKS,),
            in_specs=[whole(*perm.shape)]
            + [row(sent // HALVES, LANES)] * GROUPS
            + [pl.BlockSpec((part // CAP, DATA + SIDE, LANES), lambda i, at: (first(i), 0, 0))]
            + [whole(ff, width), row(part, ff), row(part, ff), row(part, ff), row(part, width)],
            out_specs=[
                out(width, ff),
                out(width, ff),
                out(ff, width),
                whole(1, LANES),
                whole(experts, width // LANES, LANES),
            ],
            scratch_shapes=[
                pltpu.VMEM((rows, width), BF),
                pltpu.VMEM((rows, ff), BF),
                pltpu.VMEM((rows, ff), BF),
                pltpu.VMEM((width, rows), BF),
                pltpu.VMEM((ff, rows), BF),
                pltpu.VMEM((experts, width), F32),
                pltpu.VMEM((SIDE, width), F32),
            ],
        ),
        out_shape=[
            pltpu.HBM((width, ff), F32),
            pltpu.HBM((width, ff), F32),
            pltpu.HBM((ff, width), F32),
            jax.ShapeDtypeStruct((1, LANES), F32),
            jax.ShapeDtypeStruct((experts, width // LANES, LANES), F32),
        ],
        compiler_params=params(),
        name="expert_backward",
    )(
        index, perm, *messages, side, in_hbm(w_down), in_hbm(hidden), in_hbm(by_gate), in_hbm(by_up),
        in_hbm(rows_x),
    )


NET_ROWS = 32


def two_parts(x):
    high = x.astype(BF)
    return high, (x - high.astype(F32)).astype(BF)


def spread_kernel(coef, to):
    k = UNITS * NET_ROWS
    c = 8 * NET_ROWS
    same = iota((k, c), 0) % NET_ROWS == iota((k, c), 1) % NET_ROWS
    feature = iota((k, c), 1) // NET_ROWS
    value = jnp.zeros((k, c), F32)
    for part in range(3):
        a = coef[:, part : part + 1]
        high = a.astype(BF).astype(F32)
        low = a - high
        if part < 2:
            values = (high, low, high)
        else:
            values = (high, low)
        for i, v in enumerate(values):
            value = jnp.where(feature == part * 3 + i, v, value)
    to[...] = jnp.where(same, value, 0.0).astype(BF)


def spread_weights(mlp_in, weight_scale):
    coef = jnp.stack([mlp_in[0], mlp_in[2], mlp_in[1] * weight_scale], axis=1)
    coef = jnp.repeat(coef, NET_ROWS, axis=0)
    return pl.pallas_call(
        spread_kernel,
        out_shape=jax.ShapeDtypeStruct((UNITS * NET_ROWS, 8 * NET_ROWS), BF),
        compiler_params=params(),
        name="spread_weights",
    )(coef)


def step_kernel(scalars, rms, spread, grad, weight, out, *, rows):
    n = NET_ROWS
    height, width = grad.shape
    inverse = rms[0]
    constant = scalars[2, 0]

    def features(r, c, lanes):
        w = weight[pl.ds(r, n), c : c + lanes]
        f0 = grad[pl.ds(r, n), c : c + lanes] * inverse
        h0, l0 = two_parts(f0)
        h2, l2 = two_parts(jnp.tanh(f0))
        return jnp.concatenate([h0, h0, l0, h2, h2, l2, w, w], axis=0)

    def network(feats):
        y = dot(spread[...], feats)
        total = jnp.full((n, feats.shape[1]), constant, F32)
        for j in range(UNITS):
            total = total + scalars[1, j] * jnp.maximum(y[j * n : (j + 1) * n], scalars[0, j])
        return total.astype(BF)

    def body(i, carry):
        r = pl.multiple_of(i * rows, rows)
        for pair in range(0, rows, 2 * n):
            at = [r + pair, r + pair + n]
            whole = width // 256 * 256
            for c in range(0, whole, 256):
                for a in at:
                    out[pl.ds(a, n), c : c + 256] = network(features(a, c, 256))
            if whole < width:
                u = network(jnp.concatenate([features(a, whole, 128) for a in at], axis=1))
                for i, a in enumerate(at):
                    out[pl.ds(a, n), whole:width] = u[:, i * 128 : (i + 1) * 128]
        return carry

    lax.fori_loop(0, height // rows, body, 0)


def learned_step(grad, weight, rms, spread, scalars):
    height, width = grad.shape
    block = 128
    tile = pl.BlockSpec((block, width), lambda i: (i, 0))
    return pl.pallas_call(
        functools.partial(step_kernel, rows=128),
        grid=(height // block,),
        in_specs=[
            pl.BlockSpec(memory_space=pltpu.SMEM),
            pl.BlockSpec(memory_space=pltpu.SMEM),
            pl.BlockSpec(spread.shape, lambda i: (0, 0)),
            tile,
            tile,
        ],
        out_specs=tile,
        out_shape=jax.ShapeDtypeStruct((height, width), BF),
        compiler_params=params(),
        name="learned_step",
    )(scalars, rms, spread, in_hbm(grad), in_hbm(weight))


def mix_kernel(at, aux, tok_cols, back, out, *, size):
    del at
    rows = back.shape[0]
    later = jnp.concatenate([back[CAP:, :], back[:CAP, :]], axis=0)
    both = jnp.concatenate([back[...], later], axis=1)
    total = tok_cols[...].astype(F32)
    for k in range(2):
        base = aux[:, 2 + k : 3 + k] * size + aux[:, 4 + k : 5 + k]
        total = total + aux[:, k : k + 1] * dot(one_hot(base.astype(jnp.int32), rows), both)
    out[...] = total.astype(BF)


def mix(index, aux, tokens, back, experts):
    n = tokens.shape[0]
    cols = 2 * LANES
    whole = lambda *shape: pl.BlockSpec(shape, lambda i, at: (0,) * len(shape))
    mine = pl.BlockSpec((n, cols), lambda i, at: (0, at[0]))
    return pl.pallas_call(
        functools.partial(mix_kernel, size=back.shape[0] // experts),
        grid_spec=pltpu.PrefetchScalarGridSpec(
            num_scalar_prefetch=1,
            grid=(1,),
            in_specs=[whole(n, LANES), mine, whole(*back.shape)],
            out_specs=whole(n, cols),
        ),
        out_shape=jax.ShapeDtypeStruct((n, cols), BF),
        compiler_params=params(),
        name="mix",
    )(index, aux, tokens, back)


def router_step_kernel(net, columns, weight, out):
    experts, width = weight.shape
    grad = jnp.concatenate([columns[:, j, :] for j in range(width // LANES)], axis=1)
    mean = jnp.sum(row_sum(grad * grad), axis=0, keepdims=True) * (1.0 / grad.size)
    f0 = grad / jnp.sqrt(mean + EPSILON)
    f1 = weight[...].astype(F32) * D**0.5
    f2 = jnp.tanh(f0)
    total = jnp.zeros_like(f0)
    for j in range(UNITS):
        total = total + net[4, j] * jnp.maximum(
            net[0, j] * f0 + net[1, j] * f1 + net[2, j] * f2 + net[3, j], 0.0
        )
    out[...] = total.astype(BF)


def router_step(net, parts, weight):
    return pl.pallas_call(
        router_step_kernel,
        in_specs=[
            pl.BlockSpec(memory_space=pltpu.SMEM),
            pl.BlockSpec(memory_space=pltpu.VMEM),
            pl.BlockSpec(memory_space=pltpu.VMEM),
        ],
        out_shape=jax.ShapeDtypeStruct(weight.shape, BF),
        compiler_params=params(),
        name="router_step",
    )(net, parts, weight)


def to_experts(x, peers):
    sent = x.reshape(peers, -1, x.shape[-1])
    return lax.all_to_all(sent, EXPERT, 0, 0, tiled=True)


def from_members(pieces):
    return [pieces[0]] + [
        lax.ppermute(pieces[k], "mp", [(i, (i + k) % GROUPS) for i in range(GROUPS)])
        for k in range(1, GROUPS)
    ]


def together(values):
    return lax.optimization_barrier(values)


def on_device(
    tokens,
    cotangent,
    routes,
    router_weight,
    gate_weight,
    up_weight,
    down_weight,
    mlp_in,
    mlp_bias,
    mlp_out,
):
    experts = lax.axis_size(EXPERT)
    groups = lax.axis_size("mp")
    width = tokens.shape[1]
    index = jnp.stack([lax.axis_index("mp"), lax.axis_index(EXPERT)]).astype(jnp.int32)
    w_gate = gate_weight[0]
    w_up = up_weight[0]
    w_down = down_weight[0]

    pos = jnp.arange(2 * BLOCK, dtype=jnp.int32)
    inner = pos % BLOCK
    source_row = inner + inner // CAP * CAP + pos // BLOCK * CAP
    perm = (source_row[:, None] == pos[None, :]).astype(BF)
    perm_t = (source_row[None, :] == pos[:, None]).astype(BF)
    spread_in = spread_weights(mlp_in, D**0.5)
    spread_down = spread_weights(mlp_in, FF**0.5)
    scalars = jnp.stack(
        [-mlp_bias, mlp_out, jnp.broadcast_to(jnp.sum(mlp_bias * mlp_out), mlp_out.shape)]
    )
    net = jnp.concatenate([mlp_in, mlp_bias[None], mlp_out[None]], axis=0)
    router_across = router_weight.T

    routes_across = in_hbm(routes.T)
    sent_x = send_x(in_hbm(tokens), routes_across, experts, index)
    own_x = to_experts(sent_x, experts).reshape(-1, LANES)
    sent_dy, aux = send_dy(in_hbm(tokens), in_hbm(cotangent), routes_across, router_across, index)
    sent_dy, perm, perm_t, spread_in, spread_down, scalars, net = together(
        (sent_dy, perm, perm_t, spread_in, spread_down, scalars, net)
    )
    msg_x = from_members([own_x] * GROUPS)
    all_dy = to_experts(sent_dy, experts)
    own_dy = all_dy[:, :DATA].reshape(-1, LANES)
    perm, own_dy = together((perm, own_dy))
    msg_dy = from_members([own_dy] * GROUPS)

    rows_x, hidden, by_gate, by_up, *parts = expert_forward(
        index, perm, msg_x, w_gate, w_up, w_down
    )

    g_gate, g_up, g_down, squares, router_part = expert_backward(
        index, perm, msg_dy, all_dy, w_down, hidden, by_gate, by_up, rows_x
    )
    high = lax.reduce_precision(squares, 8, 7)
    row = iota((SIDE, LANES), 0)
    squares = jnp.where(row == 0, high, jnp.where(row == 1, squares - high, 0.0))
    terms = jnp.concatenate(
        [router_part, jnp.broadcast_to(squares[None], (experts, SIDE, LANES))], axis=1
    ).astype(BF)
    parts, terms = together((parts, terms))
    swapped = from_members(parts)
    sums = jnp.sum(to_experts(terms, experts).astype(F32), axis=0)
    sums = sum(from_members([sums] * GROUPS))
    total_count = experts * width * w_gate.shape[1] * groups
    inverse = 1.0 / jnp.sqrt((sums[SIDE] + sums[SIDE + 1]) / total_count + EPSILON)
    column = sums[:SIDE]
    high = lax.reduce_precision(column, 8, 7)
    column = jnp.concatenate([high, column - high], axis=0).astype(BF)
    column = jnp.broadcast_to(column[None], (experts, 2 * SIDE, LANES))

    down_update = learned_step(g_down, w_down, inverse[2:3], spread_down, scalars)
    swapped, down_update = together((swapped, down_update))
    expert_out = pack_rows(perm_t, swapped).reshape(experts, DATA, LANES)
    back = jnp.concatenate([expert_out, column], axis=1)
    back, g_gate, g_up = together((back, g_gate, g_up))
    back = to_experts(back, experts)
    gate_update = learned_step(g_gate, w_gate, inverse[0:1], spread_in, scalars)
    up_update = learned_step(g_up, w_up, inverse[1:2], spread_in, scalars)
    back, up_update = together((back, up_update))
    mixed = mix(index, aux, tokens, back.reshape(-1, LANES), experts)
    columns = back[:, DATA : DATA + SIDE].astype(F32) + back[:, DATA + SIDE :].astype(F32)
    router_update = router_step(net, columns, router_across).T
    return (mixed, gate_update[None], up_update[None], down_update[None], router_update)


def solution(mesh):
    torus = Mesh(
        mesh.devices.reshape(8, 4, 2, mesh.shape["mp"]), ("expert_0", "expert_1", "expert_2", "mp")
    )
    placed = (
        P(EXPERT, None),
        P(EXPERT, None),
        P(EXPERT, None),
        P(),
        P(EXPERT, None, "mp"),
        P(EXPERT, None, "mp"),
        P(EXPERT, "mp", None),
        P(),
        P(),
        P(),
    )
    return jax.shard_map(
        on_device,
        mesh=torus,
        in_specs=placed,
        out_specs=(
            P(EXPERT, "mp"),
            P(EXPERT, None, "mp"),
            P(EXPERT, None, "mp"),
            P(EXPERT, "mp", None),
            P(),
        ),
        check_vma=False,
    )
```

```python
import functools

import jax
import jax.numpy as jnp
from jax import lax
from jax.experimental import pallas as pl
from jax.experimental.pallas import tpu as pltpu
from jax.sharding import Mesh
from jax.sharding import PartitionSpec as P

D = 1024
FF = 3584
UNITS = 16
EXPERT = ("expert_0", "expert_1", "expert_2")
EPSILON = 1e-06

CAP = 12
GROUP = 16
GROUPS = 4
BLOCK = GROUP * CAP
LANES = 128
BF = jnp.bfloat16
F32 = jnp.float32
HIGHEST = lax.Precision.HIGHEST


def params(**kw):
    return pltpu.CompilerParams(vmem_limit_bytes=48 << 20, **kw)


def in_hbm(x):
    return pltpu.with_memory_space_constraint(x, pltpu.HBM)


def iota(shape, dim):
    return lax.broadcasted_iota(jnp.int32, shape, dim)


def dot(a, b, dims=((1,), (0,)), **kw):
    return lax.dot_general(a, b, (dims, ((), ())), preferred_element_type=F32, **kw)


def row_sum(x):
    return jnp.sum(x, axis=1, keepdims=True)


DATA = 2 * CAP
SIDE = 8


def routing(routes, experts):
    across = routes[...].astype(F32).T
    n = across.shape[0]
    ids = [across[:, k : k + 1].astype(jnp.int32) for k in range(2)]
    hits = [(ids[k] == iota((n, experts), 1)).astype(F32) for k in range(2)]
    earlier = (iota((n, n), 0) > iota((n, n), 1)).astype(F32).astype(BF)
    before = dot(earlier, (hits[0] + hits[1]).astype(BF))
    places = [row_sum(before * hits[k]).astype(jnp.int32) for k in range(2)]
    return ids, places, hits


def one_hot(index, size):
    return (index == iota((index.shape[0], size), 1)).astype(F32).astype(BF)


def send_x_kernel(at, tok_cols, routes, x_out, *, experts):
    del at
    n = tok_cols.shape[0]
    rows = x_out.shape[0]
    ids = [routes[k : k + 1, :] for k in range(2)]
    hits = [(ids[k] == iota((experts, n), 0)).astype(F32) for k in range(2)]
    earlier = (iota((n, n), 0) < iota((n, n), 1)).astype(F32).astype(BF)
    before = dot((hits[0] + hits[1]).astype(BF), earlier)
    base = [
        ids[k] * DATA + jnp.sum(before * hits[k], axis=0, keepdims=True).astype(jnp.int32)
        for k in range(2)
    ]
    row = iota((rows, n), 0)
    total = jnp.zeros((rows, LANES), F32)
    for h in range(2):
        picked = (base[0] + h * CAP == row) | (base[1] + h * CAP == row)
        total = total + dot(
            picked.astype(F32).astype(BF), tok_cols[:, h * LANES : (h + 1) * LANES]
        )
    x_out[...] = total.astype(BF)


def send_dy_kernel(mp, tok, cot_cols, routes, router, dy_out, aux_out):
    del mp
    n = tok.shape[0]
    experts = router.shape[0]
    rows = dy_out.shape[0]
    size = DATA + SIDE
    ids, places, hits = routing(routes, experts)
    logits = dot(tok[...], router[...], ((1,), (1,)))
    sig = [1.0 / (1.0 + jnp.exp(-row_sum(logits * hits[k]))) for k in range(2)]
    denominator = sig[0] + sig[1]
    gates = [s / denominator for s in sig]
    cot = cot_cols[...].astype(F32)
    total = jnp.zeros((rows, LANES), F32)
    sides = [jnp.zeros((experts, LANES), F32) for _ in range(5)]
    for k in range(2):
        scaled = (gates[k] * cot).astype(BF)
        for h in range(2):
            pick = one_hot(ids[k] * size + places[k] + h * CAP, rows)
            total = total + dot(pick, scaled[:, h * LANES : (h + 1) * LANES], ((0,), (0,)))
        own = gates[1 - k] * (1.0 - sig[k])
        other = -gates[1 - k] * (1.0 - sig[1 - k])
        values = two_parts(own) + two_parts(other) + (ids[1 - k],)
        slot = one_hot(places[k], LANES).astype(F32)
        for i, value in enumerate(values):
            placed = (slot * value.astype(F32)).astype(BF)
            sides[i] = sides[i] + dot(hits[k].astype(BF), placed, ((0,), (0,)))
    expert = iota((experts, rows), 0) * size + DATA
    for i in range(5):
        row = (expert + i == iota((experts, rows), 1)).astype(F32).astype(BF)
        total = total + dot(row, sides[i].astype(BF), ((0,), (0,)))
    dy_out[...] = total.astype(BF)
    lane = iota((n, LANES), 1)
    aux = jnp.zeros((n, LANES), F32)
    for i, column in enumerate(gates + [i.astype(F32) for i in ids + places]):
        aux = jnp.where(lane == i, column, aux)
    aux_out[...] = aux


def send_x(tokens, routes, experts, index):
    n, _ = tokens.shape
    rows = experts * DATA
    return pl.pallas_call(
        functools.partial(send_x_kernel, experts=experts),
        grid_spec=pltpu.PrefetchScalarGridSpec(
            num_scalar_prefetch=1,
            grid=(1,),
            in_specs=[
                pl.BlockSpec((n, 2 * LANES), lambda i, at: (0, at[0])),
                pl.BlockSpec((2, n), lambda i, at: (0, 0)),
            ],
            out_specs=pl.BlockSpec((rows, LANES), lambda i, at: (0, 0)),
        ),
        out_shape=jax.ShapeDtypeStruct((rows, LANES), BF),
        compiler_params=params(),
        name="send_x",
    )(index, tokens, routes)


def send_dy(tokens, cotangent, routes, router, index):
    n, width = tokens.shape
    experts = router.shape[0]
    rows = experts * (DATA + SIDE)
    whole = lambda *shape: pl.BlockSpec(shape, lambda i, at: (0,) * len(shape))
    return pl.pallas_call(
        send_dy_kernel,
        grid_spec=pltpu.PrefetchScalarGridSpec(
            num_scalar_prefetch=1,
            grid=(1,),
            in_specs=[
                whole(n, width),
                pl.BlockSpec((n, 2 * LANES), lambda i, at: (0, at[0])),
                whole(2, n),
                whole(experts, width),
            ],
            out_specs=[whole(rows, LANES), whole(n, LANES)],
        ),
        out_shape=[
            jax.ShapeDtypeStruct((rows, LANES), BF),
            jax.ShapeDtypeStruct((n, LANES), F32),
        ],
        compiler_params=params(),
        name="send_dy",
    )(index, tokens, cotangent, routes, router)


def column_of(mp, k, h):
    member = lax.rem(mp + k + GROUPS, GROUPS)
    return pl.multiple_of((2 * member + h) * LANES, LANES)


def unpack_rows(perm, mp, messages, to, blocks):
    def body(b, carry):
        at = pl.ds(pl.multiple_of(b * 2 * BLOCK, 2 * BLOCK), 2 * BLOCK)
        rows = pl.ds(pl.multiple_of(b * BLOCK, BLOCK), BLOCK)
        both = dot(perm[...], jnp.concatenate([m[at, :] for m in messages], axis=1)).astype(BF)
        for h in range(2):
            for k in range(GROUPS):
                to[rows, pl.ds(column_of(mp, -k, h), LANES)] = both[
                    h * BLOCK : (h + 1) * BLOCK, k * LANES : (k + 1) * LANES
                ]
        return carry

    lax.fori_loop(0, blocks, body, 0)


def forward_kernel(mp, perm, m0, m1, m2, m3, gate, up, down, *refs):
    rows_x, hidden, by_gate, by_up = refs[:4]
    parts = refs[4 : 4 + GROUPS]
    outs = refs[4 + GROUPS]
    step = pl.program_id(0)
    blocks = rows_x.shape[0] // BLOCK

    @pl.when(step == 0)
    def _():
        unpack_rows(perm, mp[0], (m0, m1, m2, m3), rows_x, blocks)

    acts = dot(rows_x[...], jnp.concatenate([gate[...], up[...]], axis=1))
    act_gate = acts[:, :LANES]
    act_up = acts[:, LANES:]
    s = 1.0 / (1.0 + jnp.exp(-act_gate))
    silu = act_gate * s
    hidden[:, pl.ds(pl.multiple_of(step * LANES, LANES), LANES)] = (silu * act_up).astype(BF)
    by_gate[...] = act_up * s * (1.0 + act_gate * (1.0 - s))
    by_up[...] = silu

    @pl.when(step == pl.num_programs(0) - 1)
    def _():
        outs[...] = dot(hidden[...], down[...]).astype(BF)
        for k in range(GROUPS):
            parts[k][...] = outs[:, pl.ds(column_of(mp[0], k, 0), 2 * LANES)]


def expert_forward(mp_index, perm, messages, w_gate, w_up, w_down):
    sent, _ = messages[0].shape
    rows = sent // 2
    width, ff = w_gate.shape
    whole = lambda *shape: pl.BlockSpec(shape, lambda i, mp: (0,) * len(shape))
    column = lambda n: pl.BlockSpec((n, LANES), lambda i, mp: (0, i))
    return pl.pallas_call(
        forward_kernel,
        grid_spec=pltpu.PrefetchScalarGridSpec(
            num_scalar_prefetch=1,
            grid=(ff // LANES,),
            in_specs=[whole(*perm.shape)]
            + [whole(sent, LANES)] * GROUPS
            + [column(width), column(width), whole(ff, width)],
            out_specs=[whole(rows, width), whole(rows, ff), column(rows), column(rows)]
            + [whole(rows, 2 * LANES)] * GROUPS,
            scratch_shapes=[pltpu.VMEM((rows, width), BF)],
        ),
        out_shape=[
            pltpu.HBM((rows, width), BF),
            pltpu.HBM((rows, ff), BF),
            pltpu.HBM((rows, ff), F32),
            pltpu.HBM((rows, ff), F32),
        ]
        + [pltpu.HBM((rows, 2 * LANES), BF)] * GROUPS,
        compiler_params=params(),
        name="expert_forward",
    )(mp_index, perm, *messages, in_hbm(w_gate), in_hbm(w_up), in_hbm(w_down))


def pack_kernel(perm_t, p0, p1, p2, p3, out):
    for b in range(p0.shape[0] // BLOCK):
        rows = slice(b * BLOCK, (b + 1) * BLOCK)
        total = p0[rows, :].astype(F32)
        for p in (p1, p2, p3):
            total = total + p[rows, :].astype(F32)
        total = total.astype(BF)
        halves = jnp.concatenate([total[:, :LANES], total[:, LANES:]], axis=0)
        out[b * 2 * BLOCK : (b + 1) * 2 * BLOCK, :] = dot(perm_t[...], halves).astype(BF)


def pack_rows(perm_t, pieces):
    return pl.pallas_call(
        pack_kernel,
        out_shape=jax.ShapeDtypeStruct((2 * pieces[0].shape[0], LANES), BF),
        compiler_params=params(),
        name="pack_rows",
    )(perm_t, *pieces)


HALVES = 2
CHUNKS = 4


def logit_terms(q, side, expert, experts):
    part = q.shape[0]
    row = iota((part, part // CAP), 0)
    first = iota((part, part // CAP), 1) * CAP
    source = ((row >= first) & (row < first + CAP)).astype(F32)
    place = (iota((part, 1), 0).astype(F32) - row_sum(source * first.astype(F32))).astype(jnp.int32)
    slot = (place == iota((part, LANES), 1)).astype(F32)
    both = side[...].astype(F32)
    both = jnp.concatenate([both[:, DATA + i, :] for i in range(5)], axis=1).astype(BF)
    spread = dot(source.astype(BF), both)
    values = [row_sum(spread[:, i * LANES : (i + 1) * LANES] * slot) for i in range(5)]
    own = q * (values[0] + values[1])
    other = q * (values[2] + values[3])
    lane = iota((part, experts), 1)
    grads = jnp.where(lane == expert, own, 0.0)
    return jnp.where(lane == values[4].astype(jnp.int32), other, grads)


def backward_kernel(
    at, perm, m0, m1, m2, m3, side, down, hidden, by_gate, by_up, rows_x,
    g_gate, g_up, g_down, squares, router,
    rows_dy, d_gate, d_up, x_across, hidden_across, router_total, sums,
):
    step = pl.program_id(0)
    part = rows_x.shape[0]
    experts = router.shape[0]

    @pl.when(step < HALVES)
    def _():
        at_rows = pl.ds(pl.multiple_of(step * part, part), part)
        dy = rows_dy.at[at_rows]
        unpack_rows(perm, at[0], (m0, m1, m2, m3), dy, part // BLOCK)
        grad_hidden = dot(dy[...], down[...], ((1,), (1,)))
        d_gate[at_rows, :] = (grad_hidden * by_gate[...]).astype(BF)
        d_up[at_rows, :] = (grad_hidden * by_up[...]).astype(BF)
        x_across[:, at_rows] = rows_x[...].T
        hidden_across[:, at_rows] = hidden[...].T
        q = row_sum(hidden[...].astype(F32) * grad_hidden)
        grads = logit_terms(q, side, at[1], experts)
        both = dot(jnp.concatenate(two_parts(grads), axis=1), rows_x[...], ((0,), (0,)))
        grad = both[:experts] + both[experts:]

        @pl.when(step == 0)
        def _():
            router_total[...] = grad
            sums[...] = jnp.zeros_like(sums)

        @pl.when(step == HALVES - 1)
        def _():
            whole = router_total[...] + grad
            for j in range(router.shape[1]):
                router[:, j, :] = whole[:, j * LANES : (j + 1) * LANES]

    @pl.when(step >= HALVES)
    def _():
        chunk = step - HALVES
        outs = (
            (g_gate, x_across, d_gate),
            (g_up, x_across, d_up),
            (g_down, hidden_across, rows_dy),
        )
        for i, (out, left, right) in enumerate(outs):
            n = out.shape[0]
            grad = dot(left[pl.ds(pl.multiple_of(chunk * n, n), n), :], right[...])
            out[...] = grad
            total = jnp.sum(grad * grad, axis=0, keepdims=True)
            sums[i : i + 1, : grad.shape[1]] += total

    @pl.when(step == pl.num_programs(0) - 1)
    def _():
        lane = iota(squares.shape, 1)
        values = jnp.zeros(squares.shape, F32)
        for i in range(3):
            values = jnp.where(lane == i, row_sum(sums[i : i + 1, :]), values)
        squares[...] = values


def expert_backward(index, perm, messages, side, w_down, hidden, by_gate, by_up, rows_x):
    sent, _ = messages[0].shape
    rows = sent // 2
    part = rows // HALVES
    experts = rows // CAP
    ff, width = w_down.shape
    first = lambda i: jnp.minimum(i, HALVES - 1)
    then = lambda i: jnp.maximum(i - HALVES, 0)
    whole = lambda *shape: pl.BlockSpec(shape, lambda i, at: (0,) * len(shape))
    row = lambda n, m: pl.BlockSpec((n, m), lambda i, at: (first(i), 0))
    out = lambda n, m: pl.BlockSpec((n // CHUNKS, m), lambda i, at: (then(i), 0))
    return pl.pallas_call(
        backward_kernel,
        grid_spec=pltpu.PrefetchScalarGridSpec(
            num_scalar_prefetch=1,
            grid=(HALVES + CHUNKS,),
            in_specs=[whole(*perm.shape)]
            + [row(sent // HALVES, LANES)] * GROUPS
            + [pl.BlockSpec((part // CAP, DATA + SIDE, LANES), lambda i, at: (first(i), 0, 0))]
            + [whole(ff, width), row(part, ff), row(part, ff), row(part, ff), row(part, width)],
            out_specs=[
                out(width, ff),
                out(width, ff),
                out(ff, width),
                whole(1, LANES),
                whole(experts, width // LANES, LANES),
            ],
            scratch_shapes=[
                pltpu.VMEM((rows, width), BF),
                pltpu.VMEM((rows, ff), BF),
                pltpu.VMEM((rows, ff), BF),
                pltpu.VMEM((width, rows), BF),
                pltpu.VMEM((ff, rows), BF),
                pltpu.VMEM((experts, width), F32),
                pltpu.VMEM((SIDE, width), F32),
            ],
        ),
        out_shape=[
            pltpu.HBM((width, ff), F32),
            pltpu.HBM((width, ff), F32),
            pltpu.HBM((ff, width), F32),
            jax.ShapeDtypeStruct((1, LANES), F32),
            jax.ShapeDtypeStruct((experts, width // LANES, LANES), F32),
        ],
        compiler_params=params(),
        name="expert_backward",
    )(
        index, perm, *messages, side, in_hbm(w_down), in_hbm(hidden), in_hbm(by_gate), in_hbm(by_up),
        in_hbm(rows_x),
    )


NET_ROWS = 32


def two_parts(x):
    high = x.astype(BF)
    return high, (x - high.astype(F32)).astype(BF)


def spread_kernel(coef, to):
    k = UNITS * NET_ROWS
    c = 8 * NET_ROWS
    same = iota((k, c), 0) % NET_ROWS == iota((k, c), 1) % NET_ROWS
    feature = iota((k, c), 1) // NET_ROWS
    value = jnp.zeros((k, c), F32)
    for part in range(3):
        a = coef[:, part : part + 1]
        high = a.astype(BF).astype(F32)
        low = a - high
        if part < 2:
            values = (high, low, high)
        else:
            values = (high, low)
        for i, v in enumerate(values):
            value = jnp.where(feature == part * 3 + i, v, value)
    to[...] = jnp.where(same, value, 0.0).astype(BF)


def spread_weights(mlp_in, weight_scale):
    coef = jnp.stack([mlp_in[0], mlp_in[2], mlp_in[1] * weight_scale], axis=1)
    coef = jnp.repeat(coef, NET_ROWS, axis=0)
    return pl.pallas_call(
        spread_kernel,
        out_shape=jax.ShapeDtypeStruct((UNITS * NET_ROWS, 8 * NET_ROWS), BF),
        compiler_params=params(),
        name="spread_weights",
    )(coef)


def step_kernel(scalars, rms, spread, grad, weight, out, *, rows):
    n = NET_ROWS
    height, width = grad.shape
    inverse = rms[0]
    constant = scalars[2, 0]

    def features(r, c, lanes):
        w = weight[pl.ds(r, n), c : c + lanes]
        f0 = grad[pl.ds(r, n), c : c + lanes] * inverse
        h0, l0 = two_parts(f0)
        h2, l2 = two_parts(jnp.tanh(f0))
        return jnp.concatenate([h0, h0, l0, h2, h2, l2, w, w], axis=0)

    def network(feats):
        y = dot(spread[...], feats)
        total = jnp.full((n, feats.shape[1]), constant, F32)
        for j in range(UNITS):
            total = total + scalars[1, j] * jnp.maximum(y[j * n : (j + 1) * n], scalars[0, j])
        return total.astype(BF)

    def body(i, carry):
        r = pl.multiple_of(i * rows, rows)
        for pair in range(0, rows, 2 * n):
            at = [r + pair, r + pair + n]
            whole = width // 256 * 256
            for c in range(0, whole, 256):
                for a in at:
                    out[pl.ds(a, n), c : c + 256] = network(features(a, c, 256))
            if whole < width:
                u = network(jnp.concatenate([features(a, whole, 128) for a in at], axis=1))
                for i, a in enumerate(at):
                    out[pl.ds(a, n), whole:width] = u[:, i * 128 : (i + 1) * 128]
        return carry

    lax.fori_loop(0, height // rows, body, 0)


def learned_step(grad, weight, rms, spread, scalars):
    height, width = grad.shape
    block = 128
    tile = pl.BlockSpec((block, width), lambda i: (i, 0))
    return pl.pallas_call(
        functools.partial(step_kernel, rows=128),
        grid=(height // block,),
        in_specs=[
            pl.BlockSpec(memory_space=pltpu.SMEM),
            pl.BlockSpec(memory_space=pltpu.SMEM),
            pl.BlockSpec(spread.shape, lambda i: (0, 0)),
            tile,
            tile,
        ],
        out_specs=tile,
        out_shape=jax.ShapeDtypeStruct((height, width), BF),
        compiler_params=params(),
        name="learned_step",
    )(scalars, rms, spread, in_hbm(grad), in_hbm(weight))


def mix_kernel(at, aux, tok_cols, back, out, *, size):
    del at
    rows = back.shape[0]
    later = jnp.concatenate([back[CAP:, :], back[:CAP, :]], axis=0)
    both = jnp.concatenate([back[...], later], axis=1)
    total = tok_cols[...].astype(F32)
    for k in range(2):
        base = aux[:, 2 + k : 3 + k] * size + aux[:, 4 + k : 5 + k]
        total = total + aux[:, k : k + 1] * dot(one_hot(base.astype(jnp.int32), rows), both)
    out[...] = total.astype(BF)


def mix(index, aux, tokens, back, experts):
    n = tokens.shape[0]
    cols = 2 * LANES
    whole = lambda *shape: pl.BlockSpec(shape, lambda i, at: (0,) * len(shape))
    mine = pl.BlockSpec((n, cols), lambda i, at: (0, at[0]))
    return pl.pallas_call(
        functools.partial(mix_kernel, size=back.shape[0] // experts),
        grid_spec=pltpu.PrefetchScalarGridSpec(
            num_scalar_prefetch=1,
            grid=(1,),
            in_specs=[whole(n, LANES), mine, whole(*back.shape)],
            out_specs=whole(n, cols),
        ),
        out_shape=jax.ShapeDtypeStruct((n, cols), BF),
        compiler_params=params(),
        name="mix",
    )(index, aux, tokens, back)


def router_step_kernel(net, columns, weight, out):
    experts, width = weight.shape
    grad = jnp.concatenate([columns[:, j, :] for j in range(width // LANES)], axis=1)
    mean = jnp.sum(row_sum(grad * grad), axis=0, keepdims=True) * (1.0 / grad.size)
    f0 = grad / jnp.sqrt(mean + EPSILON)
    f1 = weight[...].astype(F32) * D**0.5
    f2 = jnp.tanh(f0)
    total = jnp.zeros_like(f0)
    for j in range(UNITS):
        total = total + net[4, j] * jnp.maximum(
            net[0, j] * f0 + net[1, j] * f1 + net[2, j] * f2 + net[3, j], 0.0
        )
    out[...] = total.astype(BF)


def router_step(net, parts, weight):
    return pl.pallas_call(
        router_step_kernel,
        in_specs=[
            pl.BlockSpec(memory_space=pltpu.SMEM),
            pl.BlockSpec(memory_space=pltpu.VMEM),
            pl.BlockSpec(memory_space=pltpu.VMEM),
        ],
        out_shape=jax.ShapeDtypeStruct(weight.shape, BF),
        compiler_params=params(),
        name="router_step",
    )(net, parts, weight)


def to_experts(x, peers):
    sent = x.reshape(peers, -1, x.shape[-1])
    return lax.all_to_all(sent, EXPERT, 0, 0, tiled=True)


def from_members(pieces):
    return [pieces[0]] + [
        lax.ppermute(pieces[k], "mp", [(i, (i + k) % GROUPS) for i in range(GROUPS)])
        for k in range(1, GROUPS)
    ]


def together(values):
    return lax.optimization_barrier(values)


def on_device(
    tokens,
    cotangent,
    routes,
    router_weight,
    gate_weight,
    up_weight,
    down_weight,
    mlp_in,
    mlp_bias,
    mlp_out,
):
    experts = lax.axis_size(EXPERT)
    groups = lax.axis_size("mp")
    width = tokens.shape[1]
    index = jnp.stack([lax.axis_index("mp"), lax.axis_index(EXPERT)]).astype(jnp.int32)
    w_gate = gate_weight[0]
    w_up = up_weight[0]
    w_down = down_weight[0]

    pos = jnp.arange(2 * BLOCK, dtype=jnp.int32)
    inner = pos % BLOCK
    source_row = inner + inner // CAP * CAP + pos // BLOCK * CAP
    perm = (source_row[:, None] == pos[None, :]).astype(BF)
    perm_t = (source_row[None, :] == pos[:, None]).astype(BF)
    spread_in = spread_weights(mlp_in, D**0.5)
    spread_down = spread_weights(mlp_in, FF**0.5)
    scalars = jnp.stack(
        [-mlp_bias, mlp_out, jnp.broadcast_to(jnp.sum(mlp_bias * mlp_out), mlp_out.shape)]
    )
    net = jnp.concatenate([mlp_in, mlp_bias[None], mlp_out[None]], axis=0)
    router_across = router_weight.T

    routes_across = in_hbm(routes.T)
    sent_x = send_x(in_hbm(tokens), routes_across, experts, index)
    own_x = to_experts(sent_x, experts).reshape(-1, LANES)
    sent_dy, aux = send_dy(in_hbm(tokens), in_hbm(cotangent), routes_across, router_across, index)
    sent_dy, perm, perm_t, spread_in, spread_down, scalars, net = together(
        (sent_dy, perm, perm_t, spread_in, spread_down, scalars, net)
    )
    msg_x = from_members([own_x] * GROUPS)
    all_dy = to_experts(sent_dy, experts)
    own_dy = all_dy[:, :DATA].reshape(-1, LANES)
    perm, own_dy = together((perm, own_dy))
    msg_dy = from_members([own_dy] * GROUPS)

    rows_x, hidden, by_gate, by_up, *parts = expert_forward(
        index, perm, msg_x, w_gate, w_up, w_down
    )

    swapped = from_members(parts)

    g_gate, g_up, g_down, squares, router_part = expert_backward(
        index, perm, msg_dy, all_dy, w_down, hidden, by_gate, by_up, rows_x
    )
    high = lax.reduce_precision(squares, 8, 7)
    row = iota((SIDE, LANES), 0)
    squares = jnp.where(row == 0, high, jnp.where(row == 1, squares - high, 0.0))
    terms = jnp.concatenate(
        [router_part, jnp.broadcast_to(squares[None], (experts, SIDE, LANES))], axis=1
    ).astype(BF)
    swapped, terms = together((swapped, terms))
    expert_out = pack_rows(perm_t, swapped).reshape(experts, DATA, LANES)
    sums = jnp.sum(to_experts(terms, experts).astype(F32), axis=0)
    sums = sum(from_members([sums] * GROUPS))
    total_count = experts * width * w_gate.shape[1] * groups
    inverse = 1.0 / jnp.sqrt((sums[SIDE] + sums[SIDE + 1]) / total_count + EPSILON)
    column = sums[:SIDE]
    high = lax.reduce_precision(column, 8, 7)
    column = jnp.concatenate([high, column - high], axis=0).astype(BF)
    column = jnp.broadcast_to(column[None], (experts, 2 * SIDE, LANES))
    back = to_experts(jnp.concatenate([expert_out, column], axis=1), experts)

    down_update = learned_step(g_down, w_down, inverse[2:3], spread_down, scalars)
    gate_update = learned_step(g_gate, w_gate, inverse[0:1], spread_in, scalars)
    up_update = learned_step(g_up, w_up, inverse[1:2], spread_in, scalars)
    back, up_update = together((back, up_update))
    mixed = mix(index, aux, tokens, back.reshape(-1, LANES), experts)
    columns = back[:, DATA : DATA + SIDE].astype(F32) + back[:, DATA + SIDE :].astype(F32)
    router_update = router_step(net, columns, router_across).T
    return (mixed, gate_update[None], up_update[None], down_update[None], router_update)


def solution(mesh):
    torus = Mesh(
        mesh.devices.reshape(8, 4, 2, mesh.shape["mp"]), ("expert_0", "expert_1", "expert_2", "mp")
    )
    placed = (
        P(EXPERT, None),
        P(EXPERT, None),
        P(EXPERT, None),
        P(),
        P(EXPERT, None, "mp"),
        P(EXPERT, None, "mp"),
        P(EXPERT, "mp", None),
        P(),
        P(),
        P(),
    )
    return jax.shard_map(
        on_device,
        mesh=torus,
        in_specs=placed,
        out_specs=(
            P(EXPERT, "mp"),
            P(EXPERT, None, "mp"),
            P(EXPERT, None, "mp"),
            P(EXPERT, "mp", None),
            P(),
        ),
        check_vma=False,
    )
```
